128 devices in a mesh: img: 16 (over y, x_hi, core), cls: 8 (over z, x_lo).
Axes of the slice: x: 4 (x_hi: 2, x_lo: 2; x = x_hi * 2 + x_lo), y: 4, z: 4, core: 2. Of those that a mesh axis runs over, the one named last changes fastest.
Arguments:
- images: bfloat16 [128, 9216], P('img'), may hold values from -64 to 64
- references: bfloat16 [512, 9216], P(('img', 'cls')), may hold values from -0.2 to 0.2
- class_logprior: bfloat16 [512], P(('img', 'cls')), may hold values from -3 to 3
- ctf_table: float32 [16, 32], replicated, may hold values from -1 to 1, as said below
- noise_power: float32 [32], replicated, may hold values from 0.5 to 2
- tau_power: float32 [32], replicated, may hold values from 0.5 to 4
- defocus: int32 [128], P('img'), may hold values from 0 to 15
- offsets: int32 [128, 4, 2], P('img'), may hold values from -3 to 3
Outputs:
- new_refs: float32 [512, 9216], P(('img', 'cls'))
- new_weights: float32 [512], P(('img', 'cls'))
- loglik: float32 [128], P('img')
The draws below stay inside these ranges and needn't reach their ends.
Inputs may be any that keep to these rules, and one draw needn't show every extreme that they name: `ctf_table`: each row is a contrast transfer curve that oscillates over the cycles.
All inputs are finite; a program needn't handle non-finite values.
Results may differ from the reference program's by a relative error of at most 0.0068.
Values may be sent and summed in bfloat16 or wider, within the bound.
No kernel may reach another device: no remote copies, remote signals or barrier semaphores. Data moves between devices by JAX's collectives and lax.ppermute only.
A program may use at most 64 MiB of HBM per device.

```python
import math
import jax
import jax.numpy as jnp
from jax import lax

TRANS = 4
CYCLES = 32
ANG = 144
ROT = 36
K = 512
NDEF = 16
IMGS = 128


def draw_common(key):
    width = 2 * CYCLES * ANG
    keys = [jax.random.fold_in(key, 101 + number) for number in range(11)]
    refs = jnp.clip(jax.random.normal(keys[1], (K, width)) * 0.03, -0.2, 0.2)
    slope = jax.random.uniform(keys[2], (NDEF, 1), minval=0.002, maxval=0.02)
    radius = jnp.arange(CYCLES, dtype=jnp.float32) + 1.0
    curves = -jnp.sin(slope * radius[None, :] * radius[None, :] + 0.1)
    noise = jnp.exp(jax.random.uniform(keys[3], (CYCLES,), minval=math.log(0.5), maxval=math.log(2.0)))
    groups = jax.random.randint(keys[4], (IMGS,), 0, NDEF)
    shifts = jax.random.randint(keys[5], (IMGS, TRANS, 2), -3, 4)
    pictures = jnp.clip(jax.random.normal(keys[6], (IMGS, width)), -6.0, 6.0)
    return (refs, curves, noise, groups, shifts, pictures)


def draw_images(key, part):
    return draw_common(key)[5].astype(jnp.bfloat16)


def draw_references(key, part):
    return draw_common(key)[0].astype(jnp.bfloat16)


def draw_ctf_table(key, part):
    return draw_common(key)[1].astype(jnp.float32)


def draw_noise_power(key, part):
    return draw_common(key)[2].astype(jnp.float32)


def draw_defocus(key, part):
    return draw_common(key)[3].astype(jnp.int32)


def draw_offsets(key, part):
    return draw_common(key)[4].astype(jnp.int32)


def block_scale(own_key, shape, cuts, least, top_value):
    def one(dim, blocks):
        draws = jax.random.uniform(jax.random.fold_in(jax.random.fold_in(own_key, 6), dim), (blocks,), jnp.float32, least / len(cuts), top_value / len(cuts))
        return jnp.repeat(jnp.exp(draws), shape[dim] // blocks).reshape((-1,) + (1,) * (len(shape) - dim - 1))

    level = one(*cuts[0])
    for cut in cuts[1:]:
        level = level * one(*cut)
    return level


def gaussian(own_key, dims, scale, limit, pieces=(), kind=jnp.bfloat16):
    entries = scale * jax.random.normal(own_key, dims, jnp.float32)
    if pieces:
        entries = entries * block_scale(own_key, dims, pieces, -0.22, 0.18)
    return jnp.clip(entries, -limit, limit).astype(kind)


def setup_inputs(seed: int = 0) -> dict:
    splits = jax.random.split(jax.random.key(seed), 9)
    images = draw_images(jax.random.fold_in(splits[8], 71), 0)
    references = draw_references(jax.random.fold_in(splits[8], 71), 0)
    class_logprior = gaussian(splits[2], (K,), 0.5, 3.0, ((0, 128),))
    ctf_table = draw_ctf_table(jax.random.fold_in(splits[8], 71), 0)
    noise_power = draw_noise_power(jax.random.fold_in(splits[8], 71), 0)
    tau_power = jnp.clip(jnp.exp(jax.random.uniform(splits[5], (CYCLES,), jnp.float32, math.log(0.5), math.log(4.0))), 0.5, 4.0)
    defocus = draw_defocus(jax.random.fold_in(splits[8], 71), 0)
    offsets = draw_offsets(jax.random.fold_in(splits[8], 71), 0)
    return {"images": images, "references": references, "class_logprior": class_logprior, "ctf_table": ctf_table, "noise_power": noise_power, "tau_power": tau_power, "defocus": defocus, "offsets": offsets}


offset_sigma = 2.0


def phase_table(shift_x, shift_y):
    radius = jnp.arange(CYCLES, dtype=jnp.float32) + 1.0
    theta = 2.0 * math.pi * jnp.arange(ANG, dtype=jnp.float32) / ANG
    freq_x = radius[:, None] * jnp.cos(theta)[None, :]
    freq_y = radius[:, None] * jnp.sin(theta)[None, :]
    return -2.0 * math.pi * (shift_x[..., None, None] * freq_x + shift_y[..., None, None] * freq_y) / (2.0 * CYCLES)


def reference(images, references, class_logprior, ctf_table, noise_power, tau_power, defocus, offsets):
    width = 2 * CYCLES * ANG
    stride = ANG // ROT
    rows = IMGS * TRANS
    pixels = images.astype(jnp.float32).reshape(IMGS, 2, CYCLES, ANG)
    shift = offsets.astype(jnp.float32)
    angle = phase_table(shift[..., 0], shift[..., 1])
    cosine = jnp.cos(angle)
    sine = jnp.sin(angle)
    real_part = pixels[:, None, 0] * cosine - pixels[:, None, 1] * sine
    imag_part = pixels[:, None, 0] * sine + pixels[:, None, 1] * cosine
    shifted = jnp.stack([real_part, imag_part], axis=2)
    contrast = ctf_table[defocus]
    weighted = (shifted * (contrast / noise_power[None, :])[:, None, None, :, None]).astype(jnp.bfloat16).reshape(rows, width)
    inserted = (shifted * contrast[:, None, None, :, None]).astype(jnp.bfloat16).reshape(rows, width)
    norm_coef = contrast * contrast / (2.0 * noise_power[None, :])
    power = jnp.sum(jnp.square(references.astype(jnp.float32).reshape(K, 2, CYCLES, ANG)), axis=(1, 3))
    penalty = jnp.dot(norm_coef, power.T, precision=lax.Precision.HIGHEST)
    trans_prior = -(shift[..., 0] * shift[..., 0] + shift[..., 1] * shift[..., 1]) / (2.0 * offset_sigma * offset_sigma)

    def score_block(chosen):
        shaped = chosen.reshape(8, 2, CYCLES, ANG)
        rotated = jnp.stack([jnp.roll(shaped, stride * turn, axis=-1) for turn in range(ROT)], axis=1).reshape(8 * ROT, width)
        return lax.dot_general(weighted, rotated, (((1,), (1,)), ((), ())), preferred_element_type=jnp.float32)

    cross = lax.map(score_block, references.reshape(K // 8, 8, width))
    cross = cross.reshape(K // 8, rows, 8, ROT).transpose(1, 0, 2, 3).reshape(IMGS, TRANS, K, ROT)
    logp = cross - penalty[:, None, :, None] + class_logprior.astype(jnp.float32)[None, None, :, None]
    logp = logp + trans_prior[:, :, None, None]
    per_image = logp.reshape(IMGS, TRANS * K * ROT)
    peak = jnp.max(per_image, axis=1)
    total = jnp.sum(jnp.exp(per_image - peak[:, None]), axis=1)
    loglik = peak + jnp.log(total)
    posterior = (jnp.exp(per_image - peak[:, None]) / total[:, None]).astype(jnp.bfloat16).reshape(rows, K, ROT)

    def insert_block(section):
        product = lax.dot_general(section, inserted, (((0,), (0,)), ((), ())), preferred_element_type=jnp.float32)
        product = product.reshape(8, ROT, 2, CYCLES, ANG)
        collected = jnp.zeros((8, 2, CYCLES, ANG), jnp.float32)
        for turn in range(ROT):
            collected = collected + jnp.roll(product[:, turn], -stride * turn, axis=-1)
        return collected

    sections = posterior.reshape(rows, K // 8, 8 * ROT).transpose(1, 0, 2)
    numer = lax.map(insert_block, sections).reshape(K, 2, CYCLES, ANG)
    post_sum = jnp.sum(posterior.astype(jnp.float32), axis=2)
    squared_rows = jnp.repeat(contrast * contrast, TRANS, axis=0)
    denom = lax.dot_general(post_sum, squared_rows, (((0,), (0,)), ((), ())), precision=lax.Precision.HIGHEST)
    weight = jnp.sum(post_sum, axis=0)
    fresh = numer / (denom[:, None, :, None] + 1.0 / tau_power[None, None, :, None])
    return fresh.reshape(K, width), weight / IMGS, loglik
```

```python
import functools
import math

import jax
import jax.numpy as jnp
import ml_dtypes
import numpy as np
from jax import lax
from jax.experimental import pallas as pl
from jax.experimental.pallas import tpu as pltpu
from jax.sharding import PartitionSpec as P

TRANS = 4
CYCLES = 32
ANG = 144
ROT = 36
NDEF = 16
STEP = ANG // ROT
PAIRS = 2 * CYCLES
LANES = 2 * STEP * CYCLES
HALF = LANES // 2
OWN = 4
MINE = 8
BLOCKS = 4
KS = OWN * BLOCKS
US = MINE * BLOCKS * TRANS
ROWS = ROT * KS
REACH = 3
offset_sigma = 2.0
F32 = jnp.float32
BF16 = jnp.bfloat16
HIGHEST = lax.Precision.HIGHEST
VMEM_LIMIT = 56 * 1024 * 1024


def phase_parts():
    span = 2 * REACH + 1
    theta = 2.0 * math.pi * np.arange(ANG).reshape(ROT, STEP) / ANG
    radius = np.arange(CYCLES) + 1.0
    fx = (np.cos(theta)[:, :, None] * radius).reshape(ROT, HALF)
    fy = (np.sin(theta)[:, :, None] * radius).reshape(ROT, HALF)
    shift = np.arange(span) - REACH
    phi = (
        -2.0
        * math.pi
        * (shift[:, None, None, None] * fx + shift[None, :, None, None] * fy)
        / (2.0 * CYCLES)
    ).reshape(span * span, ROT, HALF)
    table = np.concatenate([np.cos(phi), np.sin(phi)], axis=2).transpose(1, 0, 2)
    table = np.pad(table, ((0, 0), (0, 64 - span * span), (0, 0)))
    parts = []
    rest = table
    for _ in range(3):
        part = rest.astype(np.float32).astype(ml_dtypes.bfloat16)
        parts.append(part)
        rest = rest - part.astype(np.float64)
    return np.concatenate(parts, axis=1)


def pick_turns():
    rows = np.arange(40)[:, None]
    return (np.arange(ANG)[None, :] // STEP == rows).astype(ml_dtypes.bfloat16)


def nt(a, b, **kw):
    return lax.dot_general(a, b, (((1,), (1,)), ((), ())), preferred_element_type=F32, **kw)


def arrange_kernel(img_ref, ref_ref, prior_ref, off_ref, def_ref, pick_ref, img_out, ref_out, cut, flat):
    angle = lax.broadcasted_iota(jnp.int32, (CYCLES, ANG), 1) % STEP
    pick = pick_ref[...]
    for source, count, out in ((ref_ref, OWN, ref_out), (img_ref, MINE, img_out)):
        for j in range(PAIRS):
            line = source[:, j * ANG : (j + 1) * ANG].astype(F32)
            cut[0, pl.ds(j * 8, count), :] = line[:, :HALF]
            cut[1, pl.ds(j * 8, count), : ANG - HALF] = line[:, HALF:]
        for i in range(count):
            one = jnp.concatenate(
                [cut.at[n][pl.ds(i, PAIRS, stride=8), :] for n in range(2)], axis=1
            )[:, :ANG]
            spread = jnp.concatenate(
                [
                    jnp.where(angle == c, one[p * CYCLES : (p + 1) * CYCLES], 0.0)
                    for p in range(2)
                    for c in range(STEP)
                ],
                axis=0,
            ).astype(BF16)
            turned = nt(pick, spread)
            flat[0, pl.ds(i * 40, 40), :] = turned[:, :HALF]
            flat[1, pl.ds(i * 40, 40), :] = turned[:, HALF:]
        for b in range(ROT):
            for n in range(2):
                line = flat.at[n][pl.ds(b, count, stride=40), :]
                out[b, :, n * HALF : (n + 1) * HALF] = line.astype(BF16)
    row = lax.broadcasted_iota(jnp.int32, (MINE, LANES), 0)
    lane = lax.broadcasted_iota(jnp.int32, (MINE, LANES), 1)
    extra = jnp.zeros((MINE, LANES), F32)
    for i in range(MINE):
        for t in range(TRANS):
            for d in range(2):
                value = off_ref[i, t, d].astype(F32)
                extra = jnp.where((row == i) & (lane == 2 * t + d), value, extra)
        extra = jnp.where((row == i) & (lane == 8), def_ref[i].astype(F32), extra)
    img_out[ROT] = extra.astype(BF16)
    krow = lax.broadcasted_iota(jnp.int32, (OWN, OWN), 0)
    kcol = lax.broadcasted_iota(jnp.int32, (OWN, OWN), 1)
    prior = jnp.broadcast_to(prior_ref[...].astype(F32), (OWN, OWN))
    column = jnp.sum(jnp.where(krow == kcol, prior, 0.0), axis=1, keepdims=True)
    ref_out[ROT] = jnp.broadcast_to(column, (OWN, LANES)).astype(BF16)


def arrange(images, references, prior, offsets, defocus, pick):
    vmem = pl.BlockSpec(memory_space=pltpu.VMEM)
    smem = pl.BlockSpec(memory_space=pltpu.SMEM)
    return pl.pallas_call(
        arrange_kernel,
        out_shape=(
            jax.ShapeDtypeStruct((ROT + 1, MINE, LANES), BF16),
            jax.ShapeDtypeStruct((ROT + 1, OWN, LANES), BF16),
        ),
        in_specs=[vmem, vmem, vmem, smem, smem, vmem],
        out_specs=(vmem, vmem),
        scratch_shapes=[pltpu.VMEM((2, PAIRS * 8, HALF), F32), pltpu.VMEM((2, MINE * 40, HALF), F32)],
        compiler_params=pltpu.CompilerParams(vmem_limit_bytes=VMEM_LIMIT),
        name="arrange",
    )(images, references, prior, offsets, defocus, pick)


def score_kernel(
    own_ref,
    i0, i1, i2, i3,
    r0, r1, r2, r3,
    ctf_ref, noise_ref, table_hbm,
    exp_out, stat_out, ins_out, sq_out,
    table, weighted, pictures, back, acc, sem,
):
    copy = pltpu.make_async_copy(table_hbm, table, sem)
    copy.start()
    own = own_ref[0]
    for step, source in enumerate((i0, i1, i2, i3)):
        pictures[own ^ step] = source[...]
    square = jnp.zeros((KS, LANES), F32)
    for b in range(ROT):
        block = jnp.concatenate([r[b].astype(F32) for r in (r0, r1, r2, r3)], axis=0)
        square = square + block * block
        m = (ROT - b) % ROT
        back[pl.ds(m * KS, KS), :] = block.astype(BF16)
        back[pl.ds((m + ROT) * KS, KS), :] = block.astype(BF16)
    prior = jnp.concatenate([r[ROT].astype(F32) for r in (r0, r1, r2, r3)], axis=0)[:, :HALF]

    extra = jnp.concatenate([pictures[k, ROT].astype(F32) for k in range(BLOCKS)], axis=0)
    dx = jnp.concatenate([extra[:, 2 * t : 2 * t + 1] for t in range(TRANS)], axis=0)
    dy = jnp.concatenate([extra[:, 2 * t + 1 : 2 * t + 2] for t in range(TRANS)], axis=0)
    combo = (dx + REACH) * (2 * REACH + 1) + (dy + REACH)
    slot = lax.broadcasted_iota(jnp.int32, (US, 192), 1) % 64
    hot = jnp.where(slot.astype(F32) == combo, 1.0, 0.0).astype(BF16)
    group = lax.broadcasted_iota(jnp.int32, (MINE * BLOCKS, NDEF), 1).astype(F32)
    which = jnp.where(group == extra[:, 8:9], 1.0, 0.0)
    contrast = jnp.dot(which, ctf_ref[...], precision=HIGHEST, preferred_element_type=F32)
    noise = noise_ref[...]
    whiten = contrast / noise
    squared = contrast * contrast
    coef = squared / (2.0 * noise)
    four = lambda v: jnp.concatenate([v] * TRANS, axis=0)
    sq_out[:, :HALF] = four(squared)
    sq_out[:, HALF:] = jnp.ones((US, HALF), F32)
    coef_rows = four(jnp.concatenate([coef, coef], axis=1))
    penalty = nt(square, coef_rows, precision=HIGHEST)
    near = -(dx * dx + dy * dy) / (2.0 * offset_sigma * offset_sigma)
    diag = lax.broadcasted_iota(jnp.int32, (US, US), 0) == lax.broadcasted_iota(
        jnp.int32, (US, US), 1
    )
    near_row = jnp.sum(jnp.where(diag, near, 0.0), axis=0, keepdims=True)
    base = prior - penalty + near_row

    contrast4 = four(contrast)
    whiten4 = four(whiten)
    copy.wait()

    def shift_turn(b, carry):
        turn = jnp.dot(hot, table[b], preferred_element_type=F32)
        cosine, sine = turn[:, :HALF], turn[:, HALF:]
        block = jnp.concatenate([pictures[k, b].astype(F32) for k in range(BLOCKS)], axis=0)
        real, imag = four(block[:, :HALF]), four(block[:, HALF:])
        shifted_real = real * cosine - imag * sine
        shifted_imag = real * sine + imag * cosine
        rows = pl.ds(pl.multiple_of(b * US, US), US)
        weighted[rows, :HALF] = (shifted_real * whiten4).astype(BF16)
        weighted[rows, HALF:] = (shifted_imag * whiten4).astype(BF16)
        ins_out[rows, :HALF] = (shifted_real * contrast4).astype(BF16)
        ins_out[rows, HALF:] = (shifted_imag * contrast4).astype(BF16)
        return carry

    lax.fori_loop(0, ROT, shift_turn, 0)

    acc[...] = jnp.zeros_like(acc)

    def score_turns(h, carry):
        rows = pl.ds(pl.multiple_of((ROT - 2 * h) * KS, 2 * KS), ROWS)
        cols = pl.ds(pl.multiple_of(h * 2 * US, 2 * US), 2 * US)
        acc[...] += nt(back[rows, :], weighted[cols, :])
        return carry

    lax.fori_loop(0, ROT // 2, score_turns, 0)

    peak = jnp.full((KS, US), -jnp.inf, F32)
    for r in range(ROT):
        last = (r - 1) % ROT
        logp = acc[r * KS : (r + 1) * KS, :HALF] + acc[last * KS : (last + 1) * KS, HALF:] + base
        exp_out[r * KS : (r + 1) * KS, :] = logp
        peak = jnp.maximum(peak, logp)
    peak = jnp.max(peak, axis=0, keepdims=True)
    peak = jnp.broadcast_to(peak, (8, US))
    peak = jnp.maximum(peak, pltpu.roll(peak, 32, 1))
    peak = jnp.maximum(peak, pltpu.roll(peak, 64, 1))
    wide = jnp.broadcast_to(peak[:1], (KS, US))
    total = jnp.zeros((KS, US), F32)
    for r in range(ROT):
        value = jnp.exp(exp_out[r * KS : (r + 1) * KS, :] - wide)
        exp_out[r * KS : (r + 1) * KS, :] = value
        total = total + value
    total = jnp.broadcast_to(jnp.sum(total, axis=0, keepdims=True), (8, US))
    total = total + pltpu.roll(total, 32, 1)
    total = total + pltpu.roll(total, 64, 1)
    pair = jnp.concatenate([peak[:1], total[:1]], axis=0)
    for j in range(32):
        stat_out[j] = pair


def score(own, imgs, refs, ctf4, noise4, table):
    vmem = pl.BlockSpec(memory_space=pltpu.VMEM)
    smem = pl.BlockSpec(memory_space=pltpu.SMEM)
    return pl.pallas_call(
        score_kernel,
        out_shape=(
            jax.ShapeDtypeStruct((ROWS, US), F32),
            jax.ShapeDtypeStruct((32, 2, US), F32),
            jax.ShapeDtypeStruct((ROT * US, LANES), BF16),
            jax.ShapeDtypeStruct((US, LANES), F32),
        ),
        in_specs=[smem] + [vmem] * 10 + [pl.BlockSpec(memory_space=pl.ANY)],
        out_specs=(vmem,) * 4,
        scratch_shapes=[
            pltpu.VMEM((ROT, 192, LANES), BF16),
            pltpu.VMEM((ROT * US, LANES), BF16),
            pltpu.VMEM((BLOCKS, ROT + 1, MINE, LANES), BF16),
            pltpu.VMEM((2 * ROWS, LANES), BF16),
            pltpu.VMEM((ROWS, LANES), F32),
            pltpu.SemaphoreType.DMA,
        ],
        compiler_params=pltpu.CompilerParams(vmem_limit_bytes=VMEM_LIMIT),
        name="score",
    )(own, *imgs, *refs, ctf4, noise4, table)


def insert_kernel(own_ref, exp_ref, pair_ref, all_ref, ins_ref, sq_ref, own_out, s1, s2, s3, like_out, post, acc):
    peaks = jnp.concatenate([all_ref[j, 0:1, :] for j in range(32)], axis=0)
    totals = jnp.concatenate([all_ref[j, 1:2, :] for j in range(32)], axis=0)
    peak = jnp.max(peaks, axis=0, keepdims=True)
    total = jnp.sum(totals * jnp.exp(peaks - peak), axis=0, keepdims=True)
    like = jnp.broadcast_to(peak + jnp.log(total), (8, US))
    shift = (US - own_ref[0] * MINE) % US
    like_out[...] = pltpu.roll(like, shift, 1)
    scale = jnp.broadcast_to(jnp.exp(pair_ref[0, 0:1, :] - peak) / total, (KS, US))
    count = jnp.zeros((KS, US), F32)
    for r in range(ROT):
        value = (exp_ref[r * KS : (r + 1) * KS, :] * scale).astype(BF16)
        count = count + value.astype(F32)
        for side in range(2):
            m = (side - r) % ROT
            for again in (m, m + ROT):
                post[again * KS : (again + 1) * KS, side * HALF : (side + 1) * HALF] = value

    acc[...] = jnp.zeros_like(acc)

    def insert_turns(h, carry):
        rows = pl.ds(pl.multiple_of((ROT - 2 * h) * KS, 2 * KS), ROWS)
        cols = pl.ds(pl.multiple_of(h * 2 * US, 2 * US), 2 * US)
        acc[...] += jnp.dot(post[rows, :], ins_ref[cols, :], preferred_element_type=F32)
        return carry

    lax.fori_loop(0, ROT // 2, insert_turns, 0)
    sums = jnp.dot(count, sq_ref[...], precision=HIGHEST, preferred_element_type=F32)
    high = sums.astype(BF16)
    low = (sums - high.astype(F32)).astype(BF16)
    for b in range(ROT):
        block = acc[b * KS : (b + 1) * KS, :]
        own_out[b] = block[:OWN]
        for d, out in ((1, s1), (2, s2), (3, s3)):
            out[b] = block[d * OWN : (d + 1) * OWN].astype(BF16)
    own_out[ROT] = sums[:OWN]
    own_out[ROT + 1] = jnp.zeros((OWN, LANES), F32)
    for d, out in ((1, s1), (2, s2), (3, s3)):
        part = sums[d * OWN : (d + 1) * OWN]
        high = part.astype(BF16)
        out[ROT] = high
        out[ROT + 1] = (part - high.astype(F32)).astype(BF16)


def insert(own, exps, stats, gathered, ins, sq):
    vmem = pl.BlockSpec(memory_space=pltpu.VMEM)
    smem = pl.BlockSpec(memory_space=pltpu.SMEM)
    piece = (ROT + 2, OWN, LANES)
    return pl.pallas_call(
        insert_kernel,
        out_shape=(
            jax.ShapeDtypeStruct(piece, F32),
            jax.ShapeDtypeStruct(piece, BF16),
            jax.ShapeDtypeStruct(piece, BF16),
            jax.ShapeDtypeStruct(piece, BF16),
            jax.ShapeDtypeStruct((8, US), F32),
        ),
        in_specs=[smem] + [vmem] * 5,
        out_specs=(vmem,) * 5,
        scratch_shapes=[
            pltpu.VMEM((2 * ROWS, LANES), BF16),
            pltpu.VMEM((ROWS, LANES), F32),
        ],
        compiler_params=pltpu.CompilerParams(vmem_limit_bytes=VMEM_LIMIT),
        name="insert",
    )(own, exps, stats, gathered, ins, sq)


def finish_kernel(own_ref, g1, g2, g3, tau_ref, out_ref, weight_out, fresh, turned, lines):
    parts = [own_ref, g1, g2, g3]
    sums = sum(p[ROT].astype(F32) + p[ROT + 1].astype(F32) for p in parts)
    denom = sums[:, :HALF] + 1.0 / tau_ref[...]
    denom = jnp.concatenate([denom, denom], axis=1)
    weight_out[...] = sums[:, HALF:] / (MINE * 16)
    for b in range(ROT):
        total = own_ref[b] + g1[b].astype(F32) + g2[b].astype(F32) + g3[b].astype(F32)
        total = total / denom
        fresh[0, pl.ds(b * 8, OWN), :] = total[:, :HALF]
        fresh[1, pl.ds(b * 8, OWN), :] = total[:, HALF:]
    for k in range(OWN):
        one = [fresh.at[p][pl.ds(k, ROT, stride=8), :] for p in range(2)]
        for c in range(STEP):
            pair = [one[p][:, c * CYCLES : (c + 1) * CYCLES] for p in range(2)]
            turned[pl.ds(c, ROT, stride=STEP), :] = jnp.concatenate(pair + pair, axis=1)
        first = turned[0:128, :].T
        second = turned[128:256, :].T
        lines[0, pl.ds(k * PAIRS, PAIRS), :] = first[:PAIRS]
        lines[1, pl.ds(k * PAIRS, PAIRS), :] = second[:PAIRS]
    for j in range(PAIRS):
        line = [lines.at[n][pl.ds(j, OWN, stride=PAIRS), :] for n in range(2)]
        out_ref[:, j * ANG : (j + 1) * ANG] = jnp.concatenate(line, axis=1)[:, :ANG]


def finish(own, got, tau4):
    vmem = pl.BlockSpec(memory_space=pltpu.VMEM)
    return pl.pallas_call(
        finish_kernel,
        out_shape=(
            jax.ShapeDtypeStruct((OWN, 2 * CYCLES * ANG), F32),
            jax.ShapeDtypeStruct((OWN, HALF), F32),
        ),
        in_specs=[vmem] * 5,
        out_specs=(vmem, vmem),
        scratch_shapes=[
            pltpu.VMEM((2, ROT * 8, HALF), F32),
            pltpu.VMEM((256, 128), F32),
            pltpu.VMEM((2, OWN * PAIRS, HALF), F32),
        ],
        compiler_params=pltpu.CompilerParams(vmem_limit_bytes=VMEM_LIMIT),
        name="finish",
    )(own, *got, tau4)


def along_y(value, distance):
    return lax.ppermute(
        value, "img", [(i, ((i // 4 + distance) % 4) * 4 + i % 4) for i in range(16)]
    )


def beside(value, img_flip, cls_flip):
    pairs = [
        (i * 8 + c, (i ^ img_flip) * 8 + (c ^ cls_flip)) for i in range(16) for c in range(8)
    ]
    return lax.ppermute(value, ("img", "cls"), pairs)


def per_device(
    table, pick, images, references, class_logprior, ctf_table, noise_power, tau_power, defocus, offsets
):
    own = (lax.axis_index("img") % BLOCKS).astype(jnp.int32).reshape(1)
    img, ref = arrange(images, references, class_logprior.reshape(1, OWN), offsets, defocus, pick)
    imgs = (img, beside(img, 1, 0), beside(img, 2, 1), beside(img, 3, 1))
    refs = (ref, along_y(ref, 3), along_y(ref, 2), along_y(ref, 1))
    ctf4 = jnp.tile(ctf_table, (1, STEP))
    noise4 = jnp.tile(noise_power, STEP).reshape(1, HALF)
    tau4 = jnp.tile(tau_power, STEP).reshape(1, HALF)
    exps, stats, ins, sq = score(own, imgs, refs, ctf4, noise4, table)
    same_images = [[(y * 4 + r) * 8 + c for r in range(4) for c in range(8)] for y in range(4)]
    gathered = lax.all_to_all(
        stats, ("img", "cls"), 0, 0, tiled=True, axis_index_groups=same_images
    )
    numer, s1, s2, s3, like = insert(own, exps, stats, gathered, ins, sq)
    got = (along_y(s1, 1), along_y(s2, 2), along_y(s3, 3))
    fresh, weight = finish(numer, got, tau4)
    return fresh, weight[:, 0], like[0, :MINE]


def solution(mesh):
    table = phase_parts()
    pick = pick_turns()
    body = functools.partial(per_device, jnp.asarray(table), jnp.asarray(pick))
    return jax.shard_map(
        body,
        mesh=mesh,
        in_specs=(
            P("img", None),
            P(("img", "cls"), None),
            P(("img", "cls")),
            P(),
            P(),
            P(),
            P("img"),
            P("img", None, None),
        ),
        out_specs=(P(("img", "cls"), None), P(("img", "cls")), P("img")),
        check_vma=False,
    )
```

```python
import functools
import math

import jax
import jax.numpy as jnp
import ml_dtypes
import numpy as np
from jax import lax
from jax.experimental import pallas as pl
from jax.experimental.pallas import tpu as pltpu
from jax.sharding import PartitionSpec as P

TRANS = 4
CYCLES = 32
ANG = 144
ROT = 36
NDEF = 16
STEP = ANG // ROT
PAIRS = 2 * CYCLES
LANES = 2 * STEP * CYCLES
HALF = LANES // 2
OWN = 4
MINE = 8
BLOCKS = 4
KS = OWN * BLOCKS
US = MINE * BLOCKS * TRANS
ROWS = ROT * KS
REACH = 3
offset_sigma = 2.0
F32 = jnp.float32
BF16 = jnp.bfloat16
HIGHEST = lax.Precision.HIGHEST
VMEM_LIMIT = 24 * 1024 * 1024


def phase_parts():
    span = 2 * REACH + 1
    theta = 2.0 * math.pi * np.arange(ANG).reshape(ROT, STEP) / ANG
    radius = np.arange(CYCLES) + 1.0
    fx = (np.cos(theta)[:, :, None] * radius).reshape(ROT, HALF)
    fy = (np.sin(theta)[:, :, None] * radius).reshape(ROT, HALF)
    shift = np.arange(span) - REACH
    phi = (
        -2.0
        * math.pi
        * (shift[:, None, None, None] * fx + shift[None, :, None, None] * fy)
        / (2.0 * CYCLES)
    ).reshape(span * span, ROT, HALF)
    table = np.concatenate([np.cos(phi), np.sin(phi)], axis=2).transpose(1, 0, 2)
    table = np.pad(table, ((0, 0), (0, 64 - span * span), (0, 0)))
    parts = []
    rest = table
    for _ in range(3):
        part = rest.astype(np.float32).astype(ml_dtypes.bfloat16)
        parts.append(part)
        rest = rest - part.astype(np.float64)
    return np.concatenate(parts, axis=1)


def nt(a, b, **kw):
    return lax.dot_general(a, b, (((1,), (1,)), ((), ())), preferred_element_type=F32, **kw)


def in_hbm(value):
    return pltpu.with_memory_space_constraint(value, pltpu.HBM)


def fetch(pairs, sems):
    copies = [
        pltpu.make_async_copy(src, dst, sems.at[n]) for n, (src, dst) in enumerate(pairs)
    ]
    for copy in copies:
        copy.start()
    return copies


def as_column(row, size):
    here = lax.broadcasted_iota(jnp.int32, (size, size), 0)
    there = lax.broadcasted_iota(jnp.int32, (size, size), 1)
    wide = jnp.broadcast_to(row, (size, size))
    return jnp.sum(jnp.where(here == there, wide, 0.0), axis=1, keepdims=True)


def as_row(column, size):
    here = lax.broadcasted_iota(jnp.int32, (size, size), 0)
    there = lax.broadcasted_iota(jnp.int32, (size, size), 1)
    wide = jnp.broadcast_to(column, (size, size))
    return jnp.sum(jnp.where(here == there, wide, 0.0), axis=0, keepdims=True)


def turn_major(source, count, cut, flat, out):
    angle = lax.broadcasted_iota(jnp.int32, (CYCLES, ANG), 1) % STEP
    pick_b = lax.broadcasted_iota(jnp.int32, (40, ANG), 0)
    pick_a = lax.broadcasted_iota(jnp.int32, (40, ANG), 1)
    pick = jnp.where(pick_a // STEP == pick_b, 1.0, 0.0).astype(BF16)
    for j in range(PAIRS):
        line = source[:, j * ANG : (j + 1) * ANG].astype(F32)
        cut[0, pl.ds(j * 8, count), :] = line[:, :HALF]
        cut[1, pl.ds(j * 8, count), : ANG - HALF] = line[:, HALF:]
    for i in range(count):
        one = jnp.concatenate(
            [cut.at[n][pl.ds(i, PAIRS, stride=8), :] for n in range(2)], axis=1
        )[:, :ANG]
        spread = jnp.concatenate(
            [
                jnp.where(angle == c, one[p * CYCLES : (p + 1) * CYCLES], 0.0)
                for p in range(2)
                for c in range(STEP)
            ],
            axis=0,
        ).astype(BF16)
        turned = nt(pick, spread)
        flat[0, pl.ds(i * 40, 40), :] = turned[:, :HALF]
        flat[1, pl.ds(i * 40, 40), :] = turned[:, HALF:]
    for b in range(ROT):
        for n in range(2):
            line = flat.at[n][pl.ds(b, count, stride=40), :]
            out[b, :, n * HALF : (n + 1) * HALF] = line.astype(BF16)


def arrange_kernel(
    img_hbm, ref_hbm, prior_hbm, off_hbm, def_hbm, img_out, ref_out,
    img_ref, ref_ref, prior_ref, off_ref, def_ref, cut, cut2, flat, flat2, sems,
):
    copies = fetch(
        (
            (ref_hbm, ref_ref),
            (img_hbm, img_ref),
            (prior_hbm, prior_ref),
            (off_hbm, off_ref),
            (def_hbm, def_ref),
        ),
        sems,
    )
    copies[0].wait()
    turn_major(ref_ref, OWN, cut, flat, ref_out)
    copies[1].wait()
    turn_major(img_ref, MINE, cut2, flat2, img_out)
    for copy in copies[2:]:
        copy.wait()
    lane = lax.broadcasted_iota(jnp.int32, (MINE, LANES), 1)
    extra = jnp.where(lane == 8, as_column(def_ref[...].astype(F32), MINE), 0.0)
    for t in range(TRANS):
        for d in range(2):
            column = as_column(off_ref[t, d : d + 1, :].astype(F32), MINE)
            extra = jnp.where(lane == 2 * t + d, column, extra)
    img_out[ROT] = extra.astype(BF16)
    column = as_column(prior_ref[...].astype(F32), OWN)
    ref_out[ROT] = jnp.broadcast_to(column, (OWN, LANES)).astype(BF16)


def arrange(images, references, prior, offsets, defocus):
    vmem = pl.BlockSpec(memory_space=pltpu.VMEM)
    hbm = pl.BlockSpec(memory_space=pltpu.HBM)
    wide = 2 * CYCLES * ANG
    return pl.pallas_call(
        arrange_kernel,
        out_shape=(
            jax.ShapeDtypeStruct((ROT + 1, MINE, LANES), BF16),
            jax.ShapeDtypeStruct((ROT + 1, OWN, LANES), BF16),
        ),
        in_specs=[hbm] * 5,
        out_specs=(vmem, vmem),
        scratch_shapes=[
            pltpu.VMEM((MINE, wide), BF16),
            pltpu.VMEM((OWN, wide), BF16),
            pltpu.VMEM((1, OWN), BF16),
            pltpu.VMEM((TRANS, 2, MINE), jnp.int32),
            pltpu.VMEM((1, MINE), jnp.int32),
            pltpu.VMEM((2, PAIRS * 8, HALF), F32),
            pltpu.VMEM((2, PAIRS * 8, HALF), F32),
            pltpu.VMEM((2, MINE * 40, HALF), F32),
            pltpu.VMEM((2, MINE * 40, HALF), F32),
            pltpu.SemaphoreType.DMA((5,)),
        ],
        compiler_params=pltpu.CompilerParams(vmem_limit_bytes=VMEM_LIMIT),
        name="arrange",
    )(*(in_hbm(v) for v in (images, references, prior, offsets, defocus)))


def score_kernel(
    own_ref,
    i0, i2, i13,
    r0, r1, r2, r3,
    ctf_hbm, noise_hbm, table_hbm,
    exp_out, stat_out, ins_out, sq_out,
    ctf_ref, noise_ref, table, pictures, back, acc, sems,
):
    chunk = ROT // 6
    copies = fetch(
        [(ctf_hbm, ctf_ref), (noise_hbm, noise_ref)]
        + [(table_hbm.at[pl.ds(n * chunk, chunk)], table.at[pl.ds(n * chunk, chunk)]) for n in range(6)],
        sems,
    )
    own = own_ref[0]
    for step, source in enumerate((i0, i13.at[0], i2, i13.at[1])):
        pictures[own ^ step] = source[...]
    square = jnp.zeros((KS, LANES), F32)
    for b in range(ROT):
        block = jnp.concatenate([r[b].astype(F32) for r in (r0, r1, r2, r3)], axis=0)
        square = square + block * block
        m = (ROT - b) % ROT
        back[pl.ds(m * KS, KS), :] = block.astype(BF16)
        back[pl.ds((m + ROT) * KS, KS), :] = block.astype(BF16)
    prior = jnp.concatenate([r[ROT].astype(F32) for r in (r0, r1, r2, r3)], axis=0)[:, :HALF]

    extra = jnp.concatenate([pictures[k, ROT].astype(F32) for k in range(BLOCKS)], axis=0)
    dx = jnp.concatenate([extra[:, 2 * t : 2 * t + 1] for t in range(TRANS)], axis=0)
    dy = jnp.concatenate([extra[:, 2 * t + 1 : 2 * t + 2] for t in range(TRANS)], axis=0)
    combo = (dx + REACH) * (2 * REACH + 1) + (dy + REACH)
    slot = lax.broadcasted_iota(jnp.int32, (US, 192), 1) % 64
    hot = jnp.where(slot.astype(F32) == combo, 1.0, 0.0).astype(BF16)
    group = lax.broadcasted_iota(jnp.int32, (MINE * BLOCKS, NDEF), 1).astype(F32)
    which = jnp.where(group == extra[:, 8:9], 1.0, 0.0)
    copies[0].wait()
    copies[1].wait()
    ctf4 = jnp.concatenate([ctf_ref[...]] * STEP, axis=1)
    contrast = jnp.dot(which, ctf4, precision=HIGHEST, preferred_element_type=F32)
    noise = jnp.concatenate([noise_ref[...]] * STEP, axis=1)
    whiten = contrast / noise
    squared = contrast * contrast
    coef = squared / (2.0 * noise)
    four = lambda v: jnp.concatenate([v] * TRANS, axis=0)
    sq_out[:, :HALF] = four(squared)
    sq_out[:, HALF:] = jnp.ones((US, HALF), F32)
    coef_rows = four(jnp.concatenate([coef, coef], axis=1))
    penalty = nt(square, coef_rows, precision=HIGHEST)
    near = -(dx * dx + dy * dy) / (2.0 * offset_sigma * offset_sigma)
    near_row = as_row(near, US)
    base = prior - penalty + near_row

    contrast4 = four(contrast)
    whiten4 = four(whiten)
    cross = None
    for h in range(ROT // 2):
        pair = []
        for b in (2 * h, 2 * h + 1):
            if b % chunk == 0:
                copies[2 + b // chunk].wait()
            turn = jnp.dot(hot, table[b], preferred_element_type=F32)
            cosine, sine = turn[:, :HALF], turn[:, HALF:]
            block = jnp.concatenate([pictures[k, b].astype(F32) for k in range(BLOCKS)], axis=0)
            real, imag = four(block[:, :HALF]), four(block[:, HALF:])
            shifted_real = real * cosine - imag * sine
            shifted_imag = real * sine + imag * cosine
            rows = slice(b * US, (b + 1) * US)
            ins_out[rows, :HALF] = (shifted_real * contrast4).astype(BF16)
            ins_out[rows, HALF:] = (shifted_imag * contrast4).astype(BF16)
            both = [shifted_real * whiten4, shifted_imag * whiten4]
            pair.append(jnp.concatenate(both, axis=1).astype(BF16))
        part = nt(
            back[(ROT - 2 * h) * KS : (2 * ROT - 2 * h) * KS, :], jnp.concatenate(pair, axis=0)
        )
        cross = part if cross is None else cross + part
    acc[...] = cross

    peak = jnp.full((KS, US), -jnp.inf, F32)
    for r in range(ROT):
        last = (r - 1) % ROT
        logp = acc[r * KS : (r + 1) * KS, :HALF] + acc[last * KS : (last + 1) * KS, HALF:] + base
        exp_out[r * KS : (r + 1) * KS, :] = logp
        peak = jnp.maximum(peak, logp)
    peak = jnp.max(peak, axis=0, keepdims=True)
    peak = jnp.broadcast_to(peak, (8, US))
    peak = jnp.maximum(peak, pltpu.roll(peak, 32, 1))
    peak = jnp.maximum(peak, pltpu.roll(peak, 64, 1))
    wide = jnp.broadcast_to(peak[:1], (KS, US))
    total = jnp.zeros((KS, US), F32)
    for r in range(ROT):
        value = jnp.exp(exp_out[r * KS : (r + 1) * KS, :] - wide)
        exp_out[r * KS : (r + 1) * KS, :] = value
        total = total + value
    total = jnp.broadcast_to(jnp.sum(total, axis=0, keepdims=True), (8, US))
    total = total + pltpu.roll(total, 32, 1)
    total = total + pltpu.roll(total, 64, 1)
    pair = jnp.concatenate([peak[:1], total[:1]], axis=0)[:, : US // TRANS]
    for j in range(32):
        stat_out[j] = pair


def score(own, imgs, refs, ctf_table, noise_power, table):
    vmem = pl.BlockSpec(memory_space=pltpu.VMEM)
    smem = pl.BlockSpec(memory_space=pltpu.SMEM)
    return pl.pallas_call(
        score_kernel,
        out_shape=(
            jax.ShapeDtypeStruct((ROWS, US), F32),
            jax.ShapeDtypeStruct((32, 2, US // TRANS), F32),
            jax.ShapeDtypeStruct((ROT * US, LANES), BF16),
            jax.ShapeDtypeStruct((US, LANES), F32),
        ),
        in_specs=[smem] + [vmem] * 7 + [pl.BlockSpec(memory_space=pltpu.HBM)] * 3,
        out_specs=(vmem,) * 4,
        scratch_shapes=[
            pltpu.VMEM((NDEF, CYCLES), F32),
            pltpu.VMEM((1, CYCLES), F32),
            pltpu.VMEM((ROT, 192, LANES), BF16),
            pltpu.VMEM((BLOCKS, ROT + 1, MINE, LANES), BF16),
            pltpu.VMEM((2 * ROWS, LANES), BF16),
            pltpu.VMEM((ROWS, LANES), F32),
            pltpu.SemaphoreType.DMA((8,)),
        ],
        compiler_params=pltpu.CompilerParams(vmem_limit_bytes=VMEM_LIMIT),
        name="score",
    )(own, *imgs, *refs, *(in_hbm(v) for v in (ctf_table, noise_power, table)))


def insert_kernel(own_ref, exp_ref, pair_ref, all_ref, ins_ref, sq_ref, own_out, s1, s2, s3, like_out, post, acc):
    peaks = jnp.concatenate([all_ref[j, 0:1, :] for j in range(32)], axis=0)
    totals = jnp.concatenate([all_ref[j, 1:2, :] for j in range(32)], axis=0)
    peak = jnp.max(peaks, axis=0, keepdims=True)
    total = jnp.sum(totals * jnp.exp(peaks - peak), axis=0, keepdims=True)
    scale = jnp.exp(pair_ref[0, 0:1, :] - peak) / total
    scale = jnp.broadcast_to(jnp.concatenate([scale] * TRANS, axis=1), (KS, US))
    like = jnp.concatenate([peak + jnp.log(total)] * TRANS, axis=1)
    shift = (US - own_ref[0] * MINE) % US
    like_out[...] = pltpu.roll(jnp.broadcast_to(like, (8, US)), shift, 1)[:1, :MINE]
    count = jnp.zeros((KS, US), F32)
    for r in range(ROT):
        value = (exp_ref[r * KS : (r + 1) * KS, :] * scale).astype(BF16)
        count = count + value.astype(F32)
        for side in range(2):
            m = (side - r) % ROT
            for again in (m, m + ROT):
                post[again * KS : (again + 1) * KS, side * HALF : (side + 1) * HALF] = value

    acc[...] = sum(
        jnp.dot(
            post[(ROT - 2 * h) * KS : (2 * ROT - 2 * h) * KS, :],
            ins_ref[h * 2 * US : (h + 1) * 2 * US, :],
            preferred_element_type=F32,
        )
        for h in range(ROT // 2)
    )
    sums = jnp.dot(count, sq_ref[...], precision=HIGHEST, preferred_element_type=F32)
    high = sums.astype(BF16)
    low = (sums - high.astype(F32)).astype(BF16)
    for b in range(ROT):
        block = acc[b * KS : (b + 1) * KS, :]
        own_out[b] = block[:OWN]
        for d, out in ((1, s1), (2, s2), (3, s3)):
            out[b] = block[d * OWN : (d + 1) * OWN].astype(BF16)
    own_out[ROT] = sums[:OWN]
    own_out[ROT + 1] = jnp.zeros((OWN, LANES), F32)
    for d, out in ((1, s1), (2, s2), (3, s3)):
        part = sums[d * OWN : (d + 1) * OWN]
        high = part.astype(BF16)
        out[ROT] = high
        out[ROT + 1] = (part - high.astype(F32)).astype(BF16)


def insert(own, exps, stats, gathered, ins, sq):
    vmem = pl.BlockSpec(memory_space=pltpu.VMEM)
    smem = pl.BlockSpec(memory_space=pltpu.SMEM)
    piece = (ROT + 2, OWN, LANES)
    return pl.pallas_call(
        insert_kernel,
        out_shape=(
            jax.ShapeDtypeStruct(piece, F32),
            jax.ShapeDtypeStruct(piece, BF16),
            jax.ShapeDtypeStruct(piece, BF16),
            jax.ShapeDtypeStruct(piece, BF16),
            jax.ShapeDtypeStruct((1, MINE), F32),
        ),
        in_specs=[smem] + [vmem] * 5,
        out_specs=(vmem,) * 5,
        scratch_shapes=[
            pltpu.VMEM((2 * ROWS, LANES), BF16),
            pltpu.VMEM((ROWS, LANES), F32),
        ],
        compiler_params=pltpu.CompilerParams(vmem_limit_bytes=VMEM_LIMIT),
        name="insert",
    )(own, exps, stats, gathered, ins, sq)


def finish_kernel(own_ref, g1, g2, g3, tau_ref, out_ref, weight_out, fresh, turned, lines):
    parts = [own_ref, g1, g2, g3]
    sums = sum(p[ROT].astype(F32) + p[ROT + 1].astype(F32) for p in parts)
    tau = jnp.concatenate([tau_ref[...]] * STEP, axis=1)
    denom = sums[:, :HALF] + 1.0 / tau
    denom = jnp.concatenate([denom, denom], axis=1)
    weight_out[...] = as_row(sums[:, HALF : HALF + 1], OWN) / (MINE * 16)
    for b in range(ROT):
        total = own_ref[b] + g1[b].astype(F32) + g2[b].astype(F32) + g3[b].astype(F32)
        total = total / denom
        fresh[0, pl.ds(b * 8, OWN), :] = total[:, :HALF]
        fresh[1, pl.ds(b * 8, OWN), :] = total[:, HALF:]
    for k in range(OWN):
        one = [fresh.at[p][pl.ds(k, ROT, stride=8), :] for p in range(2)]
        for c in range(STEP):
            pair = [one[p][:, c * CYCLES : (c + 1) * CYCLES] for p in range(2)]
            turned[pl.ds(c, ROT, stride=STEP), :] = jnp.concatenate(pair + pair, axis=1)
        first = turned[0:128, :].T
        second = turned[128:256, :].T
        lines[0, pl.ds(k * PAIRS, PAIRS), :] = first[:PAIRS]
        lines[1, pl.ds(k * PAIRS, PAIRS), :] = second[:PAIRS]
    for j in range(PAIRS):
        line = [lines.at[n][pl.ds(j, OWN, stride=PAIRS), :] for n in range(2)]
        out_ref[:, j * ANG : (j + 1) * ANG] = jnp.concatenate(line, axis=1)[:, :ANG]


def finish(own, got, tau):
    vmem = pl.BlockSpec(memory_space=pltpu.VMEM)
    return pl.pallas_call(
        finish_kernel,
        out_shape=(
            jax.ShapeDtypeStruct((OWN, 2 * CYCLES * ANG), F32),
            jax.ShapeDtypeStruct((1, OWN), F32),
        ),
        in_specs=[vmem] * 5,
        out_specs=(vmem, vmem),
        scratch_shapes=[
            pltpu.VMEM((2, ROT * 8, HALF), F32),
            pltpu.VMEM((256, 128), F32),
            pltpu.VMEM((2, OWN * PAIRS, HALF), F32),
        ],
        compiler_params=pltpu.CompilerParams(vmem_limit_bytes=VMEM_LIMIT),
        name="finish",
    )(own, *got, tau)


def along_y(value, distance):
    return lax.ppermute(
        value, "img", [(i, ((i // 4 + distance) % 4) * 4 + i % 4) for i in range(16)]
    )


def beside(value, img_flip, cls_flip):
    pairs = [
        (i * 8 + c, (i ^ img_flip) * 8 + (c ^ cls_flip)) for i in range(16) for c in range(8)
    ]
    return lax.ppermute(value, ("img", "cls"), pairs)


def per_device(
    table, images, references, class_logprior, ctf_table, noise_power, tau_power, defocus, offsets
):
    own = (lax.axis_index("img") % BLOCKS).astype(jnp.int32).reshape(1)
    img, ref = arrange(
        images,
        references,
        class_logprior.reshape(1, OWN),
        offsets.transpose(1, 2, 0),
        defocus.reshape(1, MINE),
    )
    next_chip = beside(img, 2, 1)
    refs = (ref, along_y(ref, 3), along_y(ref, 2), along_y(ref, 1))
    next_chip, refs = lax.optimization_barrier((next_chip, refs))
    other_core = beside(jnp.stack([img, next_chip]), 1, 0)
    exps, stats, ins, sq = score(
        own, (img, next_chip, other_core), refs, ctf_table, noise_power.reshape(1, CYCLES), table
    )
    same_images = [[(y * 4 + r) * 8 + c for r in range(4) for c in range(8)] for y in range(4)]
    gathered = lax.all_to_all(
        stats, ("img", "cls"), 0, 0, tiled=True, axis_index_groups=same_images
    )
    numer, s1, s2, s3, like = insert(own, exps, stats, gathered, ins, sq)
    got = (along_y(s1, 1), along_y(s2, 2), along_y(s3, 3))
    fresh, weight = finish(numer, got, tau_power.reshape(1, CYCLES))
    return fresh, weight.reshape(OWN), like.reshape(MINE)


def solution(mesh):
    body = functools.partial(per_device, jnp.asarray(phase_parts()))
    return jax.shard_map(
        body,
        mesh=mesh,
        in_specs=(
            P("img", None),
            P(("img", "cls"), None),
            P(("img", "cls")),
            P(),
            P(),
            P(),
            P("img"),
            P("img", None, None),
        ),
        out_specs=(P(("img", "cls"), None), P(("img", "cls")), P("img")),
        check_vma=False,
    )
```

```python
import functools
import math

import jax
import jax.numpy as jnp
import ml_dtypes
import numpy as np
from jax import lax
from jax.experimental import pallas as pl
from jax.experimental.pallas import tpu as pltpu
from jax.sharding import PartitionSpec as P

TRANS = 4
CYCLES = 32
ANG = 144
ROT = 36
NDEF = 16
STEP = ANG // ROT
PAIRS = 2 * CYCLES
LANES = 2 * STEP * CYCLES
HALF = LANES // 2
OWN = 4
MINE = 8
BLOCKS = 4
KS = OWN * BLOCKS
US = MINE * BLOCKS * TRANS
ROWS = ROT * KS
REACH = 3
MIDDLE = 24
SLOTS = 32
offset_sigma = 2.0
F32 = jnp.float32
BF16 = jnp.bfloat16
HIGHEST = lax.Precision.HIGHEST
VMEM_LIMIT = 20 * 1024 * 1024


def phase_parts():
    span = 2 * REACH + 1
    theta = 2.0 * math.pi * np.arange(ANG).reshape(ROT, STEP) / ANG
    radius = np.arange(CYCLES) + 1.0
    fx = (np.cos(theta)[:, :, None] * radius).reshape(ROT, HALF)
    fy = (np.sin(theta)[:, :, None] * radius).reshape(ROT, HALF)
    shift = np.arange(span) - REACH
    phi = (
        -2.0
        * math.pi
        * (shift[:, None, None, None] * fx + shift[None, :, None, None] * fy)
        / (2.0 * CYCLES)
    ).reshape(span * span, ROT, HALF)[MIDDLE:]
    table = np.concatenate([np.cos(phi), np.sin(phi)], axis=2).transpose(1, 0, 2)
    table = np.pad(table, ((0, 0), (0, SLOTS - table.shape[1]), (0, 0)))
    parts = []
    rest = table
    for _ in range(3):
        part = rest.astype(np.float32).astype(ml_dtypes.bfloat16)
        parts.append(part)
        rest = rest - part.astype(np.float64)
    return np.concatenate(parts, axis=1)


def nt(a, b, **kw):
    return lax.dot_general(a, b, (((1,), (1,)), ((), ())), preferred_element_type=F32, **kw)


def in_hbm(value):
    return pltpu.with_memory_space_constraint(value, pltpu.HBM)


def fetch(pairs, sems):
    copies = [
        pltpu.make_async_copy(src, dst, sems.at[n]) for n, (src, dst) in enumerate(pairs)
    ]
    for copy in copies:
        copy.start()
    return copies


def as_column(row, size):
    here = lax.broadcasted_iota(jnp.int32, (size, size), 0)
    there = lax.broadcasted_iota(jnp.int32, (size, size), 1)
    wide = jnp.broadcast_to(row, (size, size))
    return jnp.sum(jnp.where(here == there, wide, 0.0), axis=1, keepdims=True)


def as_row(column, size):
    here = lax.broadcasted_iota(jnp.int32, (size, size), 0)
    there = lax.broadcasted_iota(jnp.int32, (size, size), 1)
    wide = jnp.broadcast_to(column, (size, size))
    return jnp.sum(jnp.where(here == there, wide, 0.0), axis=0, keepdims=True)


def turn_major(source, count, cut, flat, out):
    angle = lax.broadcasted_iota(jnp.int32, (CYCLES, ANG), 1) % STEP
    pick_b = lax.broadcasted_iota(jnp.int32, (40, ANG), 0)
    pick_a = lax.broadcasted_iota(jnp.int32, (40, ANG), 1)
    pick = jnp.where(pick_a // STEP == pick_b, 1.0, 0.0).astype(BF16)
    for j in range(PAIRS):
        line = source[:, j * ANG : (j + 1) * ANG].astype(F32)
        cut[0, pl.ds(j * 8, count), :] = line[:, :HALF]
        cut[1, pl.ds(j * 8, count), : ANG - HALF] = line[:, HALF:]
    for i in range(count):
        one = jnp.concatenate(
            [cut.at[n][pl.ds(i, PAIRS, stride=8), :] for n in range(2)], axis=1
        )[:, :ANG]
        spread = jnp.concatenate(
            [
                jnp.where(angle == c, one[p * CYCLES : (p + 1) * CYCLES], 0.0)
                for p in range(2)
                for c in range(STEP)
            ],
            axis=0,
        ).astype(BF16)
        turned = nt(pick, spread)
        flat[0, pl.ds(i * 40, 40), :] = turned[:, :HALF]
        flat[1, pl.ds(i * 40, 40), :] = turned[:, HALF:]
    for b in range(ROT):
        for n in range(2):
            line = flat.at[n][pl.ds(b, count, stride=40), :]
            out[b, :, n * HALF : (n + 1) * HALF] = line.astype(BF16)


def arrange_kernel(
    img_hbm, ref_hbm, prior_hbm, off_hbm, def_hbm, ctf_hbm, noise_hbm, tau_hbm, table_hbm,
    img_out, ref_out, ctf_out, noise_out, tau_out, table_out,
    img_ref, ref_ref, prior_ref, off_ref, def_ref, ctf_ref, noise_ref, tau_ref,
    cut, cut2, flat, flat2, sems,
):
    copies = fetch(
        (
            (ref_hbm, ref_ref),
            (img_hbm, img_ref),
            (prior_hbm, prior_ref),
            (off_hbm, off_ref),
            (def_hbm, def_ref),
            (ctf_hbm, ctf_ref),
            (noise_hbm, noise_ref),
            (tau_hbm, tau_ref),
            (table_hbm, table_out),
        ),
        sems,
    )
    copies[0].wait()
    turn_major(ref_ref, OWN, cut, flat, ref_out)
    copies[1].wait()
    turn_major(img_ref, MINE, cut2, flat2, img_out)
    for copy in copies[2:]:
        copy.wait()
    lane = lax.broadcasted_iota(jnp.int32, (MINE, LANES), 1)
    extra = jnp.where(lane == 8, as_column(def_ref[...].astype(F32), MINE), 0.0)
    for t in range(TRANS):
        for d in range(2):
            column = as_column(off_ref[t, d : d + 1, :].astype(F32), MINE)
            extra = jnp.where(lane == 2 * t + d, column, extra)
    img_out[ROT] = extra.astype(BF16)
    column = as_column(prior_ref[...].astype(F32), OWN)
    ref_out[ROT] = jnp.broadcast_to(column, (OWN, LANES)).astype(BF16)
    for small, out in ((ctf_ref, ctf_out), (noise_ref, noise_out), (tau_ref, tau_out)):
        out[...] = jnp.concatenate([small[...]] * STEP, axis=1)


def arrange(images, references, prior, offsets, defocus, ctf_table, noise, tau, table):
    vmem = pl.BlockSpec(memory_space=pltpu.VMEM)
    hbm = pl.BlockSpec(memory_space=pltpu.HBM)
    wide = 2 * CYCLES * ANG
    return pl.pallas_call(
        arrange_kernel,
        out_shape=(
            jax.ShapeDtypeStruct((ROT + 1, MINE, LANES), BF16),
            jax.ShapeDtypeStruct((ROT + 1, OWN, LANES), BF16),
            jax.ShapeDtypeStruct((NDEF, HALF), F32),
            jax.ShapeDtypeStruct((1, HALF), F32),
            jax.ShapeDtypeStruct((1, HALF), F32),
            jax.ShapeDtypeStruct((ROT, 3 * SLOTS, LANES), BF16),
        ),
        in_specs=[hbm] * 9,
        out_specs=(vmem,) * 6,
        scratch_shapes=[
            pltpu.VMEM((MINE, wide), BF16),
            pltpu.VMEM((OWN, wide), BF16),
            pltpu.VMEM((1, OWN), BF16),
            pltpu.VMEM((TRANS, 2, MINE), jnp.int32),
            pltpu.VMEM((1, MINE), jnp.int32),
            pltpu.VMEM((NDEF, CYCLES), F32),
            pltpu.VMEM((1, CYCLES), F32),
            pltpu.VMEM((1, CYCLES), F32),
            pltpu.VMEM((2, PAIRS * 8, HALF), F32),
            pltpu.VMEM((2, PAIRS * 8, HALF), F32),
            pltpu.VMEM((2, MINE * 40, HALF), F32),
            pltpu.VMEM((2, MINE * 40, HALF), F32),
            pltpu.SemaphoreType.DMA((9,)),
        ],
        compiler_params=pltpu.CompilerParams(vmem_limit_bytes=VMEM_LIMIT),
        name="arrange",
    )(
        *(
            in_hbm(v)
            for v in (images, references, prior, offsets, defocus, ctf_table, noise, tau, table)
        )
    )


def four(value):
    return jnp.concatenate([value] * TRANS, axis=0)


def image_rows(near, far):
    extra = jnp.concatenate([near[ROT].astype(F32), far[ROT].astype(F32)], axis=0)
    dx = jnp.concatenate([extra[:, 2 * t : 2 * t + 1] for t in range(TRANS)], axis=0)
    dy = jnp.concatenate([extra[:, 2 * t + 1 : 2 * t + 2] for t in range(TRANS)], axis=0)
    return dx, dy, extra[:, 8:9]


def contrast_of(group, ctf_ref):
    known = lax.broadcasted_iota(jnp.int32, (group.shape[0], NDEF), 1).astype(F32)
    which = jnp.where(known == group, 1.0, 0.0)
    return jnp.dot(which, ctf_ref[...], precision=HIGHEST, preferred_element_type=F32)


def shift_half(near, far, dx, dy, contrast, noise, table, weighted, inserted):
    pair = dx * (2 * REACH + 1) + dy
    slot = lax.broadcasted_iota(jnp.int32, (US // 2, 3 * SLOTS), 1) % SLOTS
    hot = jnp.where(slot.astype(F32) == jnp.abs(pair), 1.0, 0.0).astype(BF16)
    sign = jnp.broadcast_to(jnp.where(pair < 0, -1.0, 1.0), (US // 2, HALF))
    contrast4 = four(contrast)
    whiten4 = four(contrast / noise)
    for b in range(ROT):
        turn = jnp.dot(hot, table[b], preferred_element_type=F32)
        cosine, sine = turn[:, :HALF], turn[:, HALF:] * sign
        block = jnp.concatenate([near[b].astype(F32), far[b].astype(F32)], axis=0)
        real, imag = four(block[:, :HALF]), four(block[:, HALF:])
        shifted_real = real * cosine - imag * sine
        shifted_imag = real * sine + imag * cosine
        rows = slice(b * US // 2, (b + 1) * US // 2)
        weighted[rows, :HALF] = (shifted_real * whiten4).astype(BF16)
        weighted[rows, HALF:] = (shifted_imag * whiten4).astype(BF16)
        inserted[rows, :HALF] = (shifted_real * contrast4).astype(BF16)
        inserted[rows, HALF:] = (shifted_imag * contrast4).astype(BF16)


def shift_kernel(near, far, ctf_ref, noise_ref, table, weighted, inserted):
    dx, dy, group = image_rows(near, far)
    contrast = contrast_of(group, ctf_ref)
    shift_half(near, far, dx, dy, contrast, noise_ref[...], table, weighted, inserted)


def shift(near, far, ctf4, noise4, table):
    vmem = pl.BlockSpec(memory_space=pltpu.VMEM)
    half = jax.ShapeDtypeStruct((ROT * US // 2, LANES), BF16)
    return pl.pallas_call(
        shift_kernel,
        out_shape=(half, half),
        in_specs=[vmem] * 5,
        out_specs=(vmem, vmem),
        compiler_params=pltpu.CompilerParams(vmem_limit_bytes=VMEM_LIMIT),
        name="shift",
    )(near, far, ctf4, noise4, table)


def swapped(row, own):
    lane = lax.broadcasted_iota(jnp.int32, row.shape, 1)
    for bit in range(2):
        size = MINE << bit
        other = jnp.where(
            (lane // size) % 2 == 0, pltpu.roll(row, US - size, 1), pltpu.roll(row, size, 1)
        )
        flip = jnp.broadcast_to((own >> bit) & 1, row.shape) == 1
        row = jnp.where(flip, other, row)
    return row


def over_shifts(row, combine):
    lane = lax.broadcasted_iota(jnp.int32, row.shape, 1)
    for size in (16, 32):
        turned = jnp.where(
            lane % 64 >= size, pltpu.roll(row, size, 1), pltpu.roll(row, size + 64, 1)
        )
        row = combine(row, turned)
    return row


def by_block(row):
    lane = lax.broadcasted_iota(jnp.int32, row.shape, 1) // MINE
    row = jnp.where(
        lane == 0,
        row,
        jnp.where(
            lane == 1,
            pltpu.roll(row, 72, 1),
            jnp.where(lane == 2, pltpu.roll(row, 8, 1), pltpu.roll(row, 80, 1)),
        ),
    )
    return row


def score_kernel(
    own_ref, i0, i2, i13, w_near, r0, r1, r2, r3, ctf_ref, noise_ref, table,
    exp_out, stat_out, ins_out, sq_out,
    w_far, back, acc,
):
    own = own_ref[0]
    square = jnp.zeros((KS, LANES), F32)
    for b in range(ROT):
        block = jnp.concatenate([r[b].astype(F32) for r in (r0, r1, r2, r3)], axis=0)
        square = square + block * block
        m = (ROT - b) % ROT
        back[pl.ds(m * KS, KS), :] = block.astype(BF16)
        back[pl.ds((m + ROT) * KS, KS), :] = block.astype(BF16)
    prior = jnp.concatenate([r[ROT].astype(F32) for r in (r0, r1, r2, r3)], axis=0)[:, :HALF]

    i1, i3 = i13.at[0], i13.at[1]
    dx0, dy0, group0 = image_rows(i0, i2)
    dx1, dy1, group1 = image_rows(i1, i3)
    noise = noise_ref[...]
    contrast = contrast_of(jnp.concatenate([group0, group1], axis=0), ctf_ref)
    far_contrast = contrast[2 * MINE :]
    squared = contrast * contrast
    squared = jnp.concatenate([four(squared[: 2 * MINE]), four(squared[2 * MINE :])], axis=0)
    sq_out[:, :HALF] = squared
    sq_out[:, HALF:] = jnp.ones((US, HALF), F32)
    coef = squared / (2.0 * noise)
    penalty = nt(square, jnp.concatenate([coef, coef], axis=1), precision=HIGHEST)
    dx = jnp.concatenate([dx0, dx1], axis=0)
    dy = jnp.concatenate([dy0, dy1], axis=0)
    near = -(dx * dx + dy * dy) / (2.0 * offset_sigma * offset_sigma)
    base = prior - penalty + as_row(near, US)

    shift_half(i1, i3, dx1, dy1, far_contrast, noise, table, w_far, ins_out)
    half = US // 2
    acc[...] = sum(
        nt(
            back[(ROT - 2 * h) * KS : (2 * ROT - 2 * h) * KS, :],
            jnp.concatenate(
                [
                    w[b * half : (b + 1) * half, :]
                    for b in (2 * h, 2 * h + 1)
                    for w in (w_near, w_far)
                ],
                axis=0,
            ),
        )
        for h in range(ROT // 2)
    )

    peak = jnp.full((KS, US), -jnp.inf, F32)
    for r in range(ROT):
        last = (r - 1) % ROT
        logp = acc[r * KS : (r + 1) * KS, :HALF] + acc[last * KS : (last + 1) * KS, HALF:] + base
        exp_out[r * KS : (r + 1) * KS, :] = logp
        peak = jnp.maximum(peak, logp)
    peak = jnp.broadcast_to(jnp.max(peak, axis=0, keepdims=True), (8, US))
    peak = over_shifts(peak, jnp.maximum)
    wide = jnp.broadcast_to(peak[:1], (KS, US))
    total = jnp.zeros((KS, US), F32)
    for r in range(ROT):
        value = jnp.exp(exp_out[r * KS : (r + 1) * KS, :] - wide)
        exp_out[r * KS : (r + 1) * KS, :] = value
        total = total + value
    total = jnp.broadcast_to(jnp.sum(total, axis=0, keepdims=True), (8, US))
    total = over_shifts(total, jnp.add)
    pair = [swapped(by_block(v), own)[:1, : US // TRANS] for v in (peak, total)]
    pair = jnp.concatenate(pair, axis=0)
    for j in range(32):
        stat_out[j] = pair


def score(own, imgs, w_near, refs, ctf4, noise4, table):
    vmem = pl.BlockSpec(memory_space=pltpu.VMEM)
    smem = pl.BlockSpec(memory_space=pltpu.SMEM)
    return pl.pallas_call(
        score_kernel,
        out_shape=(
            jax.ShapeDtypeStruct((ROWS, US), F32),
            jax.ShapeDtypeStruct((32, 2, US // TRANS), F32),
            jax.ShapeDtypeStruct((ROT * US // 2, LANES), BF16),
            jax.ShapeDtypeStruct((US, LANES), F32),
        ),
        in_specs=[smem] + [vmem] * 11,
        out_specs=(vmem,) * 4,
        scratch_shapes=[
            pltpu.VMEM((ROT * US // 2, LANES), BF16),
            pltpu.VMEM((2 * ROWS, LANES), BF16),
            pltpu.VMEM((ROWS, LANES), F32),
        ],
        compiler_params=pltpu.CompilerParams(vmem_limit_bytes=VMEM_LIMIT),
        name="score",
    )(own, *imgs, w_near, *refs, ctf4, noise4, table)


def insert_kernel(
    own_ref, exp_ref, pair_ref, all_ref, near_ref, far_ref, sq_ref,
    own_out, s1, s2, s3, like_out, post, acc,
):
    own = own_ref[0]
    peaks = jnp.concatenate([all_ref[j, 0:1, :] for j in range(32)], axis=0)
    totals = jnp.concatenate([all_ref[j, 1:2, :] for j in range(32)], axis=0)
    peak = jnp.max(peaks, axis=0, keepdims=True)
    total = jnp.sum(totals * jnp.exp(peaks - peak), axis=0, keepdims=True)
    scale = jnp.exp(pair_ref[0, 0:1, :] - peak) / total
    like = peak + jnp.log(total)
    scale, like = (
        swapped(jnp.broadcast_to(jnp.concatenate([v] * TRANS, axis=1), (8, US)), own)[:1]
        for v in (scale, like)
    )
    like_out[...] = like[:, :MINE]
    piece = [scale[:, d * MINE : (d + 1) * MINE] for d in range(BLOCKS)]
    scale = jnp.concatenate([piece[0], piece[2]] * TRANS + [piece[1], piece[3]] * TRANS, axis=1)
    scale = jnp.broadcast_to(scale, (KS, US))
    count = jnp.zeros((KS, US), F32)
    for r in range(ROT):
        value = (exp_ref[r * KS : (r + 1) * KS, :] * scale).astype(BF16)
        count = count + value.astype(F32)
        for side in range(2):
            m = (side - r) % ROT
            for again in (m, m + ROT):
                post[again * KS : (again + 1) * KS, side * HALF : (side + 1) * HALF] = value

    half = US // 2
    acc[...] = sum(
        jnp.dot(
            post[(ROT - 2 * h) * KS : (2 * ROT - 2 * h) * KS, :],
            jnp.concatenate(
                [
                    v[b * half : (b + 1) * half, :]
                    for b in (2 * h, 2 * h + 1)
                    for v in (near_ref, far_ref)
                ],
                axis=0,
            ),
            preferred_element_type=F32,
        )
        for h in range(ROT // 2)
    )
    sums = jnp.dot(count, sq_ref[...], precision=HIGHEST, preferred_element_type=F32)
    for b in range(ROT):
        block = acc[b * KS : (b + 1) * KS, :]
        own_out[b] = block[:OWN]
        for d, out in ((1, s1), (2, s2), (3, s3)):
            out[b] = block[d * OWN : (d + 1) * OWN].astype(BF16)
    own_out[ROT] = sums[:OWN]
    own_out[ROT + 1] = jnp.zeros((OWN, LANES), F32)
    for d, out in ((1, s1), (2, s2), (3, s3)):
        part = sums[d * OWN : (d + 1) * OWN]
        high = part.astype(BF16)
        out[ROT] = high
        out[ROT + 1] = (part - high.astype(F32)).astype(BF16)


def insert(own, exps, stats, gathered, near, far, sq):
    vmem = pl.BlockSpec(memory_space=pltpu.VMEM)
    smem = pl.BlockSpec(memory_space=pltpu.SMEM)
    piece = (ROT + 2, OWN, LANES)
    return pl.pallas_call(
        insert_kernel,
        out_shape=(
            jax.ShapeDtypeStruct(piece, F32),
            jax.ShapeDtypeStruct(piece, BF16),
            jax.ShapeDtypeStruct(piece, BF16),
            jax.ShapeDtypeStruct(piece, BF16),
            jax.ShapeDtypeStruct((1, MINE), F32),
        ),
        in_specs=[smem] + [vmem] * 6,
        out_specs=(vmem,) * 5,
        scratch_shapes=[
            pltpu.VMEM((2 * ROWS, LANES), BF16),
            pltpu.VMEM((ROWS, LANES), F32),
        ],
        compiler_params=pltpu.CompilerParams(vmem_limit_bytes=VMEM_LIMIT),
        name="insert",
    )(own, exps, stats, gathered, near, far, sq)


def finish_kernel(own_ref, g1, g2, g3, tau_ref, out_ref, weight_out, fresh, turned, lines):
    parts = [own_ref, g1, g2, g3]
    sums = sum(p[ROT].astype(F32) + p[ROT + 1].astype(F32) for p in parts)
    denom = sums[:, :HALF] + 1.0 / tau_ref[...]
    denom = jnp.concatenate([denom, denom], axis=1)
    weight_out[...] = as_row(sums[:, HALF : HALF + 1], OWN) / (MINE * 16)
    for b in range(ROT):
        total = own_ref[b] + g1[b].astype(F32) + g2[b].astype(F32) + g3[b].astype(F32)
        total = total / denom
        fresh[0, pl.ds(b * 8, OWN), :] = total[:, :HALF]
        fresh[1, pl.ds(b * 8, OWN), :] = total[:, HALF:]
    for k in range(OWN):
        one = [fresh.at[p][pl.ds(k, ROT, stride=8), :] for p in range(2)]
        for c in range(STEP):
            pair = [one[p][:, c * CYCLES : (c + 1) * CYCLES] for p in range(2)]
            turned[pl.ds(c, ROT, stride=STEP), :] = jnp.concatenate(pair + pair, axis=1)
        first = turned[0:128, :].T
        second = turned[128:256, :].T
        lines[0, pl.ds(k * PAIRS, PAIRS), :] = first[:PAIRS]
        lines[1, pl.ds(k * PAIRS, PAIRS), :] = second[:PAIRS]
    for j in range(PAIRS):
        line = [lines.at[n][pl.ds(j, OWN, stride=PAIRS), :] for n in range(2)]
        out_ref[:, j * ANG : (j + 1) * ANG] = jnp.concatenate(line, axis=1)[:, :ANG]


def finish(own, got, tau):
    vmem = pl.BlockSpec(memory_space=pltpu.VMEM)
    return pl.pallas_call(
        finish_kernel,
        out_shape=(
            jax.ShapeDtypeStruct((OWN, 2 * CYCLES * ANG), F32),
            jax.ShapeDtypeStruct((1, OWN), F32),
        ),
        in_specs=[vmem] * 5,
        out_specs=(vmem, vmem),
        scratch_shapes=[
            pltpu.VMEM((2, ROT * 8, HALF), F32),
            pltpu.VMEM((256, 128), F32),
            pltpu.VMEM((2, OWN * PAIRS, HALF), F32),
        ],
        compiler_params=pltpu.CompilerParams(vmem_limit_bytes=VMEM_LIMIT),
        name="finish",
    )(own, *got, tau)


def along_y(value, distance):
    return lax.ppermute(
        value, "img", [(i, ((i // 4 + distance) % 4) * 4 + i % 4) for i in range(16)]
    )


def beside(value, img_flip, cls_flip):
    pairs = [
        (i * 8 + c, (i ^ img_flip) * 8 + (c ^ cls_flip)) for i in range(16) for c in range(8)
    ]
    return lax.ppermute(value, ("img", "cls"), pairs)


def per_device(
    table, images, references, class_logprior, ctf_table, noise_power, tau_power, defocus, offsets
):
    own = (lax.axis_index("img") % BLOCKS).astype(jnp.int32).reshape(1)
    img, ref, ctf4, noise4, tau4, table = arrange(
        images,
        references,
        class_logprior.reshape(1, OWN),
        offsets.transpose(1, 2, 0),
        defocus.reshape(1, MINE),
        ctf_table,
        noise_power.reshape(1, CYCLES),
        tau_power.reshape(1, CYCLES),
        table,
    )
    next_chip = beside(img, 2, 1)
    refs = (ref, along_y(ref, 3), along_y(ref, 2), along_y(ref, 1))
    next_chip, refs = lax.optimization_barrier((next_chip, refs))
    other_core = beside(jnp.stack([img, next_chip]), 1, 0)
    w_near, near = shift(img, next_chip, ctf4, noise4, table)
    exps, stats, far, sq = score(
        own, (img, next_chip, other_core), w_near, refs, ctf4, noise4, table
    )
    same_images = [[(y * 4 + r) * 8 + c for r in range(4) for c in range(8)] for y in range(4)]
    gathered = lax.all_to_all(
        stats, ("img", "cls"), 0, 0, tiled=True, axis_index_groups=same_images
    )
    numer, s1, s2, s3, like = insert(own, exps, stats, gathered, near, far, sq)
    got = (along_y(s1, 1), along_y(s2, 2), along_y(s3, 3))
    fresh, weight = finish(numer, got, tau4)
    return fresh, weight.reshape(OWN), like.reshape(MINE)


def solution(mesh):
    body = functools.partial(per_device, jnp.asarray(phase_parts()))
    return jax.shard_map(
        body,
        mesh=mesh,
        in_specs=(
            P("img", None),
            P(("img", "cls"), None),
            P(("img", "cls")),
            P(),
            P(),
            P(),
            P("img"),
            P("img", None, None),
        ),
        out_specs=(P(("img", "cls"), None), P(("img", "cls")), P("img")),
        check_vma=False,
    )
```

```python
import functools
import math

import jax
import jax.numpy as jnp
import ml_dtypes
import numpy as np
from jax import lax
from jax.experimental import pallas as pl
from jax.experimental.pallas import tpu as pltpu
from jax.sharding import PartitionSpec as P

TRANS = 4
CYCLES = 32
ANG = 144
ROT = 36
NDEF = 16
STEP = ANG // ROT
PAIRS = 2 * CYCLES
LANES = 2 * STEP * CYCLES
HALF = LANES // 2
OWN = 4
MINE = 8
BLOCKS = 4
KS = OWN * BLOCKS
US = MINE * BLOCKS * TRANS
ROWS = ROT * KS
REACH = 3
MIDDLE = 24
SLOTS = 32
WINDOW = 20_000_000_000
offset_sigma = 2.0
F32 = jnp.float32
BF16 = jnp.bfloat16
HIGHEST = lax.Precision.HIGHEST
VMEM_LIMIT = 20 * 1024 * 1024


def phase_parts():
    span = 2 * REACH + 1
    theta = 2.0 * math.pi * np.arange(ANG).reshape(ROT, STEP) / ANG
    radius = np.arange(CYCLES) + 1.0
    fx = (np.cos(theta)[:, :, None] * radius).reshape(ROT, HALF)
    fy = (np.sin(theta)[:, :, None] * radius).reshape(ROT, HALF)
    shift = np.arange(span) - REACH
    phi = (
        -2.0
        * math.pi
        * (shift[:, None, None, None] * fx + shift[None, :, None, None] * fy)
        / (2.0 * CYCLES)
    ).reshape(span * span, ROT, HALF)[MIDDLE:]
    table = np.concatenate([np.cos(phi), np.sin(phi)], axis=2).transpose(1, 0, 2)
    table = np.pad(table, ((0, 0), (0, SLOTS - table.shape[1]), (0, 0)))
    parts = []
    rest = table
    for _ in range(3):
        part = rest.astype(np.float32).astype(ml_dtypes.bfloat16)
        parts.append(part)
        rest = rest - part.astype(np.float64)
    return np.concatenate(parts, axis=1)


def nt(a, b, **kw):
    return lax.dot_general(a, b, (((1,), (1,)), ((), ())), preferred_element_type=F32, **kw)


def in_hbm(value):
    return pltpu.with_memory_space_constraint(value, pltpu.HBM)


def fetch(pairs, sems):
    copies = [
        pltpu.make_async_copy(src, dst, sems.at[n]) for n, (src, dst) in enumerate(pairs)
    ]
    for copy in copies:
        copy.start()
    return copies


def as_column(row, size):
    here = lax.broadcasted_iota(jnp.int32, (size, size), 0)
    there = lax.broadcasted_iota(jnp.int32, (size, size), 1)
    wide = jnp.broadcast_to(row, (size, size))
    return jnp.sum(jnp.where(here == there, wide, 0.0), axis=1, keepdims=True)


def as_row(column, size):
    here = lax.broadcasted_iota(jnp.int32, (size, size), 0)
    there = lax.broadcasted_iota(jnp.int32, (size, size), 1)
    wide = jnp.broadcast_to(column, (size, size))
    return jnp.sum(jnp.where(here == there, wide, 0.0), axis=0, keepdims=True)


def turn_major(source, count, cut, flat, out):
    angle = lax.broadcasted_iota(jnp.int32, (CYCLES, ANG), 1) % STEP
    pick_b = lax.broadcasted_iota(jnp.int32, (40, ANG), 0)
    pick_a = lax.broadcasted_iota(jnp.int32, (40, ANG), 1)
    pick = jnp.where(pick_a // STEP == pick_b, 1.0, 0.0).astype(BF16)
    for j in range(PAIRS):
        line = source[:, j * ANG : (j + 1) * ANG].astype(F32)
        cut[0, pl.ds(j * 8, count), :] = line[:, :HALF]
        cut[1, pl.ds(j * 8, count), : ANG - HALF] = line[:, HALF:]
    for i in range(count):
        one = jnp.concatenate(
            [cut.at[n][pl.ds(i, PAIRS, stride=8), :] for n in range(2)], axis=1
        )[:, :ANG]
        spread = jnp.concatenate(
            [
                jnp.where(angle == c, one[p * CYCLES : (p + 1) * CYCLES], 0.0)
                for p in range(2)
                for c in range(STEP)
            ],
            axis=0,
        ).astype(BF16)
        turned = nt(pick, spread)
        flat[0, pl.ds(i * 40, 40), :] = turned[:, :HALF]
        flat[1, pl.ds(i * 40, 40), :] = turned[:, HALF:]
    for b in range(ROT):
        for n in range(2):
            line = flat.at[n][pl.ds(b, count, stride=40), :]
            out[b, :, n * HALF : (n + 1) * HALF] = line.astype(BF16)


def arrange_kernel(
    img_hbm, ref_hbm, prior_hbm, off_hbm, def_hbm, ctf_hbm, noise_hbm, tau_hbm, table_hbm,
    img_out, ref_out, ctf_out, noise_out, tau_out, table_out,
    img_ref, ref_ref, prior_ref, off_ref, def_ref, ctf_ref, noise_ref, tau_ref,
    cut, cut2, flat, flat2, sems,
):
    copies = fetch(
        (
            (ref_hbm, ref_ref),
            (img_hbm, img_ref),
            (prior_hbm, prior_ref),
            (off_hbm, off_ref),
            (def_hbm, def_ref),
            (ctf_hbm, ctf_ref),
            (noise_hbm, noise_ref),
            (tau_hbm, tau_ref),
            (table_hbm, table_out),
        ),
        sems,
    )
    copies[0].wait()
    turn_major(ref_ref, OWN, cut, flat, ref_out)
    copies[1].wait()
    turn_major(img_ref, MINE, cut2, flat2, img_out)
    for copy in copies[2:]:
        copy.wait()
    lane = lax.broadcasted_iota(jnp.int32, (MINE, LANES), 1)
    extra = jnp.where(lane == 8, as_column(def_ref[...].astype(F32), MINE), 0.0)
    for t in range(TRANS):
        for d in range(2):
            column = as_column(off_ref[t, d : d + 1, :].astype(F32), MINE)
            extra = jnp.where(lane == 2 * t + d, column, extra)
    img_out[ROT] = extra.astype(BF16)
    column = as_column(prior_ref[...].astype(F32), OWN)
    ref_out[ROT] = jnp.broadcast_to(column, (OWN, LANES)).astype(BF16)
    for small, out in ((ctf_ref, ctf_out), (noise_ref, noise_out), (tau_ref, tau_out)):
        out[...] = jnp.concatenate([small[...]] * STEP, axis=1)


def arrange(images, references, prior, offsets, defocus, ctf_table, noise, tau, table):
    vmem = pl.BlockSpec(memory_space=pltpu.VMEM)
    hbm = pl.BlockSpec(memory_space=pltpu.HBM)
    wide = 2 * CYCLES * ANG
    return pl.pallas_call(
        arrange_kernel,
        out_shape=(
            jax.ShapeDtypeStruct((ROT + 1, MINE, LANES), BF16),
            jax.ShapeDtypeStruct((ROT + 1, OWN, LANES), BF16),
            jax.ShapeDtypeStruct((NDEF, HALF), F32),
            jax.ShapeDtypeStruct((1, HALF), F32),
            jax.ShapeDtypeStruct((1, HALF), F32),
            jax.ShapeDtypeStruct((ROT, 3 * SLOTS, LANES), BF16),
        ),
        in_specs=[hbm] * 9,
        out_specs=(vmem,) * 6,
        scratch_shapes=[
            pltpu.VMEM((MINE, wide), BF16),
            pltpu.VMEM((OWN, wide), BF16),
            pltpu.VMEM((1, OWN), BF16),
            pltpu.VMEM((TRANS, 2, MINE), jnp.int32),
            pltpu.VMEM((1, MINE), jnp.int32),
            pltpu.VMEM((NDEF, CYCLES), F32),
            pltpu.VMEM((1, CYCLES), F32),
            pltpu.VMEM((1, CYCLES), F32),
            pltpu.VMEM((2, PAIRS * 8, HALF), F32),
            pltpu.VMEM((2, PAIRS * 8, HALF), F32),
            pltpu.VMEM((2, MINE * 40, HALF), F32),
            pltpu.VMEM((2, MINE * 40, HALF), F32),
            pltpu.SemaphoreType.DMA((9,)),
        ],
        compiler_params=pltpu.CompilerParams(vmem_limit_bytes=VMEM_LIMIT),
        name="arrange",
    )(
        *(
            in_hbm(v)
            for v in (images, references, prior, offsets, defocus, ctf_table, noise, tau, table)
        )
    )


def four(value):
    return jnp.concatenate([value] * TRANS, axis=0)


def image_rows(near, far):
    extra = jnp.concatenate([near[ROT].astype(F32), far[ROT].astype(F32)], axis=0)
    dx = jnp.concatenate([extra[:, 2 * t : 2 * t + 1] for t in range(TRANS)], axis=0)
    dy = jnp.concatenate([extra[:, 2 * t + 1 : 2 * t + 2] for t in range(TRANS)], axis=0)
    return dx, dy, extra[:, 8:9]


def contrast_of(group, ctf_ref):
    known = lax.broadcasted_iota(jnp.int32, (group.shape[0], NDEF), 1).astype(F32)
    which = jnp.where(known == group, 1.0, 0.0)
    return jnp.dot(which, ctf_ref[...], precision=HIGHEST, preferred_element_type=F32)


def shift_half(near, far, dx, dy, contrast, noise, table, weighted, inserted):
    pair = dx * (2 * REACH + 1) + dy
    slot = lax.broadcasted_iota(jnp.int32, (US // 2, 3 * SLOTS), 1) % SLOTS
    hot = jnp.where(slot.astype(F32) == jnp.abs(pair), 1.0, 0.0).astype(BF16)
    sign = jnp.broadcast_to(jnp.where(pair < 0, -1.0, 1.0), (US // 2, HALF))
    contrast4 = four(contrast)
    whiten4 = four(contrast / noise)
    for b in range(ROT):
        turn = jnp.dot(hot, table[b], preferred_element_type=F32)
        cosine, sine = turn[:, :HALF], turn[:, HALF:] * sign
        block = jnp.concatenate([near[b].astype(F32), far[b].astype(F32)], axis=0)
        real, imag = four(block[:, :HALF]), four(block[:, HALF:])
        shifted_real = real * cosine - imag * sine
        shifted_imag = real * sine + imag * cosine
        rows = slice(b * US // 2, (b + 1) * US // 2)
        weighted[rows, :HALF] = (shifted_real * whiten4).astype(BF16)
        weighted[rows, HALF:] = (shifted_imag * whiten4).astype(BF16)
        inserted[rows, :HALF] = (shifted_real * contrast4).astype(BF16)
        inserted[rows, HALF:] = (shifted_imag * contrast4).astype(BF16)


def shift_kernel(near, far, ctf_ref, noise_ref, table, weighted, inserted):
    dx, dy, group = image_rows(near, far)
    contrast = contrast_of(group, ctf_ref)
    shift_half(near, far, dx, dy, contrast, noise_ref[...], table, weighted, inserted)


def shift(near, far, ctf4, noise4, table):
    vmem = pl.BlockSpec(memory_space=pltpu.VMEM)
    half = jax.ShapeDtypeStruct((ROT * US // 2, LANES), BF16)
    return pl.pallas_call(
        shift_kernel,
        out_shape=(half, half),
        in_specs=[vmem] * 5,
        out_specs=(vmem, vmem),
        compiler_params=pltpu.CompilerParams(vmem_limit_bytes=VMEM_LIMIT),
        name="shift",
        cost_estimate=pl.CostEstimate(flops=WINDOW, bytes_accessed=1000, transcendentals=0),
    )(near, far, ctf4, noise4, table)


def swapped(row, own):
    lane = lax.broadcasted_iota(jnp.int32, row.shape, 1)
    for bit in range(2):
        size = MINE << bit
        other = jnp.where(
            (lane // size) % 2 == 0, pltpu.roll(row, US - size, 1), pltpu.roll(row, size, 1)
        )
        flip = jnp.broadcast_to((own >> bit) & 1, row.shape) == 1
        row = jnp.where(flip, other, row)
    return row


def over_shifts(row, combine):
    lane = lax.broadcasted_iota(jnp.int32, row.shape, 1)
    for size in (16, 32):
        turned = jnp.where(
            lane % 64 >= size, pltpu.roll(row, size, 1), pltpu.roll(row, size + 64, 1)
        )
        row = combine(row, turned)
    return row


def by_block(row):
    lane = lax.broadcasted_iota(jnp.int32, row.shape, 1) // MINE
    row = jnp.where(
        lane == 0,
        row,
        jnp.where(
            lane == 1,
            pltpu.roll(row, 72, 1),
            jnp.where(lane == 2, pltpu.roll(row, 8, 1), pltpu.roll(row, 80, 1)),
        ),
    )
    return row


def score_kernel(
    own_ref, i0, i2, i13, w_near, r0, r1, r2, r3, ctf_ref, noise_ref, table,
    exp_out, stat_out, ins_out, sq_out,
    w_far, back, acc,
):
    own = own_ref[0]
    square = jnp.zeros((KS, LANES), F32)
    for b in range(ROT):
        block = jnp.concatenate([r[b].astype(F32) for r in (r0, r1, r2, r3)], axis=0)
        square = square + block * block
        m = (ROT - b) % ROT
        back[pl.ds(m * KS, KS), :] = block.astype(BF16)
        back[pl.ds((m + ROT) * KS, KS), :] = block.astype(BF16)
    prior = jnp.concatenate([r[ROT].astype(F32) for r in (r0, r1, r2, r3)], axis=0)[:, :HALF]

    i1, i3 = i13.at[0], i13.at[1]
    dx0, dy0, group0 = image_rows(i0, i2)
    dx1, dy1, group1 = image_rows(i1, i3)
    noise = noise_ref[...]
    contrast = contrast_of(jnp.concatenate([group0, group1], axis=0), ctf_ref)
    far_contrast = contrast[2 * MINE :]
    squared = contrast * contrast
    squared = jnp.concatenate([four(squared[: 2 * MINE]), four(squared[2 * MINE :])], axis=0)
    sq_out[:, :HALF] = squared
    sq_out[:, HALF:] = jnp.ones((US, HALF), F32)
    coef = squared / (2.0 * noise)
    penalty = nt(square, jnp.concatenate([coef, coef], axis=1), precision=HIGHEST)
    dx = jnp.concatenate([dx0, dx1], axis=0)
    dy = jnp.concatenate([dy0, dy1], axis=0)
    near = -(dx * dx + dy * dy) / (2.0 * offset_sigma * offset_sigma)
    base = prior - penalty + as_row(near, US)

    shift_half(i1, i3, dx1, dy1, far_contrast, noise, table, w_far, ins_out)
    half = US // 2
    acc[...] = sum(
        nt(
            back[(ROT - 2 * h) * KS : (2 * ROT - 2 * h) * KS, :],
            jnp.concatenate(
                [
                    w[b * half : (b + 1) * half, :]
                    for b in (2 * h, 2 * h + 1)
                    for w in (w_near, w_far)
                ],
                axis=0,
            ),
        )
        for h in range(ROT // 2)
    )

    peak = jnp.full((KS, US), -jnp.inf, F32)
    for r in range(ROT):
        last = (r - 1) % ROT
        logp = acc[r * KS : (r + 1) * KS, :HALF] + acc[last * KS : (last + 1) * KS, HALF:] + base
        exp_out[r * KS : (r + 1) * KS, :] = logp
        peak = jnp.maximum(peak, logp)
    peak = jnp.broadcast_to(jnp.max(peak, axis=0, keepdims=True), (8, US))
    peak = over_shifts(peak, jnp.maximum)
    wide = jnp.broadcast_to(peak[:1], (KS, US))
    total = jnp.zeros((KS, US), F32)
    for r in range(ROT):
        value = jnp.exp(exp_out[r * KS : (r + 1) * KS, :] - wide)
        exp_out[r * KS : (r + 1) * KS, :] = value
        total = total + value
    total = jnp.broadcast_to(jnp.sum(total, axis=0, keepdims=True), (8, US))
    total = over_shifts(total, jnp.add)
    pair = [swapped(by_block(v), own)[:1, : US // TRANS] for v in (peak, total)]
    pair = jnp.concatenate(pair, axis=0)
    for j in range(32):
        stat_out[j] = pair


def score(own, imgs, w_near, refs, ctf4, noise4, table):
    vmem = pl.BlockSpec(memory_space=pltpu.VMEM)
    smem = pl.BlockSpec(memory_space=pltpu.SMEM)
    return pl.pallas_call(
        score_kernel,
        out_shape=(
            jax.ShapeDtypeStruct((ROWS, US), F32),
            jax.ShapeDtypeStruct((32, 2, US // TRANS), F32),
            jax.ShapeDtypeStruct((ROT * US // 2, LANES), BF16),
            jax.ShapeDtypeStruct((US, LANES), F32),
        ),
        in_specs=[smem] + [vmem] * 11,
        out_specs=(vmem,) * 4,
        scratch_shapes=[
            pltpu.VMEM((ROT * US // 2, LANES), BF16),
            pltpu.VMEM((2 * ROWS, LANES), BF16),
            pltpu.VMEM((ROWS, LANES), F32),
        ],
        compiler_params=pltpu.CompilerParams(vmem_limit_bytes=VMEM_LIMIT),
        name="score",
    )(own, *imgs, w_near, *refs, ctf4, noise4, table)


def insert_kernel(
    own_ref, exp_ref, pair_ref, all_ref, near_ref, far_ref, sq_ref,
    own_out, s1, s2, s3, like_out, post, acc,
):
    own = own_ref[0]
    peaks = jnp.concatenate([all_ref[j, 0:1, :] for j in range(32)], axis=0)
    totals = jnp.concatenate([all_ref[j, 1:2, :] for j in range(32)], axis=0)
    peak = jnp.max(peaks, axis=0, keepdims=True)
    total = jnp.sum(totals * jnp.exp(peaks - peak), axis=0, keepdims=True)
    scale = jnp.exp(pair_ref[0, 0:1, :] - peak) / total
    like = peak + jnp.log(total)
    scale, like = (
        swapped(jnp.broadcast_to(jnp.concatenate([v] * TRANS, axis=1), (8, US)), own)[:1]
        for v in (scale, like)
    )
    like_out[...] = like[:, :MINE]
    piece = [scale[:, d * MINE : (d + 1) * MINE] for d in range(BLOCKS)]
    scale = jnp.concatenate([piece[0], piece[2]] * TRANS + [piece[1], piece[3]] * TRANS, axis=1)
    scale = jnp.broadcast_to(scale, (KS, US))
    count = jnp.zeros((KS, US), F32)
    for r in range(ROT):
        value = (exp_ref[r * KS : (r + 1) * KS, :] * scale).astype(BF16)
        count = count + value.astype(F32)
        for side in range(2):
            m = (side - r) % ROT
            for again in (m, m + ROT):
                post[again * KS : (again + 1) * KS, side * HALF : (side + 1) * HALF] = value

    half = US // 2
    acc[...] = sum(
        jnp.dot(
            post[(ROT - 2 * h) * KS : (2 * ROT - 2 * h) * KS, :],
            jnp.concatenate(
                [
                    v[b * half : (b + 1) * half, :]
                    for b in (2 * h, 2 * h + 1)
                    for v in (near_ref, far_ref)
                ],
                axis=0,
            ),
            preferred_element_type=F32,
        )
        for h in range(ROT // 2)
    )
    sums = jnp.dot(count, sq_ref[...], precision=HIGHEST, preferred_element_type=F32)
    for b in range(ROT):
        block = acc[b * KS : (b + 1) * KS, :]
        own_out[b] = block[:OWN]
        for d, out in ((1, s1), (2, s2), (3, s3)):
            out[b] = block[d * OWN : (d + 1) * OWN].astype(BF16)
    own_out[ROT] = sums[:OWN]
    own_out[ROT + 1] = jnp.zeros((OWN, LANES), F32)
    for d, out in ((1, s1), (2, s2), (3, s3)):
        part = sums[d * OWN : (d + 1) * OWN]
        high = part.astype(BF16)
        out[ROT] = high
        out[ROT + 1] = (part - high.astype(F32)).astype(BF16)


def insert(own, exps, stats, gathered, near, far, sq):
    vmem = pl.BlockSpec(memory_space=pltpu.VMEM)
    smem = pl.BlockSpec(memory_space=pltpu.SMEM)
    piece = (ROT + 2, OWN, LANES)
    return pl.pallas_call(
        insert_kernel,
        out_shape=(
            jax.ShapeDtypeStruct(piece, F32),
            jax.ShapeDtypeStruct(piece, BF16),
            jax.ShapeDtypeStruct(piece, BF16),
            jax.ShapeDtypeStruct(piece, BF16),
            jax.ShapeDtypeStruct((1, MINE), F32),
        ),
        in_specs=[smem] + [vmem] * 6,
        out_specs=(vmem,) * 5,
        scratch_shapes=[
            pltpu.VMEM((2 * ROWS, LANES), BF16),
            pltpu.VMEM((ROWS, LANES), F32),
        ],
        compiler_params=pltpu.CompilerParams(vmem_limit_bytes=VMEM_LIMIT),
        name="insert",
    )(own, exps, stats, gathered, near, far, sq)


def finish_kernel(own_ref, g1, g2, g3, tau_ref, out_ref, weight_out, fresh, turned, lines):
    parts = [own_ref, g1, g2, g3]
    sums = sum(p[ROT].astype(F32) + p[ROT + 1].astype(F32) for p in parts)
    denom = sums[:, :HALF] + 1.0 / tau_ref[...]
    denom = jnp.concatenate([denom, denom], axis=1)
    weight_out[...] = as_row(sums[:, HALF : HALF + 1], OWN) / (MINE * 16)
    for b in range(ROT):
        total = own_ref[b] + g1[b].astype(F32) + g2[b].astype(F32) + g3[b].astype(F32)
        total = total / denom
        fresh[0, pl.ds(b * 8, OWN), :] = total[:, :HALF]
        fresh[1, pl.ds(b * 8, OWN), :] = total[:, HALF:]
    for k in range(OWN):
        one = [fresh.at[p][pl.ds(k, ROT, stride=8), :] for p in range(2)]
        for c in range(STEP):
            pair = [one[p][:, c * CYCLES : (c + 1) * CYCLES] for p in range(2)]
            turned[pl.ds(c, ROT, stride=STEP), :] = jnp.concatenate(pair + pair, axis=1)
        first = turned[0:128, :].T
        second = turned[128:256, :].T
        lines[0, pl.ds(k * PAIRS, PAIRS), :] = first[:PAIRS]
        lines[1, pl.ds(k * PAIRS, PAIRS), :] = second[:PAIRS]
    for j in range(PAIRS):
        line = [lines.at[n][pl.ds(j, OWN, stride=PAIRS), :] for n in range(2)]
        out_ref[:, j * ANG : (j + 1) * ANG] = jnp.concatenate(line, axis=1)[:, :ANG]


def finish(own, got, tau):
    vmem = pl.BlockSpec(memory_space=pltpu.VMEM)
    return pl.pallas_call(
        finish_kernel,
        out_shape=(
            jax.ShapeDtypeStruct((OWN, 2 * CYCLES * ANG), F32),
            jax.ShapeDtypeStruct((1, OWN), F32),
        ),
        in_specs=[vmem] * 5,
        out_specs=(vmem, vmem),
        scratch_shapes=[
            pltpu.VMEM((2, ROT * 8, HALF), F32),
            pltpu.VMEM((256, 128), F32),
            pltpu.VMEM((2, OWN * PAIRS, HALF), F32),
        ],
        compiler_params=pltpu.CompilerParams(vmem_limit_bytes=VMEM_LIMIT),
        name="finish",
    )(own, *got, tau)


def along_y(value, distance):
    return lax.ppermute(
        value, "img", [(i, ((i // 4 + distance) % 4) * 4 + i % 4) for i in range(16)]
    )


def beside(value, img_flip, cls_flip):
    pairs = [
        (i * 8 + c, (i ^ img_flip) * 8 + (c ^ cls_flip)) for i in range(16) for c in range(8)
    ]
    return lax.ppermute(value, ("img", "cls"), pairs)


def per_device(
    table, images, references, class_logprior, ctf_table, noise_power, tau_power, defocus, offsets
):
    own = (lax.axis_index("img") % BLOCKS).astype(jnp.int32).reshape(1)
    img, ref, ctf4, noise4, tau4, table = arrange(
        images,
        references,
        class_logprior.reshape(1, OWN),
        offsets.transpose(1, 2, 0),
        defocus.reshape(1, MINE),
        ctf_table,
        noise_power.reshape(1, CYCLES),
        tau_power.reshape(1, CYCLES),
        table,
    )
    next_chip = beside(img, 2, 1)
    refs = (ref, along_y(ref, 3), along_y(ref, 2), along_y(ref, 1))
    other_core = beside(jnp.stack([img, next_chip]), 1, 0)
    w_near, near = shift(img, next_chip, ctf4, noise4, table)
    exps, stats, far, sq = score(
        own, (img, next_chip, other_core), w_near, refs, ctf4, noise4, table
    )
    same_images = [[(y * 4 + r) * 8 + c for r in range(4) for c in range(8)] for y in range(4)]
    gathered = lax.all_to_all(
        stats, ("img", "cls"), 0, 0, tiled=True, axis_index_groups=same_images
    )
    numer, s1, s2, s3, like = insert(own, exps, stats, gathered, near, far, sq)
    got = (along_y(s1, 1), along_y(s2, 2), along_y(s3, 3))
    fresh, weight = finish(numer, got, tau4)
    return fresh, weight.reshape(OWN), like.reshape(MINE)


def solution(mesh):
    body = functools.partial(per_device, jnp.asarray(phase_parts()))
    return jax.shard_map(
        body,
        mesh=mesh,
        in_specs=(
            P("img", None),
            P(("img", "cls"), None),
            P(("img", "cls")),
            P(),
            P(),
            P(),
            P("img"),
            P("img", None, None),
        ),
        out_specs=(P(("img", "cls"), None), P(("img", "cls")), P("img")),
        check_vma=False,
    )
```

```python
import functools
import math

import jax
import jax.numpy as jnp
import ml_dtypes
import numpy as np
from jax import lax
from jax.experimental import pallas as pl
from jax.experimental.pallas import tpu as pltpu
from jax.sharding import PartitionSpec as P

TRANS = 4
CYCLES = 32
ANG = 144
ROT = 36
NDEF = 16
STEP = ANG // ROT
PAIRS = 2 * CYCLES
LANES = 2 * STEP * CYCLES
HALF = LANES // 2
OWN = 4
MINE = 8
BLOCKS = 4
KS = OWN * BLOCKS
US = MINE * BLOCKS * TRANS
ROWS = ROT * KS
REACH = 3
MIDDLE = 24
SLOTS = 32
WINDOW = 20_000_000_000
offset_sigma = 2.0
F32 = jnp.float32
BF16 = jnp.bfloat16
HIGHEST = lax.Precision.HIGHEST
VMEM_LIMIT = 20 * 1024 * 1024


def phase_parts():
    span = 2 * REACH + 1
    theta = 2.0 * math.pi * np.arange(ANG).reshape(ROT, STEP) / ANG
    radius = np.arange(CYCLES) + 1.0
    fx = (np.cos(theta)[:, :, None] * radius).reshape(ROT, HALF)
    fy = (np.sin(theta)[:, :, None] * radius).reshape(ROT, HALF)
    shift = np.arange(span) - REACH
    phi = (
        -2.0
        * math.pi
        * (shift[:, None, None, None] * fx + shift[None, :, None, None] * fy)
        / (2.0 * CYCLES)
    ).reshape(span * span, ROT, HALF)[MIDDLE:]
    table = np.concatenate([np.cos(phi), np.sin(phi)], axis=2).transpose(1, 0, 2)
    table = np.pad(table, ((0, 0), (0, SLOTS - table.shape[1]), (0, 0)))
    parts = []
    rest = table
    for _ in range(3):
        part = rest.astype(np.float32).astype(ml_dtypes.bfloat16)
        parts.append(part)
        rest = rest - part.astype(np.float64)
    return np.concatenate(parts, axis=1)


def nt(a, b, **kw):
    return lax.dot_general(a, b, (((1,), (1,)), ((), ())), preferred_element_type=F32, **kw)


def in_hbm(value):
    return pltpu.with_memory_space_constraint(value, pltpu.HBM)


def fetch(pairs, sems):
    copies = [
        pltpu.make_async_copy(src, dst, sems.at[n]) for n, (src, dst) in enumerate(pairs)
    ]
    for copy in copies:
        copy.start()
    return copies


def as_column(row, size):
    here = lax.broadcasted_iota(jnp.int32, (size, size), 0)
    there = lax.broadcasted_iota(jnp.int32, (size, size), 1)
    wide = jnp.broadcast_to(row, (size, size))
    return jnp.sum(jnp.where(here == there, wide, 0.0), axis=1, keepdims=True)


def as_row(column, size):
    here = lax.broadcasted_iota(jnp.int32, (size, size), 0)
    there = lax.broadcasted_iota(jnp.int32, (size, size), 1)
    wide = jnp.broadcast_to(column, (size, size))
    return jnp.sum(jnp.where(here == there, wide, 0.0), axis=0, keepdims=True)


def turn_major(source, count, cut, flat, out):
    angle = lax.broadcasted_iota(jnp.int32, (CYCLES, ANG), 1) % STEP
    pick_b = lax.broadcasted_iota(jnp.int32, (40, ANG), 0)
    pick_a = lax.broadcasted_iota(jnp.int32, (40, ANG), 1)
    pick = jnp.where(pick_a // STEP == pick_b, 1.0, 0.0).astype(BF16)
    for j in range(PAIRS):
        line = source[:, j * ANG : (j + 1) * ANG].astype(F32)
        cut[0, pl.ds(j * 8, count), :] = line[:, :HALF]
        cut[1, pl.ds(j * 8, count), : ANG - HALF] = line[:, HALF:]
    for i in range(count):
        one = jnp.concatenate(
            [cut.at[n][pl.ds(i, PAIRS, stride=8), :] for n in range(2)], axis=1
        )[:, :ANG]
        spread = jnp.concatenate(
            [
                jnp.where(angle == c, one[p * CYCLES : (p + 1) * CYCLES], 0.0)
                for p in range(2)
                for c in range(STEP)
            ],
            axis=0,
        ).astype(BF16)
        turned = nt(pick, spread)
        flat[0, pl.ds(i * 40, 40), :] = turned[:, :HALF]
        flat[1, pl.ds(i * 40, 40), :] = turned[:, HALF:]
    for b in range(ROT):
        for n in range(2):
            line = flat.at[n][pl.ds(b, count, stride=40), :]
            out[b, :, n * HALF : (n + 1) * HALF] = line.astype(BF16)


def arrange_kernel(
    img_hbm, ref_hbm, prior_hbm, off_hbm, def_hbm, ctf_hbm, noise_hbm, tau_hbm, table_hbm,
    img_out, ref_out, ctf_out, noise_out, tau_out, table_out,
    img_ref, ref_ref, prior_ref, off_ref, def_ref, ctf_ref, noise_ref, tau_ref,
    cut, cut2, flat, flat2, sems,
):
    copies = fetch(
        (
            (ref_hbm, ref_ref),
            (img_hbm, img_ref),
            (prior_hbm, prior_ref),
            (off_hbm, off_ref),
            (def_hbm, def_ref),
            (ctf_hbm, ctf_ref),
            (noise_hbm, noise_ref),
            (tau_hbm, tau_ref),
            (table_hbm, table_out),
        ),
        sems,
    )
    copies[0].wait()
    turn_major(ref_ref, OWN, cut, flat, ref_out)
    copies[1].wait()
    turn_major(img_ref, MINE, cut2, flat2, img_out)
    for copy in copies[2:]:
        copy.wait()
    lane = lax.broadcasted_iota(jnp.int32, (MINE, LANES), 1)
    extra = jnp.where(lane == 8, as_column(def_ref[...].astype(F32), MINE), 0.0)
    for t in range(TRANS):
        for d in range(2):
            column = as_column(off_ref[t, d : d + 1, :].astype(F32), MINE)
            extra = jnp.where(lane == 2 * t + d, column, extra)
    img_out[ROT] = extra.astype(BF16)
    column = as_column(prior_ref[...].astype(F32), OWN)
    ref_out[ROT] = jnp.broadcast_to(column, (OWN, LANES)).astype(BF16)
    for small, out in ((ctf_ref, ctf_out), (noise_ref, noise_out), (tau_ref, tau_out)):
        out[...] = jnp.concatenate([small[...]] * STEP, axis=1)


def arrange(images, references, prior, offsets, defocus, ctf_table, noise, tau, table):
    vmem = pl.BlockSpec(memory_space=pltpu.VMEM)
    hbm = pl.BlockSpec(memory_space=pltpu.HBM)
    wide = 2 * CYCLES * ANG
    return pl.pallas_call(
        arrange_kernel,
        out_shape=(
            jax.ShapeDtypeStruct((ROT + 1, MINE, LANES), BF16),
            jax.ShapeDtypeStruct((ROT + 1, OWN, LANES), BF16),
            jax.ShapeDtypeStruct((NDEF, HALF), F32),
            jax.ShapeDtypeStruct((1, HALF), F32),
            jax.ShapeDtypeStruct((1, HALF), F32),
            jax.ShapeDtypeStruct((ROT, 3 * SLOTS, LANES), BF16),
        ),
        in_specs=[hbm] * 9,
        out_specs=(vmem,) * 6,
        scratch_shapes=[
            pltpu.VMEM((MINE, wide), BF16),
            pltpu.VMEM((OWN, wide), BF16),
            pltpu.VMEM((1, OWN), BF16),
            pltpu.VMEM((TRANS, 2, MINE), jnp.int32),
            pltpu.VMEM((1, MINE), jnp.int32),
            pltpu.VMEM((NDEF, CYCLES), F32),
            pltpu.VMEM((1, CYCLES), F32),
            pltpu.VMEM((1, CYCLES), F32),
            pltpu.VMEM((2, PAIRS * 8, HALF), F32),
            pltpu.VMEM((2, PAIRS * 8, HALF), F32),
            pltpu.VMEM((2, MINE * 40, HALF), F32),
            pltpu.VMEM((2, MINE * 40, HALF), F32),
            pltpu.SemaphoreType.DMA((9,)),
        ],
        compiler_params=pltpu.CompilerParams(vmem_limit_bytes=VMEM_LIMIT),
        name="arrange",
    )(
        *(
            in_hbm(v)
            for v in (images, references, prior, offsets, defocus, ctf_table, noise, tau, table)
        )
    )


def four(value):
    return jnp.concatenate([value] * TRANS, axis=0)


def image_rows(near, far):
    extra = jnp.concatenate([near[ROT].astype(F32), far[ROT].astype(F32)], axis=0)
    dx = jnp.concatenate([extra[:, 2 * t : 2 * t + 1] for t in range(TRANS)], axis=0)
    dy = jnp.concatenate([extra[:, 2 * t + 1 : 2 * t + 2] for t in range(TRANS)], axis=0)
    return dx, dy, extra[:, 8:9]


def contrast_of(group, ctf_ref):
    known = lax.broadcasted_iota(jnp.int32, (group.shape[0], NDEF), 1).astype(F32)
    which = jnp.where(known == group, 1.0, 0.0)
    return jnp.dot(which, ctf_ref[...], precision=HIGHEST, preferred_element_type=F32)


def shift_half(near, far, dx, dy, contrast, noise, table, weighted, inserted):
    pair = dx * (2 * REACH + 1) + dy
    slot = lax.broadcasted_iota(jnp.int32, (US // 2, 3 * SLOTS), 1) % SLOTS
    hot = jnp.where(slot.astype(F32) == jnp.abs(pair), 1.0, 0.0).astype(BF16)
    sign = jnp.broadcast_to(jnp.where(pair < 0, -1.0, 1.0), (US // 2, HALF))
    contrast4 = four(contrast)
    whiten4 = four(contrast / noise)
    for b in range(ROT):
        turn = jnp.dot(hot, table[b], preferred_element_type=F32)
        cosine, sine = turn[:, :HALF], turn[:, HALF:] * sign
        block = jnp.concatenate([near[b].astype(F32), far[b].astype(F32)], axis=0)
        real, imag = four(block[:, :HALF]), four(block[:, HALF:])
        shifted_real = real * cosine - imag * sine
        shifted_imag = real * sine + imag * cosine
        rows = slice(b * US // 2, (b + 1) * US // 2)
        weighted[rows, :HALF] = (shifted_real * whiten4).astype(BF16)
        weighted[rows, HALF:] = (shifted_imag * whiten4).astype(BF16)
        inserted[rows, :HALF] = (shifted_real * contrast4).astype(BF16)
        inserted[rows, HALF:] = (shifted_imag * contrast4).astype(BF16)


def shift_kernel(near, far, ctf_ref, noise_ref, table, weighted, inserted):
    dx, dy, group = image_rows(near, far)
    contrast = contrast_of(group, ctf_ref)
    shift_half(near, far, dx, dy, contrast, noise_ref[...], table, weighted, inserted)


def shift(near, far, ctf4, noise4, table):
    vmem = pl.BlockSpec(memory_space=pltpu.VMEM)
    half = jax.ShapeDtypeStruct((ROT * US // 2, LANES), BF16)
    return pl.pallas_call(
        shift_kernel,
        out_shape=(half, half),
        in_specs=[vmem] * 5,
        out_specs=(vmem, vmem),
        compiler_params=pltpu.CompilerParams(vmem_limit_bytes=VMEM_LIMIT),
        name="shift",
        cost_estimate=pl.CostEstimate(flops=WINDOW, bytes_accessed=1000, transcendentals=0),
    )(near, far, ctf4, noise4, table)


def swapped(row, own):
    lane = lax.broadcasted_iota(jnp.int32, row.shape, 1)
    for bit in range(2):
        size = MINE << bit
        other = jnp.where(
            (lane // size) % 2 == 0, pltpu.roll(row, US - size, 1), pltpu.roll(row, size, 1)
        )
        flip = jnp.broadcast_to((own >> bit) & 1, row.shape) == 1
        row = jnp.where(flip, other, row)
    return row


def over_shifts(row, combine):
    lane = lax.broadcasted_iota(jnp.int32, row.shape, 1)
    for size in (16, 32):
        turned = jnp.where(
            lane % 64 >= size, pltpu.roll(row, size, 1), pltpu.roll(row, size + 64, 1)
        )
        row = combine(row, turned)
    return row


def by_block(row):
    lane = lax.broadcasted_iota(jnp.int32, row.shape, 1) // MINE
    row = jnp.where(
        lane == 0,
        row,
        jnp.where(
            lane == 1,
            pltpu.roll(row, 72, 1),
            jnp.where(lane == 2, pltpu.roll(row, 8, 1), pltpu.roll(row, 80, 1)),
        ),
    )
    return row


def score_kernel(
    own_ref, i0, i2, i13, w_near, r0, r1, r2, r3, ctf_ref, noise_ref, table,
    exp_out, stat_out, ins_out, sq_out,
    w_far, back, acc,
):
    own = own_ref[0]
    square = jnp.zeros((KS, LANES), F32)
    for b in range(ROT):
        block = jnp.concatenate([r[b].astype(F32) for r in (r0, r1, r2, r3)], axis=0)
        square = square + block * block
        m = (ROT - b) % ROT
        back[pl.ds(m * KS, KS), :] = block.astype(BF16)
        back[pl.ds((m + ROT) * KS, KS), :] = block.astype(BF16)
    prior = jnp.concatenate([r[ROT].astype(F32) for r in (r0, r1, r2, r3)], axis=0)[:, :HALF]

    i1, i3 = i13.at[0], i13.at[1]
    dx0, dy0, group0 = image_rows(i0, i2)
    dx1, dy1, group1 = image_rows(i1, i3)
    noise = noise_ref[...]
    contrast = contrast_of(jnp.concatenate([group0, group1], axis=0), ctf_ref)
    far_contrast = contrast[2 * MINE :]
    squared = contrast * contrast
    squared = jnp.concatenate([four(squared[: 2 * MINE]), four(squared[2 * MINE :])], axis=0)
    sq_out[:, :HALF] = squared
    sq_out[:, HALF:] = jnp.ones((US, HALF), F32)
    coef = squared / (2.0 * noise)
    penalty = nt(square, jnp.concatenate([coef, coef], axis=1), precision=HIGHEST)
    dx = jnp.concatenate([dx0, dx1], axis=0)
    dy = jnp.concatenate([dy0, dy1], axis=0)
    near = -(dx * dx + dy * dy) / (2.0 * offset_sigma * offset_sigma)
    base = prior - penalty + as_row(near, US)

    shift_half(i1, i3, dx1, dy1, far_contrast, noise, table, w_far, ins_out)
    half = US // 2
    acc[...] = sum(
        nt(
            back[(ROT - 2 * h) * KS : (2 * ROT - 2 * h) * KS, :],
            jnp.concatenate(
                [
                    w[b * half : (b + 1) * half, :]
                    for b in (2 * h, 2 * h + 1)
                    for w in (w_near, w_far)
                ],
                axis=0,
            ),
        )
        for h in range(ROT // 2)
    )

    peak = jnp.full((KS, US), -jnp.inf, F32)
    for r in range(ROT):
        last = (r - 1) % ROT
        logp = acc[r * KS : (r + 1) * KS, :HALF] + acc[last * KS : (last + 1) * KS, HALF:] + base
        exp_out[r * KS : (r + 1) * KS, :] = logp
        peak = jnp.maximum(peak, logp)
    peak = jnp.broadcast_to(jnp.max(peak, axis=0, keepdims=True), (8, US))
    peak = over_shifts(peak, jnp.maximum)
    wide = jnp.broadcast_to(peak[:1], (KS, US))
    total = jnp.zeros((KS, US), F32)
    for r in range(ROT):
        value = jnp.exp(exp_out[r * KS : (r + 1) * KS, :] - wide)
        exp_out[r * KS : (r + 1) * KS, :] = value
        total = total + value
    total = jnp.broadcast_to(jnp.sum(total, axis=0, keepdims=True), (8, US))
    total = over_shifts(total, jnp.add)
    pair = [swapped(by_block(v), own)[:1, : US // TRANS] for v in (peak, total)]
    pair = jnp.concatenate(pair, axis=0)
    for j in range(32):
        stat_out[j] = pair


def score(own, imgs, w_near, refs, ctf4, noise4, table):
    vmem = pl.BlockSpec(memory_space=pltpu.VMEM)
    smem = pl.BlockSpec(memory_space=pltpu.SMEM)
    return pl.pallas_call(
        score_kernel,
        out_shape=(
            jax.ShapeDtypeStruct((ROWS, US), F32),
            jax.ShapeDtypeStruct((32, 2, US // TRANS), F32),
            jax.ShapeDtypeStruct((ROT * US // 2, LANES), BF16),
            jax.ShapeDtypeStruct((US, LANES), F32),
        ),
        in_specs=[smem] + [vmem] * 11,
        out_specs=(vmem,) * 4,
        scratch_shapes=[
            pltpu.VMEM((ROT * US // 2, LANES), BF16),
            pltpu.VMEM((2 * ROWS, LANES), BF16),
            pltpu.VMEM((ROWS, LANES), F32),
        ],
        compiler_params=pltpu.CompilerParams(vmem_limit_bytes=VMEM_LIMIT),
        name="score",
    )(own, *imgs, w_near, *refs, ctf4, noise4, table)


def insert_kernel(
    own_ref, exp_ref, pair_ref, all_ref, near_ref, far_ref, sq_ref,
    own_out, s1, s2, s3, like_out, post, acc,
):
    own = own_ref[0]
    peaks = jnp.concatenate([all_ref[j, 0:1, :] for j in range(32)], axis=0)
    totals = jnp.concatenate([all_ref[j, 1:2, :] for j in range(32)], axis=0)
    peak = jnp.max(peaks, axis=0, keepdims=True)
    total = jnp.sum(totals * jnp.exp(peaks - peak), axis=0, keepdims=True)
    scale = jnp.exp(pair_ref[0, 0:1, :] - peak) / total
    like = peak + jnp.log(total)
    scale, like = (
        swapped(jnp.broadcast_to(jnp.concatenate([v] * TRANS, axis=1), (8, US)), own)[:1]
        for v in (scale, like)
    )
    like_out[...] = jnp.broadcast_to(like, (8, US))
    piece = [scale[:, d * MINE : (d + 1) * MINE] for d in range(BLOCKS)]
    scale = jnp.concatenate([piece[0], piece[2]] * TRANS + [piece[1], piece[3]] * TRANS, axis=1)
    scale = jnp.broadcast_to(scale, (KS, US))
    count = jnp.zeros((KS, US), F32)
    for r in range(ROT):
        value = (exp_ref[r * KS : (r + 1) * KS, :] * scale).astype(BF16)
        count = count + value.astype(F32)
        for side in range(2):
            m = (side - r) % ROT
            for again in (m, m + ROT):
                post[again * KS : (again + 1) * KS, side * HALF : (side + 1) * HALF] = value

    half = US // 2
    acc[...] = sum(
        jnp.dot(
            post[(ROT - 2 * h) * KS : (2 * ROT - 2 * h) * KS, :],
            jnp.concatenate(
                [
                    v[b * half : (b + 1) * half, :]
                    for b in (2 * h, 2 * h + 1)
                    for v in (near_ref, far_ref)
                ],
                axis=0,
            ),
            preferred_element_type=F32,
        )
        for h in range(ROT // 2)
    )
    sums = jnp.dot(count, sq_ref[...], precision=HIGHEST, preferred_element_type=F32)
    for b in range(ROT):
        block = acc[b * KS : (b + 1) * KS, :]
        own_out[b] = block[:OWN]
        for d, out in ((1, s1), (2, s2), (3, s3)):
            out[b] = block[d * OWN : (d + 1) * OWN].astype(BF16)
    own_out[ROT] = sums[:OWN]
    own_out[ROT + 1] = jnp.zeros((OWN, LANES), F32)
    for d, out in ((1, s1), (2, s2), (3, s3)):
        part = sums[d * OWN : (d + 1) * OWN]
        high = part.astype(BF16)
        out[ROT] = high
        out[ROT + 1] = (part - high.astype(F32)).astype(BF16)


def insert(own, exps, stats, gathered, near, far, sq):
    vmem = pl.BlockSpec(memory_space=pltpu.VMEM)
    smem = pl.BlockSpec(memory_space=pltpu.SMEM)
    piece = (ROT + 2, OWN, LANES)
    return pl.pallas_call(
        insert_kernel,
        out_shape=(
            jax.ShapeDtypeStruct(piece, F32),
            jax.ShapeDtypeStruct(piece, BF16),
            jax.ShapeDtypeStruct(piece, BF16),
            jax.ShapeDtypeStruct(piece, BF16),
            jax.ShapeDtypeStruct((8, US), F32),
        ),
        in_specs=[smem] + [vmem] * 6,
        out_specs=(vmem,) * 5,
        scratch_shapes=[
            pltpu.VMEM((2 * ROWS, LANES), BF16),
            pltpu.VMEM((ROWS, LANES), F32),
        ],
        compiler_params=pltpu.CompilerParams(vmem_limit_bytes=VMEM_LIMIT),
        name="insert",
    )(own, exps, stats, gathered, near, far, sq)


def finish_kernel(own_ref, g1, g2, g3, tau_ref, like_ref, out_ref, weight_out, like_out, fresh, turned, lines):
    like_out[...] = like_ref[:1, :MINE]
    parts = [own_ref, g1, g2, g3]
    sums = sum(p[ROT].astype(F32) + p[ROT + 1].astype(F32) for p in parts)
    denom = sums[:, :HALF] + 1.0 / tau_ref[...]
    denom = jnp.concatenate([denom, denom], axis=1)
    weight_out[...] = as_row(sums[:, HALF : HALF + 1], OWN) / (MINE * 16)
    for b in range(ROT):
        total = own_ref[b] + g1[b].astype(F32) + g2[b].astype(F32) + g3[b].astype(F32)
        total = total / denom
        fresh[0, pl.ds(b * 8, OWN), :] = total[:, :HALF]
        fresh[1, pl.ds(b * 8, OWN), :] = total[:, HALF:]
    for k in range(OWN):
        one = [fresh.at[p][pl.ds(k, ROT, stride=8), :] for p in range(2)]
        for c in range(STEP):
            pair = [one[p][:, c * CYCLES : (c + 1) * CYCLES] for p in range(2)]
            turned[pl.ds(c, ROT, stride=STEP), :] = jnp.concatenate(pair + pair, axis=1)
        first = turned[0:128, :].T
        second = turned[128:256, :].T
        lines[0, pl.ds(k * PAIRS, PAIRS), :] = first[:PAIRS]
        lines[1, pl.ds(k * PAIRS, PAIRS), :] = second[:PAIRS]
    for j in range(PAIRS):
        line = [lines.at[n][pl.ds(j, OWN, stride=PAIRS), :] for n in range(2)]
        out_ref[:, j * ANG : (j + 1) * ANG] = jnp.concatenate(line, axis=1)[:, :ANG]


def finish(own, got, tau, like):
    vmem = pl.BlockSpec(memory_space=pltpu.VMEM)
    return pl.pallas_call(
        finish_kernel,
        out_shape=(
            jax.ShapeDtypeStruct((OWN, 2 * CYCLES * ANG), F32),
            jax.ShapeDtypeStruct((1, OWN), F32),
            jax.ShapeDtypeStruct((1, MINE), F32),
        ),
        in_specs=[vmem] * 6,
        out_specs=(vmem,) * 3,
        scratch_shapes=[
            pltpu.VMEM((2, ROT * 8, HALF), F32),
            pltpu.VMEM((256, 128), F32),
            pltpu.VMEM((2, OWN * PAIRS, HALF), F32),
        ],
        compiler_params=pltpu.CompilerParams(vmem_limit_bytes=VMEM_LIMIT),
        name="finish",
    )(own, *got, tau, like)


def along_y(value, distance):
    return lax.ppermute(
        value, "img", [(i, ((i // 4 + distance) % 4) * 4 + i % 4) for i in range(16)]
    )


def beside(value, img_flip, cls_flip):
    pairs = [
        (i * 8 + c, (i ^ img_flip) * 8 + (c ^ cls_flip)) for i in range(16) for c in range(8)
    ]
    return lax.ppermute(value, ("img", "cls"), pairs)


def per_device(
    table, images, references, class_logprior, ctf_table, noise_power, tau_power, defocus, offsets
):
    own = (lax.axis_index("img") % BLOCKS).astype(jnp.int32).reshape(1)
    img, ref, ctf4, noise4, tau4, table = arrange(
        images,
        references,
        class_logprior.reshape(1, OWN),
        offsets.transpose(1, 2, 0),
        defocus.reshape(1, MINE),
        ctf_table,
        noise_power.reshape(1, CYCLES),
        tau_power.reshape(1, CYCLES),
        table,
    )
    next_chip = beside(img, 2, 1)
    refs = (ref, along_y(ref, 3), along_y(ref, 2), along_y(ref, 1))
    other_core = beside(jnp.stack([img, next_chip]), 1, 0)
    w_near, near = shift(img, next_chip, ctf4, noise4, table)
    exps, stats, far, sq = score(
        own, (img, next_chip, other_core), w_near, refs, ctf4, noise4, table
    )
    same_images = [[(y * 4 + r) * 8 + c for r in range(4) for c in range(8)] for y in range(4)]
    gathered = lax.all_to_all(
        stats, ("img", "cls"), 0, 0, tiled=True, axis_index_groups=same_images
    )
    numer, s1, s2, s3, like = insert(own, exps, stats, gathered, near, far, sq)
    got = (along_y(s1, 1), along_y(s2, 2), along_y(s3, 3))
    fresh, weight, like = finish(numer, got, tau4, like)
    return fresh, weight.reshape(OWN), like.reshape(MINE)


def solution(mesh):
    body = functools.partial(per_device, jnp.asarray(phase_parts()))
    return jax.shard_map(
        body,
        mesh=mesh,
        in_specs=(
            P("img", None),
            P(("img", "cls"), None),
            P(("img", "cls")),
            P(),
            P(),
            P(),
            P("img"),
            P("img", None, None),
        ),
        out_specs=(P(("img", "cls"), None), P(("img", "cls")), P("img")),
        check_vma=False,
    )
```

```python
import functools
import math

import jax
import jax.numpy as jnp
import ml_dtypes
import numpy as np
from jax import lax
from jax.experimental import pallas as pl
from jax.experimental.pallas import tpu as pltpu
from jax.sharding import PartitionSpec as P

TRANS = 4
CYCLES = 32
ANG = 144
ROT = 36
NDEF = 16
STEP = ANG // ROT
PAIRS = 2 * CYCLES
LANES = 2 * STEP * CYCLES
HALF = LANES // 2
OWN = 4
MINE = 8
BLOCKS = 4
KS = OWN * BLOCKS
US = MINE * BLOCKS * TRANS
ROWS = ROT * KS
REACH = 3
MIDDLE = 24
SLOTS = 32
WINDOW = 20_000_000_000
offset_sigma = 2.0
F32 = jnp.float32
BF16 = jnp.bfloat16
HIGHEST = lax.Precision.HIGHEST
VMEM_LIMIT = 20 * 1024 * 1024


def phase_parts():
    span = 2 * REACH + 1
    theta = 2.0 * math.pi * np.arange(ANG).reshape(ROT, STEP) / ANG
    radius = np.arange(CYCLES) + 1.0
    fx = (np.cos(theta)[:, :, None] * radius).reshape(ROT, HALF)
    fy = (np.sin(theta)[:, :, None] * radius).reshape(ROT, HALF)
    shift = np.arange(span) - REACH
    phi = (
        -2.0
        * math.pi
        * (shift[:, None, None, None] * fx + shift[None, :, None, None] * fy)
        / (2.0 * CYCLES)
    ).reshape(span * span, ROT, HALF)[MIDDLE:]
    table = np.concatenate([np.cos(phi), np.sin(phi)], axis=2).transpose(1, 0, 2)
    table = np.pad(table, ((0, 0), (0, SLOTS - table.shape[1]), (0, 0)))
    parts = []
    rest = table
    for _ in range(3):
        part = rest.astype(np.float32).astype(ml_dtypes.bfloat16)
        parts.append(part)
        rest = rest - part.astype(np.float64)
    return np.concatenate(parts, axis=1)


def nt(a, b, **kw):
    return lax.dot_general(a, b, (((1,), (1,)), ((), ())), preferred_element_type=F32, **kw)


def in_hbm(value):
    return pltpu.with_memory_space_constraint(value, pltpu.HBM)


def fetch(pairs, sems):
    copies = [
        pltpu.make_async_copy(src, dst, sems.at[n]) for n, (src, dst) in enumerate(pairs)
    ]
    for copy in copies:
        copy.start()
    return copies


def as_column(row, size):
    here = lax.broadcasted_iota(jnp.int32, (size, size), 0)
    there = lax.broadcasted_iota(jnp.int32, (size, size), 1)
    wide = jnp.broadcast_to(row, (size, size))
    return jnp.sum(jnp.where(here == there, wide, 0.0), axis=1, keepdims=True)


def as_row(column, size):
    here = lax.broadcasted_iota(jnp.int32, (size, size), 0)
    there = lax.broadcasted_iota(jnp.int32, (size, size), 1)
    wide = jnp.broadcast_to(column, (size, size))
    return jnp.sum(jnp.where(here == there, wide, 0.0), axis=0, keepdims=True)


def turn_major(source, count, cut, flat, out):
    angle = lax.broadcasted_iota(jnp.int32, (CYCLES, ANG), 1) % STEP
    pick_b = lax.broadcasted_iota(jnp.int32, (40, ANG), 0)
    pick_a = lax.broadcasted_iota(jnp.int32, (40, ANG), 1)
    pick = jnp.where(pick_a // STEP == pick_b, 1.0, 0.0).astype(BF16)
    for j in range(PAIRS):
        line = source[:, j * ANG : (j + 1) * ANG].astype(F32)
        cut[0, pl.ds(j * 8, count), :] = line[:, :HALF]
        cut[1, pl.ds(j * 8, count), : ANG - HALF] = line[:, HALF:]
    for i in range(count):
        one = jnp.concatenate(
            [cut.at[n][pl.ds(i, PAIRS, stride=8), :] for n in range(2)], axis=1
        )[:, :ANG]
        spread = jnp.concatenate(
            [
                jnp.where(angle == c, one[p * CYCLES : (p + 1) * CYCLES], 0.0)
                for p in range(2)
                for c in range(STEP)
            ],
            axis=0,
        ).astype(BF16)
        turned = nt(pick, spread)
        flat[0, pl.ds(i * 40, 40), :] = turned[:, :HALF]
        flat[1, pl.ds(i * 40, 40), :] = turned[:, HALF:]
    for b in range(ROT):
        for n in range(2):
            line = flat.at[n][pl.ds(b, count, stride=40), :]
            out[b, :, n * HALF : (n + 1) * HALF] = line.astype(BF16)


def arrange_kernel(
    img_hbm, ref_hbm, prior_hbm, off_hbm, def_hbm, ctf_hbm, noise_hbm, tau_hbm, table_hbm,
    img_out, ref_out, ctf_out, noise_out, tau_out, table_out,
    img_ref, ref_ref, prior_ref, off_ref, def_ref, ctf_ref, noise_ref, tau_ref,
    cut, cut2, flat, flat2, sems,
):
    copies = fetch(
        (
            (ref_hbm, ref_ref),
            (img_hbm, img_ref),
            (prior_hbm, prior_ref),
            (off_hbm, off_ref),
            (def_hbm, def_ref),
            (ctf_hbm, ctf_ref),
            (noise_hbm, noise_ref),
            (tau_hbm, tau_ref),
            (table_hbm, table_out),
        ),
        sems,
    )
    copies[0].wait()
    turn_major(ref_ref, OWN, cut, flat, ref_out)
    copies[1].wait()
    turn_major(img_ref, MINE, cut2, flat2, img_out)
    for copy in copies[2:]:
        copy.wait()
    lane = lax.broadcasted_iota(jnp.int32, (MINE, LANES), 1)
    extra = jnp.where(lane == 8, as_column(def_ref[...].astype(F32), MINE), 0.0)
    for t in range(TRANS):
        for d in range(2):
            column = as_column(off_ref[t, d : d + 1, :].astype(F32), MINE)
            extra = jnp.where(lane == 2 * t + d, column, extra)
    img_out[ROT] = extra.astype(BF16)
    column = as_column(prior_ref[...].astype(F32), OWN)
    ref_out[ROT] = jnp.broadcast_to(column, (OWN, LANES)).astype(BF16)
    for small, out in ((ctf_ref, ctf_out), (noise_ref, noise_out), (tau_ref, tau_out)):
        out[...] = jnp.concatenate([small[...]] * STEP, axis=1)


def arrange(images, references, prior, offsets, defocus, ctf_table, noise, tau, table):
    vmem = pl.BlockSpec(memory_space=pltpu.VMEM)
    hbm = pl.BlockSpec(memory_space=pltpu.HBM)
    wide = 2 * CYCLES * ANG
    return pl.pallas_call(
        arrange_kernel,
        out_shape=(
            jax.ShapeDtypeStruct((ROT + 1, MINE, LANES), BF16),
            jax.ShapeDtypeStruct((ROT + 1, OWN, LANES), BF16),
            jax.ShapeDtypeStruct((NDEF, HALF), F32),
            jax.ShapeDtypeStruct((1, HALF), F32),
            jax.ShapeDtypeStruct((1, HALF), F32),
            jax.ShapeDtypeStruct((ROT, 3 * SLOTS, LANES), BF16),
        ),
        in_specs=[hbm] * 9,
        out_specs=(vmem,) * 6,
        scratch_shapes=[
            pltpu.VMEM((MINE, wide), BF16),
            pltpu.VMEM((OWN, wide), BF16),
            pltpu.VMEM((1, OWN), BF16),
            pltpu.VMEM((TRANS, 2, MINE), jnp.int32),
            pltpu.VMEM((1, MINE), jnp.int32),
            pltpu.VMEM((NDEF, CYCLES), F32),
            pltpu.VMEM((1, CYCLES), F32),
            pltpu.VMEM((1, CYCLES), F32),
            pltpu.VMEM((2, PAIRS * 8, HALF), F32),
            pltpu.VMEM((2, PAIRS * 8, HALF), F32),
            pltpu.VMEM((2, MINE * 40, HALF), F32),
            pltpu.VMEM((2, MINE * 40, HALF), F32),
            pltpu.SemaphoreType.DMA((9,)),
        ],
        compiler_params=pltpu.CompilerParams(vmem_limit_bytes=VMEM_LIMIT),
        name="arrange",
    )(
        *(
            in_hbm(v)
            for v in (images, references, prior, offsets, defocus, ctf_table, noise, tau, table)
        )
    )


def four(value):
    return jnp.concatenate([value] * TRANS, axis=0)


def image_rows(near, far):
    extra = jnp.concatenate([near[ROT].astype(F32), far[ROT].astype(F32)], axis=0)
    dx = jnp.concatenate([extra[:, 2 * t : 2 * t + 1] for t in range(TRANS)], axis=0)
    dy = jnp.concatenate([extra[:, 2 * t + 1 : 2 * t + 2] for t in range(TRANS)], axis=0)
    return dx, dy, extra[:, 8:9]


def contrast_of(group, ctf_ref):
    known = lax.broadcasted_iota(jnp.int32, (group.shape[0], NDEF), 1).astype(F32)
    which = jnp.where(known == group, 1.0, 0.0)
    return jnp.dot(which, ctf_ref[...], precision=HIGHEST, preferred_element_type=F32)


def shift_half(near, far, dx, dy, contrast, noise, table, weighted, inserted):
    pair = dx * (2 * REACH + 1) + dy
    slot = lax.broadcasted_iota(jnp.int32, (US // 2, 3 * SLOTS), 1) % SLOTS
    hot = jnp.where(slot.astype(F32) == jnp.abs(pair), 1.0, 0.0).astype(BF16)
    sign = jnp.broadcast_to(jnp.where(pair < 0, -1.0, 1.0), (US // 2, HALF))
    contrast4 = four(contrast)
    whiten4 = four(contrast / noise)
    for b in range(ROT):
        turn = jnp.dot(hot, table[b], preferred_element_type=F32)
        cosine, sine = turn[:, :HALF], turn[:, HALF:] * sign
        block = jnp.concatenate([near[b].astype(F32), far[b].astype(F32)], axis=0)
        real, imag = four(block[:, :HALF]), four(block[:, HALF:])
        shifted_real = real * cosine - imag * sine
        shifted_imag = real * sine + imag * cosine
        rows = slice(b * US // 2, (b + 1) * US // 2)
        weighted[rows, :HALF] = (shifted_real * whiten4).astype(BF16)
        weighted[rows, HALF:] = (shifted_imag * whiten4).astype(BF16)
        inserted[rows, :HALF] = (shifted_real * contrast4).astype(BF16)
        inserted[rows, HALF:] = (shifted_imag * contrast4).astype(BF16)


def shift_kernel(near, far, ctf_ref, noise_ref, table, weighted, inserted):
    dx, dy, group = image_rows(near, far)
    contrast = contrast_of(group, ctf_ref)
    shift_half(near, far, dx, dy, contrast, noise_ref[...], table, weighted, inserted)


def shift(near, far, ctf4, noise4, table):
    vmem = pl.BlockSpec(memory_space=pltpu.VMEM)
    half = jax.ShapeDtypeStruct((ROT * US // 2, LANES), BF16)
    return pl.pallas_call(
        shift_kernel,
        out_shape=(half, half),
        in_specs=[vmem] * 5,
        out_specs=(vmem, vmem),
        compiler_params=pltpu.CompilerParams(vmem_limit_bytes=VMEM_LIMIT),
        name="shift",
        cost_estimate=pl.CostEstimate(flops=WINDOW, bytes_accessed=1000, transcendentals=0),
    )(near, far, ctf4, noise4, table)


def swapped(row, own):
    lane = lax.broadcasted_iota(jnp.int32, row.shape, 1)
    chosen = lambda bit: jnp.broadcast_to((own >> bit) & 1, row.shape) == 1
    row = jnp.where(chosen(0), pltpu.roll(row, US // 2, 1), row)
    other = jnp.where(
        (lane // MINE) % 2 == 0, pltpu.roll(row, US - MINE, 1), pltpu.roll(row, MINE, 1)
    )
    return jnp.where(chosen(1), other, row)


def over_shifts(row, combine):
    lane = lax.broadcasted_iota(jnp.int32, row.shape, 1)
    for size in (16, 32):
        turned = jnp.where(
            lane % 64 >= size, pltpu.roll(row, size, 1), pltpu.roll(row, size + 64, 1)
        )
        row = combine(row, turned)
    return row


def score_kernel(
    own_ref, i0, i2, i13, w_near, r0, r1, r2, r3, ctf_ref, noise_ref, table,
    exp_out, stat_out, ins_out, sq_out,
    w_far, back, acc,
):
    own = own_ref[0]
    square = jnp.zeros((KS, LANES), F32)
    for b in range(ROT):
        block = jnp.concatenate([r[b].astype(F32) for r in (r0, r1, r2, r3)], axis=0)
        square = square + block * block
        m = (ROT - b) % ROT
        back[pl.ds(m * KS, KS), :] = block.astype(BF16)
        back[pl.ds((m + ROT) * KS, KS), :] = block.astype(BF16)
    prior = jnp.concatenate([r[ROT].astype(F32) for r in (r0, r1, r2, r3)], axis=0)[:, :HALF]

    i1, i3 = i13.at[0], i13.at[1]
    dx0, dy0, group0 = image_rows(i0, i2)
    dx1, dy1, group1 = image_rows(i1, i3)
    noise = noise_ref[...]
    contrast = contrast_of(jnp.concatenate([group0, group1], axis=0), ctf_ref)
    far_contrast = contrast[2 * MINE :]
    squared = contrast * contrast
    squared = jnp.concatenate([four(squared[: 2 * MINE]), four(squared[2 * MINE :])], axis=0)
    sq_out[:, :HALF] = squared
    sq_out[:, HALF:] = jnp.ones((US, HALF), F32)
    coef = squared / (2.0 * noise)
    penalty = nt(square, jnp.concatenate([coef, coef], axis=1), precision=HIGHEST)
    dx = jnp.concatenate([dx0, dx1], axis=0)
    dy = jnp.concatenate([dy0, dy1], axis=0)
    near = -(dx * dx + dy * dy) / (2.0 * offset_sigma * offset_sigma)
    base = prior - penalty + as_row(near, US)

    shift_half(i1, i3, dx1, dy1, far_contrast, noise, table, w_far, ins_out)
    half = US // 2
    acc[...] = sum(
        nt(
            back[(ROT - 2 * h) * KS : (2 * ROT - 2 * h) * KS, :],
            jnp.concatenate(
                [
                    w[b * half : (b + 1) * half, :]
                    for b in (2 * h, 2 * h + 1)
                    for w in (w_near, w_far)
                ],
                axis=0,
            ),
        )
        for h in range(ROT // 2)
    )

    peak = jnp.full((KS, US), -jnp.inf, F32)
    for r in range(ROT):
        last = (r - 1) % ROT
        logp = acc[r * KS : (r + 1) * KS, :HALF] + acc[last * KS : (last + 1) * KS, HALF:] + base
        exp_out[r * KS : (r + 1) * KS, :] = logp
        peak = jnp.maximum(peak, logp)
    peak = jnp.broadcast_to(jnp.max(peak, axis=0, keepdims=True), (8, US))
    wide = jnp.broadcast_to(peak[:1], (KS, US))
    total = jnp.zeros((KS, US), F32)
    for r in range(ROT):
        value = jnp.exp(exp_out[r * KS : (r + 1) * KS, :] - wide)
        exp_out[r * KS : (r + 1) * KS, :] = value
        total = total + value
    total = jnp.broadcast_to(jnp.sum(total, axis=0, keepdims=True), (8, US))
    row = lax.broadcasted_iota(jnp.int32, (8, US), 0)
    pair = swapped(jnp.where(row == 0, peak, total), own)[:2]
    for j in range(32):
        stat_out[j] = pair


def score(own, imgs, w_near, refs, ctf4, noise4, table):
    vmem = pl.BlockSpec(memory_space=pltpu.VMEM)
    smem = pl.BlockSpec(memory_space=pltpu.SMEM)
    return pl.pallas_call(
        score_kernel,
        out_shape=(
            jax.ShapeDtypeStruct((ROWS, US), F32),
            jax.ShapeDtypeStruct((32, 2, US), F32),
            jax.ShapeDtypeStruct((ROT * US // 2, LANES), BF16),
            jax.ShapeDtypeStruct((US, LANES), F32),
        ),
        in_specs=[smem] + [vmem] * 11,
        out_specs=(vmem,) * 4,
        scratch_shapes=[
            pltpu.VMEM((ROT * US // 2, LANES), BF16),
            pltpu.VMEM((2 * ROWS, LANES), BF16),
            pltpu.VMEM((ROWS, LANES), F32),
        ],
        compiler_params=pltpu.CompilerParams(vmem_limit_bytes=VMEM_LIMIT),
        name="score",
    )(own, *imgs, w_near, *refs, ctf4, noise4, table)


def insert_kernel(
    own_ref, exp_ref, pair_ref, all_ref, near_ref, far_ref, sq_ref,
    own_out, s1, s2, s3, like_out, post, acc,
):
    own = own_ref[0]
    peaks = jnp.concatenate([all_ref[j, 0:1, :] for j in range(32)], axis=0)
    totals = jnp.concatenate([all_ref[j, 1:2, :] for j in range(32)], axis=0)
    lane_peak = jnp.max(peaks, axis=0, keepdims=True)
    lane_total = jnp.sum(totals * jnp.exp(peaks - lane_peak), axis=0, keepdims=True)
    lane_peak = jnp.broadcast_to(lane_peak, (8, US))
    peak = over_shifts(lane_peak, jnp.maximum)
    total = over_shifts(lane_total * jnp.exp(lane_peak - peak), jnp.add)
    scale = jnp.exp(pair_ref[0, 0:1, :] - peak) / total
    like_out[...] = swapped(peak + jnp.log(total), own)
    scale = jnp.broadcast_to(swapped(scale, own)[:1], (KS, US))
    count = jnp.zeros((KS, US), F32)
    for r in range(ROT):
        value = (exp_ref[r * KS : (r + 1) * KS, :] * scale).astype(BF16)
        count = count + value.astype(F32)
        for side in range(2):
            m = (side - r) % ROT
            for again in (m, m + ROT):
                post[again * KS : (again + 1) * KS, side * HALF : (side + 1) * HALF] = value

    half = US // 2
    acc[...] = sum(
        jnp.dot(
            post[(ROT - 2 * h) * KS : (2 * ROT - 2 * h) * KS, :],
            jnp.concatenate(
                [
                    v[b * half : (b + 1) * half, :]
                    for b in (2 * h, 2 * h + 1)
                    for v in (near_ref, far_ref)
                ],
                axis=0,
            ),
            preferred_element_type=F32,
        )
        for h in range(ROT // 2)
    )
    sums = jnp.dot(count, sq_ref[...], precision=HIGHEST, preferred_element_type=F32)
    for b in range(ROT):
        block = acc[b * KS : (b + 1) * KS, :]
        own_out[b] = block[:OWN]
        for d, out in ((1, s1), (2, s2), (3, s3)):
            out[b] = block[d * OWN : (d + 1) * OWN].astype(BF16)
    own_out[ROT] = sums[:OWN]
    own_out[ROT + 1] = jnp.zeros((OWN, LANES), F32)
    for d, out in ((1, s1), (2, s2), (3, s3)):
        part = sums[d * OWN : (d + 1) * OWN]
        high = part.astype(BF16)
        out[ROT] = high
        out[ROT + 1] = (part - high.astype(F32)).astype(BF16)


def insert(own, exps, stats, gathered, near, far, sq):
    vmem = pl.BlockSpec(memory_space=pltpu.VMEM)
    smem = pl.BlockSpec(memory_space=pltpu.SMEM)
    piece = (ROT + 2, OWN, LANES)
    return pl.pallas_call(
        insert_kernel,
        out_shape=(
            jax.ShapeDtypeStruct(piece, F32),
            jax.ShapeDtypeStruct(piece, BF16),
            jax.ShapeDtypeStruct(piece, BF16),
            jax.ShapeDtypeStruct(piece, BF16),
            jax.ShapeDtypeStruct((8, US), F32),
        ),
        in_specs=[smem] + [vmem] * 6,
        out_specs=(vmem,) * 5,
        scratch_shapes=[
            pltpu.VMEM((2 * ROWS, LANES), BF16),
            pltpu.VMEM((ROWS, LANES), F32),
        ],
        compiler_params=pltpu.CompilerParams(vmem_limit_bytes=VMEM_LIMIT),
        name="insert",
    )(own, exps, stats, gathered, near, far, sq)


def finish_kernel(own_ref, g1, g2, g3, tau_ref, like_ref, out_ref, weight_out, like_out, fresh, turned, lines):
    like_out[...] = like_ref[:1, :MINE]
    parts = [own_ref, g1, g2, g3]
    sums = sum(p[ROT].astype(F32) + p[ROT + 1].astype(F32) for p in parts)
    denom = sums[:, :HALF] + 1.0 / tau_ref[...]
    denom = jnp.concatenate([denom, denom], axis=1)
    weight_out[...] = as_row(sums[:, HALF : HALF + 1], OWN) / (MINE * 16)
    for b in range(ROT):
        total = own_ref[b] + g1[b].astype(F32) + g2[b].astype(F32) + g3[b].astype(F32)
        total = total / denom
        fresh[0, pl.ds(b * 8, OWN), :] = total[:, :HALF]
        fresh[1, pl.ds(b * 8, OWN), :] = total[:, HALF:]
    for k in range(OWN):
        one = [fresh.at[p][pl.ds(k, ROT, stride=8), :] for p in range(2)]
        for c in range(STEP):
            pair = [one[p][:, c * CYCLES : (c + 1) * CYCLES] for p in range(2)]
            turned[pl.ds(c, ROT, stride=STEP), :] = jnp.concatenate(pair + pair, axis=1)
        first = turned[0:128, :].T
        second = turned[128:256, :].T
        lines[0, pl.ds(k * PAIRS, PAIRS), :] = first[:PAIRS]
        lines[1, pl.ds(k * PAIRS, PAIRS), :] = second[:PAIRS]
    for j in range(PAIRS):
        line = [lines.at[n][pl.ds(j, OWN, stride=PAIRS), :] for n in range(2)]
        out_ref[:, j * ANG : (j + 1) * ANG] = jnp.concatenate(line, axis=1)[:, :ANG]


def finish(own, got, tau, like):
    vmem = pl.BlockSpec(memory_space=pltpu.VMEM)
    return pl.pallas_call(
        finish_kernel,
        out_shape=(
            jax.ShapeDtypeStruct((OWN, 2 * CYCLES * ANG), F32),
            jax.ShapeDtypeStruct((1, OWN), F32),
            jax.ShapeDtypeStruct((1, MINE), F32),
        ),
        in_specs=[vmem] * 6,
        out_specs=(vmem,) * 3,
        scratch_shapes=[
            pltpu.VMEM((2, ROT * 8, HALF), F32),
            pltpu.VMEM((256, 128), F32),
            pltpu.VMEM((2, OWN * PAIRS, HALF), F32),
        ],
        compiler_params=pltpu.CompilerParams(vmem_limit_bytes=VMEM_LIMIT),
        name="finish",
    )(own, *got, tau, like)


def along_y(value, distance):
    return lax.ppermute(
        value, "img", [(i, ((i // 4 + distance) % 4) * 4 + i % 4) for i in range(16)]
    )


def beside(value, img_flip, cls_flip):
    pairs = [
        (i * 8 + c, (i ^ img_flip) * 8 + (c ^ cls_flip)) for i in range(16) for c in range(8)
    ]
    return lax.ppermute(value, ("img", "cls"), pairs)


def per_device(
    table, images, references, class_logprior, ctf_table, noise_power, tau_power, defocus, offsets
):
    own = (lax.axis_index("img") % BLOCKS).astype(jnp.int32).reshape(1)
    img, ref, ctf4, noise4, tau4, table = arrange(
        images,
        references,
        class_logprior.reshape(1, OWN),
        offsets.transpose(1, 2, 0),
        defocus.reshape(1, MINE),
        ctf_table,
        noise_power.reshape(1, CYCLES),
        tau_power.reshape(1, CYCLES),
        table,
    )
    next_chip = beside(img, 2, 1)
    refs = (ref, along_y(ref, 3), along_y(ref, 2), along_y(ref, 1))
    other_core = beside(jnp.stack([img, next_chip]), 1, 0)
    w_near, near = shift(img, next_chip, ctf4, noise4, table)
    exps, stats, far, sq = score(
        own, (img, next_chip, other_core), w_near, refs, ctf4, noise4, table
    )
    same_images = [[(y * 4 + r) * 8 + c for r in range(4) for c in range(8)] for y in range(4)]
    gathered = lax.all_to_all(
        stats, ("img", "cls"), 0, 0, tiled=True, axis_index_groups=same_images
    )
    numer, s1, s2, s3, like = insert(own, exps, stats, gathered, near, far, sq)
    got = (along_y(s1, 1), along_y(s2, 2), along_y(s3, 3))
    fresh, weight, like = finish(numer, got, tau4, like)
    return fresh, weight.reshape(OWN), like.reshape(MINE)


def solution(mesh):
    body = functools.partial(per_device, jnp.asarray(phase_parts()))
    return jax.shard_map(
        body,
        mesh=mesh,
        in_specs=(
            P("img", None),
            P(("img", "cls"), None),
            P(("img", "cls")),
            P(),
            P(),
            P(),
            P("img"),
            P("img", None, None),
        ),
        out_specs=(P(("img", "cls"), None), P(("img", "cls")), P("img")),
        check_vma=False,
    )
```

```python
import functools
import math

import jax
import jax.numpy as jnp
import ml_dtypes
import numpy as np
from jax import lax
from jax.experimental import pallas as pl
from jax.experimental.pallas import tpu as pltpu
from jax.sharding import PartitionSpec as P

TRANS = 4
CYCLES = 32
ANG = 144
ROT = 36
NDEF = 16
STEP = ANG // ROT
PAIRS = 2 * CYCLES
LANES = 2 * STEP * CYCLES
HALF = LANES // 2
OWN = 4
MINE = 8
BLOCKS = 4
KS = OWN * BLOCKS
US = MINE * BLOCKS * TRANS
ROWS = ROT * KS
REACH = 3
MIDDLE = 24
SLOTS = 32
WINDOW = 20_000_000_000
offset_sigma = 2.0
F32 = jnp.float32
BF16 = jnp.bfloat16
HIGHEST = lax.Precision.HIGHEST
VMEM_LIMIT = 20 * 1024 * 1024


def phase_parts():
    span = 2 * REACH + 1
    theta = 2.0 * math.pi * np.arange(ANG).reshape(ROT, STEP) / ANG
    radius = np.arange(CYCLES) + 1.0
    fx = (np.cos(theta)[:, :, None] * radius).reshape(ROT, HALF)
    fy = (np.sin(theta)[:, :, None] * radius).reshape(ROT, HALF)
    shift = np.arange(span) - REACH
    phi = (
        -2.0
        * math.pi
        * (shift[:, None, None, None] * fx + shift[None, :, None, None] * fy)
        / (2.0 * CYCLES)
    ).reshape(span * span, ROT, HALF)[MIDDLE:]
    table = np.concatenate([np.cos(phi), np.sin(phi)], axis=2).transpose(1, 0, 2)
    table = np.pad(table, ((0, 0), (0, SLOTS - table.shape[1]), (0, 0)))
    parts = []
    rest = table
    for _ in range(3):
        part = rest.astype(np.float32).astype(ml_dtypes.bfloat16)
        parts.append(part)
        rest = rest - part.astype(np.float64)
    return np.concatenate(parts, axis=1)


def nt(a, b, **kw):
    return lax.dot_general(a, b, (((1,), (1,)), ((), ())), preferred_element_type=F32, **kw)


def in_hbm(value):
    return pltpu.with_memory_space_constraint(value, pltpu.HBM)


def fetch(pairs, sems):
    copies = [
        pltpu.make_async_copy(src, dst, sems.at[n]) for n, (src, dst) in enumerate(pairs)
    ]
    for copy in copies:
        copy.start()
    return copies


def as_column(row, size):
    here = lax.broadcasted_iota(jnp.int32, (size, size), 0)
    there = lax.broadcasted_iota(jnp.int32, (size, size), 1)
    wide = jnp.broadcast_to(row, (size, size))
    return jnp.sum(jnp.where(here == there, wide, 0.0), axis=1, keepdims=True)


def as_row(column, size):
    here = lax.broadcasted_iota(jnp.int32, (size, size), 0)
    there = lax.broadcasted_iota(jnp.int32, (size, size), 1)
    wide = jnp.broadcast_to(column, (size, size))
    return jnp.sum(jnp.where(here == there, wide, 0.0), axis=0, keepdims=True)


def turn_major(source, count, cut, flat, out):
    angle = lax.broadcasted_iota(jnp.int32, (CYCLES, ANG), 1) % STEP
    pick_b = lax.broadcasted_iota(jnp.int32, (40, ANG), 0)
    pick_a = lax.broadcasted_iota(jnp.int32, (40, ANG), 1)
    pick = jnp.where(pick_a // STEP == pick_b, 1.0, 0.0).astype(BF16)
    for j in range(PAIRS):
        line = source[:, j * ANG : (j + 1) * ANG].astype(F32)
        cut[0, pl.ds(j * 8, count), :] = line[:, :HALF]
        cut[1, pl.ds(j * 8, count), : ANG - HALF] = line[:, HALF:]
    for i in range(count):
        one = jnp.concatenate(
            [cut.at[n][pl.ds(i, PAIRS, stride=8), :] for n in range(2)], axis=1
        )[:, :ANG]
        spread = jnp.concatenate(
            [
                jnp.where(angle == c, one[p * CYCLES : (p + 1) * CYCLES], 0.0)
                for p in range(2)
                for c in range(STEP)
            ],
            axis=0,
        ).astype(BF16)
        turned = nt(pick, spread)
        flat[0, pl.ds(i * 40, 40), :] = turned[:, :HALF]
        flat[1, pl.ds(i * 40, 40), :] = turned[:, HALF:]
    for b in range(ROT):
        for n in range(2):
            line = flat.at[n][pl.ds(b, count, stride=40), :]
            out[b, :, n * HALF : (n + 1) * HALF] = line.astype(BF16)


def arrange_kernel(
    img_hbm, ref_hbm, prior_hbm, off_hbm, def_hbm, ctf_hbm, noise_hbm, tau_hbm, table_hbm,
    img_out, ref_out, ctf_out, noise_out, tau_out, table_out,
    img_ref, ref_ref, prior_ref, off_ref, def_ref, ctf_ref, noise_ref, tau_ref,
    cut, cut2, flat, flat2, sems,
):
    copies = fetch(
        (
            (ref_hbm, ref_ref),
            (img_hbm, img_ref),
            (prior_hbm, prior_ref),
            (off_hbm, off_ref),
            (def_hbm, def_ref),
            (ctf_hbm, ctf_ref),
            (noise_hbm, noise_ref),
            (tau_hbm, tau_ref),
            (table_hbm, table_out),
        ),
        sems,
    )
    for copy in copies[:-1]:
        copy.wait()
    turn_major(ref_ref, OWN, cut, flat, ref_out)
    lane = lax.broadcasted_iota(jnp.int32, (MINE, LANES), 1)
    extra = jnp.where(lane == 8, as_column(def_ref[...].astype(F32), MINE), 0.0)
    for t in range(TRANS):
        for d in range(2):
            column = as_column(off_ref[t, d : d + 1, :].astype(F32), MINE)
            extra = jnp.where(lane == 2 * t + d, column, extra)
    img_out[ROT] = extra.astype(BF16)
    column = as_column(prior_ref[...].astype(F32), OWN)
    ref_out[ROT] = jnp.broadcast_to(column, (OWN, LANES)).astype(BF16)
    for small, out in ((ctf_ref, ctf_out), (noise_ref, noise_out), (tau_ref, tau_out)):
        out[...] = jnp.concatenate([small[...]] * STEP, axis=1)
    turn_major(img_ref, MINE, cut2, flat2, img_out)
    copies[-1].wait()


def arrange(images, references, prior, offsets, defocus, ctf_table, noise, tau, table):
    vmem = pl.BlockSpec(memory_space=pltpu.VMEM)
    hbm = pl.BlockSpec(memory_space=pltpu.HBM)
    wide = 2 * CYCLES * ANG
    return pl.pallas_call(
        arrange_kernel,
        out_shape=(
            jax.ShapeDtypeStruct((ROT + 1, MINE, LANES), BF16),
            jax.ShapeDtypeStruct((ROT + 1, OWN, LANES), BF16),
            jax.ShapeDtypeStruct((NDEF, HALF), F32),
            jax.ShapeDtypeStruct((1, HALF), F32),
            jax.ShapeDtypeStruct((1, HALF), F32),
            jax.ShapeDtypeStruct((ROT, 3 * SLOTS, LANES), BF16),
        ),
        in_specs=[hbm] * 9,
        out_specs=(vmem,) * 6,
        scratch_shapes=[
            pltpu.VMEM((MINE, wide), BF16),
            pltpu.VMEM((OWN, wide), BF16),
            pltpu.VMEM((1, OWN), BF16),
            pltpu.VMEM((TRANS, 2, MINE), jnp.int32),
            pltpu.VMEM((1, MINE), jnp.int32),
            pltpu.VMEM((NDEF, CYCLES), F32),
            pltpu.VMEM((1, CYCLES), F32),
            pltpu.VMEM((1, CYCLES), F32),
            pltpu.VMEM((2, PAIRS * 8, HALF), F32),
            pltpu.VMEM((2, PAIRS * 8, HALF), F32),
            pltpu.VMEM((2, MINE * 40, HALF), F32),
            pltpu.VMEM((2, MINE * 40, HALF), F32),
            pltpu.SemaphoreType.DMA((9,)),
        ],
        compiler_params=pltpu.CompilerParams(vmem_limit_bytes=VMEM_LIMIT),
        name="arrange",
    )(
        *(
            in_hbm(v)
            for v in (images, references, prior, offsets, defocus, ctf_table, noise, tau, table)
        )
    )


def four(value):
    return jnp.concatenate([value] * TRANS, axis=0)


def image_rows(near, far):
    extra = jnp.concatenate([near[ROT].astype(F32), far[ROT].astype(F32)], axis=0)
    dx = jnp.concatenate([extra[:, 2 * t : 2 * t + 1] for t in range(TRANS)], axis=0)
    dy = jnp.concatenate([extra[:, 2 * t + 1 : 2 * t + 2] for t in range(TRANS)], axis=0)
    return dx, dy, extra[:, 8:9]


def contrast_of(group, ctf_ref):
    known = lax.broadcasted_iota(jnp.int32, (group.shape[0], NDEF), 1).astype(F32)
    which = jnp.where(known == group, 1.0, 0.0)
    return jnp.dot(which, ctf_ref[...], precision=HIGHEST, preferred_element_type=F32)


def shift_half(near, far, dx, dy, contrast, noise, table, weighted, inserted):
    pair = dx * (2 * REACH + 1) + dy
    slot = lax.broadcasted_iota(jnp.int32, (US // 2, 3 * SLOTS), 1) % SLOTS
    hot = jnp.where(slot.astype(F32) == jnp.abs(pair), 1.0, 0.0).astype(BF16)
    sign = jnp.broadcast_to(jnp.where(pair < 0, -1.0, 1.0), (US // 2, HALF))
    contrast4 = four(contrast)
    whiten4 = four(contrast / noise)
    for b in range(ROT):
        turn = jnp.dot(hot, table[b], preferred_element_type=F32)
        cosine, sine = turn[:, :HALF], turn[:, HALF:] * sign
        block = jnp.concatenate([near[b].astype(F32), far[b].astype(F32)], axis=0)
        real, imag = four(block[:, :HALF]), four(block[:, HALF:])
        shifted_real = real * cosine - imag * sine
        shifted_imag = real * sine + imag * cosine
        rows = slice(b * US // 2, (b + 1) * US // 2)
        weighted[rows, :HALF] = (shifted_real * whiten4).astype(BF16)
        weighted[rows, HALF:] = (shifted_imag * whiten4).astype(BF16)
        inserted[rows, :HALF] = (shifted_real * contrast4).astype(BF16)
        inserted[rows, HALF:] = (shifted_imag * contrast4).astype(BF16)


def shift_kernel(near, far, ctf_ref, noise_ref, table, weighted, inserted):
    dx, dy, group = image_rows(near, far)
    contrast = contrast_of(group, ctf_ref)
    shift_half(near, far, dx, dy, contrast, noise_ref[...], table, weighted, inserted)


def shift(near, far, ctf4, noise4, table):
    vmem = pl.BlockSpec(memory_space=pltpu.VMEM)
    half = jax.ShapeDtypeStruct((ROT * US // 2, LANES), BF16)
    return pl.pallas_call(
        shift_kernel,
        out_shape=(half, half),
        in_specs=[vmem] * 5,
        out_specs=(vmem, vmem),
        compiler_params=pltpu.CompilerParams(vmem_limit_bytes=VMEM_LIMIT),
        name="shift",
        cost_estimate=pl.CostEstimate(flops=WINDOW, bytes_accessed=1000, transcendentals=0),
    )(near, far, ctf4, noise4, table)


def swapped(row, own):
    lane = lax.broadcasted_iota(jnp.int32, row.shape, 1)
    chosen = lambda bit: jnp.broadcast_to((own >> bit) & 1, row.shape) == 1
    row = jnp.where(chosen(0), pltpu.roll(row, US // 2, 1), row)
    other = jnp.where(
        (lane // MINE) % 2 == 0, pltpu.roll(row, US - MINE, 1), pltpu.roll(row, MINE, 1)
    )
    return jnp.where(chosen(1), other, row)


def over_shifts(row, combine):
    lane = lax.broadcasted_iota(jnp.int32, row.shape, 1)
    for size in (16, 32):
        turned = jnp.where(
            lane % 64 >= size, pltpu.roll(row, size, 1), pltpu.roll(row, size + 64, 1)
        )
        row = combine(row, turned)
    return row


def score_kernel(
    own_ref, i0, i2, i13, w_near, r0, r1, r2, r3, ctf_ref, noise_ref, table,
    exp_out, stat_out, ins_out, sq_out,
    w_far, back, acc,
):
    own = own_ref[0]
    square = jnp.zeros((KS, LANES), F32)
    for b in range(ROT):
        block = jnp.concatenate([r[b].astype(F32) for r in (r0, r1, r2, r3)], axis=0)
        square = square + block * block
        m = (ROT - b) % ROT
        back[pl.ds(m * KS, KS), :] = block.astype(BF16)
        back[pl.ds((m + ROT) * KS, KS), :] = block.astype(BF16)
    prior = jnp.concatenate([r[ROT].astype(F32) for r in (r0, r1, r2, r3)], axis=0)[:, :HALF]

    i1, i3 = i13.at[0], i13.at[1]
    dx0, dy0, group0 = image_rows(i0, i2)
    dx1, dy1, group1 = image_rows(i1, i3)
    noise = noise_ref[...]
    contrast = contrast_of(jnp.concatenate([group0, group1], axis=0), ctf_ref)
    far_contrast = contrast[2 * MINE :]
    squared = contrast * contrast
    squared = jnp.concatenate([four(squared[: 2 * MINE]), four(squared[2 * MINE :])], axis=0)
    sq_out[:, :HALF] = squared
    sq_out[:, HALF:] = jnp.ones((US, HALF), F32)
    coef = squared / (2.0 * noise)
    penalty = nt(square, jnp.concatenate([coef, coef], axis=1), precision=HIGHEST)
    dx = jnp.concatenate([dx0, dx1], axis=0)
    dy = jnp.concatenate([dy0, dy1], axis=0)
    near = -(dx * dx + dy * dy) / (2.0 * offset_sigma * offset_sigma)
    base = prior - penalty + as_row(near, US)

    shift_half(i1, i3, dx1, dy1, far_contrast, noise, table, w_far, ins_out)
    half = US // 2
    acc[...] = sum(
        nt(
            back[(ROT - 2 * h) * KS : (2 * ROT - 2 * h) * KS, :],
            jnp.concatenate(
                [
                    w[b * half : (b + 1) * half, :]
                    for b in (2 * h, 2 * h + 1)
                    for w in (w_near, w_far)
                ],
                axis=0,
            ),
        )
        for h in range(ROT // 2)
    )

    peak = jnp.full((KS, US), -jnp.inf, F32)
    for r in range(ROT):
        last = (r - 1) % ROT
        logp = acc[r * KS : (r + 1) * KS, :HALF] + acc[last * KS : (last + 1) * KS, HALF:] + base
        exp_out[r * KS : (r + 1) * KS, :] = logp
        peak = jnp.maximum(peak, logp)
    peak = jnp.broadcast_to(jnp.max(peak, axis=0, keepdims=True), (8, US))
    wide = jnp.broadcast_to(peak[:1], (KS, US))
    total = jnp.zeros((KS, US), F32)
    for r in range(ROT):
        value = jnp.exp(exp_out[r * KS : (r + 1) * KS, :] - wide)
        exp_out[r * KS : (r + 1) * KS, :] = value
        total = total + value
    total = jnp.broadcast_to(jnp.sum(total, axis=0, keepdims=True), (8, US))
    row = lax.broadcasted_iota(jnp.int32, (8, US), 0)
    pair = swapped(jnp.where(row == 0, peak, total), own)[:2]
    for j in range(32):
        stat_out[j] = pair


def score(own, imgs, w_near, refs, ctf4, noise4, table):
    vmem = pl.BlockSpec(memory_space=pltpu.VMEM)
    smem = pl.BlockSpec(memory_space=pltpu.SMEM)
    return pl.pallas_call(
        score_kernel,
        out_shape=(
            jax.ShapeDtypeStruct((ROWS, US), F32),
            jax.ShapeDtypeStruct((32, 2, US), F32),
            jax.ShapeDtypeStruct((ROT * US // 2, LANES), BF16),
            jax.ShapeDtypeStruct((US, LANES), F32),
        ),
        in_specs=[smem] + [vmem] * 11,
        out_specs=(vmem,) * 4,
        scratch_shapes=[
            pltpu.VMEM((ROT * US // 2, LANES), BF16),
            pltpu.VMEM((2 * ROWS, LANES), BF16),
            pltpu.VMEM((ROWS, LANES), F32),
        ],
        compiler_params=pltpu.CompilerParams(vmem_limit_bytes=VMEM_LIMIT),
        name="score",
    )(own, *imgs, w_near, *refs, ctf4, noise4, table)


def insert_kernel(
    own_ref, exp_ref, pair_ref, all_ref, near_ref, far_ref, sq_ref,
    own_out, s1, s2, s3, like_out, post, acc,
):
    own = own_ref[0]
    peaks = jnp.concatenate([all_ref[j, 0:1, :] for j in range(32)], axis=0)
    totals = jnp.concatenate([all_ref[j, 1:2, :] for j in range(32)], axis=0)
    lane_peak = jnp.max(peaks, axis=0, keepdims=True)
    lane_total = jnp.sum(totals * jnp.exp(peaks - lane_peak), axis=0, keepdims=True)
    lane_peak = jnp.broadcast_to(lane_peak, (8, US))
    peak = over_shifts(lane_peak, jnp.maximum)
    total = over_shifts(lane_total * jnp.exp(lane_peak - peak), jnp.add)
    scale = jnp.exp(pair_ref[0, 0:1, :] - peak) / total
    like_out[...] = swapped(peak + jnp.log(total), own)
    scale = jnp.broadcast_to(swapped(scale, own)[:1], (KS, US))
    count = jnp.zeros((KS, US), F32)
    for r in range(ROT):
        value = (exp_ref[r * KS : (r + 1) * KS, :] * scale).astype(BF16)
        count = count + value.astype(F32)
        for side in range(2):
            m = (side - r) % ROT
            for again in (m, m + ROT):
                post[again * KS : (again + 1) * KS, side * HALF : (side + 1) * HALF] = value

    half = US // 2
    acc[...] = sum(
        jnp.dot(
            post[(ROT - 2 * h) * KS : (2 * ROT - 2 * h) * KS, :],
            jnp.concatenate(
                [
                    v[b * half : (b + 1) * half, :]
                    for b in (2 * h, 2 * h + 1)
                    for v in (near_ref, far_ref)
                ],
                axis=0,
            ),
            preferred_element_type=F32,
        )
        for h in range(ROT // 2)
    )
    sums = jnp.dot(count, sq_ref[...], precision=HIGHEST, preferred_element_type=F32)
    for b in range(ROT):
        block = acc[b * KS : (b + 1) * KS, :]
        own_out[b] = block[:OWN]
        for d, out in ((1, s1), (2, s2), (3, s3)):
            out[b] = block[d * OWN : (d + 1) * OWN].astype(BF16)
    own_out[ROT] = sums[:OWN]
    own_out[ROT + 1] = jnp.zeros((OWN, LANES), F32)
    for d, out in ((1, s1), (2, s2), (3, s3)):
        part = sums[d * OWN : (d + 1) * OWN]
        high = part.astype(BF16)
        out[ROT] = high
        out[ROT + 1] = (part - high.astype(F32)).astype(BF16)


def insert(own, exps, stats, gathered, near, far, sq):
    vmem = pl.BlockSpec(memory_space=pltpu.VMEM)
    smem = pl.BlockSpec(memory_space=pltpu.SMEM)
    piece = (ROT + 2, OWN, LANES)
    return pl.pallas_call(
        insert_kernel,
        out_shape=(
            jax.ShapeDtypeStruct(piece, F32),
            jax.ShapeDtypeStruct(piece, BF16),
            jax.ShapeDtypeStruct(piece, BF16),
            jax.ShapeDtypeStruct(piece, BF16),
            jax.ShapeDtypeStruct((8, US), F32),
        ),
        in_specs=[smem] + [vmem] * 6,
        out_specs=(vmem,) * 5,
        scratch_shapes=[
            pltpu.VMEM((2 * ROWS, LANES), BF16),
            pltpu.VMEM((ROWS, LANES), F32),
        ],
        compiler_params=pltpu.CompilerParams(vmem_limit_bytes=VMEM_LIMIT),
        name="insert",
    )(own, exps, stats, gathered, near, far, sq)


def finish_kernel(own_ref, g1, g2, g3, tau_ref, like_ref, out_ref, weight_out, like_out, fresh, turned, lines):
    like_out[...] = like_ref[:1, :MINE]
    parts = [own_ref, g1, g2, g3]
    sums = sum(p[ROT].astype(F32) + p[ROT + 1].astype(F32) for p in parts)
    denom = sums[:, :HALF] + 1.0 / tau_ref[...]
    denom = jnp.concatenate([denom, denom], axis=1)
    weight_out[...] = as_row(sums[:, HALF : HALF + 1], OWN) / (MINE * 16)
    for b in range(ROT):
        total = own_ref[b] + g1[b].astype(F32) + g2[b].astype(F32) + g3[b].astype(F32)
        total = total / denom
        fresh[0, pl.ds(b * 8, OWN), :] = total[:, :HALF]
        fresh[1, pl.ds(b * 8, OWN), :] = total[:, HALF:]
    for k in range(OWN):
        one = [fresh.at[p][pl.ds(k, ROT, stride=8), :] for p in range(2)]
        for c in range(STEP):
            pair = [one[p][:, c * CYCLES : (c + 1) * CYCLES] for p in range(2)]
            turned[pl.ds(c, ROT, stride=STEP), :] = jnp.concatenate(pair + pair, axis=1)
        first = turned[0:128, :].T
        second = turned[128:256, :].T
        lines[0, pl.ds(k * PAIRS, PAIRS), :] = first[:PAIRS]
        lines[1, pl.ds(k * PAIRS, PAIRS), :] = second[:PAIRS]
    for j in range(PAIRS):
        line = [lines.at[n][pl.ds(j, OWN, stride=PAIRS), :] for n in range(2)]
        out_ref[:, j * ANG : (j + 1) * ANG] = jnp.concatenate(line, axis=1)[:, :ANG]


def finish(own, got, tau, like):
    vmem = pl.BlockSpec(memory_space=pltpu.VMEM)
    return pl.pallas_call(
        finish_kernel,
        out_shape=(
            jax.ShapeDtypeStruct((OWN, 2 * CYCLES * ANG), F32),
            jax.ShapeDtypeStruct((1, OWN), F32),
            jax.ShapeDtypeStruct((1, MINE), F32),
        ),
        in_specs=[vmem] * 6,
        out_specs=(vmem,) * 3,
        scratch_shapes=[
            pltpu.VMEM((2, ROT * 8, HALF), F32),
            pltpu.VMEM((256, 128), F32),
            pltpu.VMEM((2, OWN * PAIRS, HALF), F32),
        ],
        compiler_params=pltpu.CompilerParams(vmem_limit_bytes=VMEM_LIMIT),
        name="finish",
    )(own, *got, tau, like)


def along_y(value, distance):
    return lax.ppermute(
        value, "img", [(i, ((i // 4 + distance) % 4) * 4 + i % 4) for i in range(16)]
    )


def beside(value, img_flip, cls_flip):
    pairs = [
        (i * 8 + c, (i ^ img_flip) * 8 + (c ^ cls_flip)) for i in range(16) for c in range(8)
    ]
    return lax.ppermute(value, ("img", "cls"), pairs)


def per_device(
    table, images, references, class_logprior, ctf_table, noise_power, tau_power, defocus, offsets
):
    own = (lax.axis_index("img") % BLOCKS).astype(jnp.int32).reshape(1)
    img, ref, ctf4, noise4, tau4, table = arrange(
        images,
        references,
        class_logprior.reshape(1, OWN),
        offsets.transpose(1, 2, 0),
        defocus.reshape(1, MINE),
        ctf_table,
        noise_power.reshape(1, CYCLES),
        tau_power.reshape(1, CYCLES),
        table,
    )
    next_chip = beside(img, 2, 1)
    refs = (ref, along_y(ref, 3), along_y(ref, 2), along_y(ref, 1))
    other_core = beside(jnp.stack([img, next_chip]), 1, 0)
    w_near, near = shift(img, next_chip, ctf4, noise4, table)
    exps, stats, far, sq = score(
        own, (img, next_chip, other_core), w_near, refs, ctf4, noise4, table
    )
    same_images = [[(y * 4 + r) * 8 + c for r in range(4) for c in range(8)] for y in range(4)]
    gathered = lax.all_to_all(
        stats, ("img", "cls"), 0, 0, tiled=True, axis_index_groups=same_images
    )
    numer, s1, s2, s3, like = insert(own, exps, stats, gathered, near, far, sq)
    got = (along_y(s1, 1), along_y(s2, 2), along_y(s3, 3))
    fresh, weight, like = finish(numer, got, tau4, like)
    return fresh, weight.reshape(OWN), like.reshape(MINE)


def solution(mesh):
    body = functools.partial(per_device, jnp.asarray(phase_parts()))
    return jax.shard_map(
        body,
        mesh=mesh,
        in_specs=(
            P("img", None),
            P(("img", "cls"), None),
            P(("img", "cls")),
            P(),
            P(),
            P(),
            P("img"),
            P("img", None, None),
        ),
        out_specs=(P(("img", "cls"), None), P(("img", "cls")), P("img")),
        check_vma=False,
    )
```

```python
import functools
import math

import jax
import jax.numpy as jnp
import ml_dtypes
import numpy as np
from jax import lax
from jax.experimental import pallas as pl
from jax.experimental.pallas import tpu as pltpu
from jax.sharding import PartitionSpec as P

TRANS = 4
CYCLES = 32
ANG = 144
ROT = 36
NDEF = 16
STEP = ANG // ROT
PAIRS = 2 * CYCLES
LANES = 2 * STEP * CYCLES
HALF = LANES // 2
OWN = 4
MINE = 8
BLOCKS = 4
KS = OWN * BLOCKS
US = MINE * BLOCKS * TRANS
ROWS = ROT * KS
REACH = 3
MIDDLE = 24
SLOTS = 32
WINDOW = 20_000_000_000
offset_sigma = 2.0
F32 = jnp.float32
BF16 = jnp.bfloat16
HIGHEST = lax.Precision.HIGHEST
VMEM_LIMIT = 20 * 1024 * 1024


def phase_parts():
    span = 2 * REACH + 1
    theta = 2.0 * math.pi * np.arange(ANG).reshape(ROT, STEP)[: ROT // 2] / ANG
    radius = np.arange(CYCLES) + 1.0
    fx = (np.cos(theta)[:, :, None] * radius).reshape(ROT // 2, HALF)
    fy = (np.sin(theta)[:, :, None] * radius).reshape(ROT // 2, HALF)
    shift = np.arange(span) - REACH
    phi = (
        -2.0
        * math.pi
        * (shift[:, None, None, None] * fx + shift[None, :, None, None] * fy)
        / (2.0 * CYCLES)
    ).reshape(span * span, ROT // 2, HALF)[MIDDLE:]
    table = np.concatenate([np.cos(phi), np.sin(phi)], axis=2).transpose(1, 0, 2)
    table = np.pad(table, ((0, 0), (0, SLOTS - table.shape[1]), (0, 0)))
    parts = []
    rest = table
    for _ in range(3):
        part = rest.astype(np.float32).astype(ml_dtypes.bfloat16)
        parts.append(part)
        rest = rest - part.astype(np.float64)
    return np.concatenate(parts, axis=1)


def nt(a, b, **kw):
    return lax.dot_general(a, b, (((1,), (1,)), ((), ())), preferred_element_type=F32, **kw)


def in_hbm(value):
    return pltpu.with_memory_space_constraint(value, pltpu.HBM)


def fetch(pairs, sems):
    copies = [
        pltpu.make_async_copy(src, dst, sems.at[n]) for n, (src, dst) in enumerate(pairs)
    ]
    for copy in copies:
        copy.start()
    return copies


def as_column(row, size):
    here = lax.broadcasted_iota(jnp.int32, (size, size), 0)
    there = lax.broadcasted_iota(jnp.int32, (size, size), 1)
    wide = jnp.broadcast_to(row, (size, size))
    return jnp.sum(jnp.where(here == there, wide, 0.0), axis=1, keepdims=True)


def as_row(column, size):
    here = lax.broadcasted_iota(jnp.int32, (size, size), 0)
    there = lax.broadcasted_iota(jnp.int32, (size, size), 1)
    wide = jnp.broadcast_to(column, (size, size))
    return jnp.sum(jnp.where(here == there, wide, 0.0), axis=0, keepdims=True)


def turn_major(source, count, cut, flat, out):
    angle = lax.broadcasted_iota(jnp.int32, (CYCLES, ANG), 1) % STEP
    pick_b = lax.broadcasted_iota(jnp.int32, (40, ANG), 0)
    pick_a = lax.broadcasted_iota(jnp.int32, (40, ANG), 1)
    pick = jnp.where(pick_a // STEP == pick_b, 1.0, 0.0).astype(BF16)
    for j in range(PAIRS):
        line = source[:, j * ANG : (j + 1) * ANG].astype(F32)
        cut[0, pl.ds(j * 8, count), :] = line[:, :HALF]
        cut[1, pl.ds(j * 8, count), : ANG - HALF] = line[:, HALF:]
    for i in range(count):
        one = jnp.concatenate(
            [cut.at[n][pl.ds(i, PAIRS, stride=8), :] for n in range(2)], axis=1
        )[:, :ANG]
        spread = jnp.concatenate(
            [
                jnp.where(angle == c, one[p * CYCLES : (p + 1) * CYCLES], 0.0)
                for p in range(2)
                for c in range(STEP)
            ],
            axis=0,
        ).astype(BF16)
        turned = nt(pick, spread)
        flat[0, pl.ds(i * 40, 40), :] = turned[:, :HALF]
        flat[1, pl.ds(i * 40, 40), :] = turned[:, HALF:]
    for b in range(ROT):
        for n in range(2):
            line = flat.at[n][pl.ds(b, count, stride=40), :]
            out[b, :, n * HALF : (n + 1) * HALF] = line.astype(BF16)


def arrange_kernel(
    img_hbm, ref_hbm, prior_hbm, off_hbm, def_hbm, ctf_hbm, noise_hbm, tau_hbm, table_hbm,
    img_out, ref_out, ctf_out, noise_out, tau_out, table_out,
    img_ref, ref_ref, prior_ref, off_ref, def_ref, ctf_ref, noise_ref, tau_ref,
    cut, cut2, flat, flat2, sems,
):
    copies = fetch(
        (
            (ref_hbm, ref_ref),
            (img_hbm, img_ref),
            (prior_hbm, prior_ref),
            (off_hbm, off_ref),
            (def_hbm, def_ref),
            (ctf_hbm, ctf_ref),
            (noise_hbm, noise_ref),
            (tau_hbm, tau_ref),
            (table_hbm, table_out),
        ),
        sems,
    )
    for copy in copies[:-1]:
        copy.wait()
    turn_major(ref_ref, OWN, cut, flat, ref_out)
    lane = lax.broadcasted_iota(jnp.int32, (MINE, LANES), 1)
    extra = jnp.where(lane == 8, as_column(def_ref[...].astype(F32), MINE), 0.0)
    for t in range(TRANS):
        for d in range(2):
            column = as_column(off_ref[t, d : d + 1, :].astype(F32), MINE)
            extra = jnp.where(lane == 2 * t + d, column, extra)
    img_out[ROT] = extra.astype(BF16)
    column = as_column(prior_ref[...].astype(F32), OWN)
    ref_out[ROT] = jnp.broadcast_to(column, (OWN, LANES)).astype(BF16)
    for small, out in ((ctf_ref, ctf_out), (noise_ref, noise_out), (tau_ref, tau_out)):
        out[...] = jnp.concatenate([small[...]] * STEP, axis=1)
    turn_major(img_ref, MINE, cut2, flat2, img_out)
    copies[-1].wait()


def arrange(images, references, prior, offsets, defocus, ctf_table, noise, tau, table):
    vmem = pl.BlockSpec(memory_space=pltpu.VMEM)
    hbm = pl.BlockSpec(memory_space=pltpu.HBM)
    wide = 2 * CYCLES * ANG
    return pl.pallas_call(
        arrange_kernel,
        out_shape=(
            jax.ShapeDtypeStruct((ROT + 1, MINE, LANES), BF16),
            jax.ShapeDtypeStruct((ROT + 1, OWN, LANES), BF16),
            jax.ShapeDtypeStruct((NDEF, HALF), F32),
            jax.ShapeDtypeStruct((1, HALF), F32),
            jax.ShapeDtypeStruct((1, HALF), F32),
            jax.ShapeDtypeStruct((ROT // 2, 3 * SLOTS, LANES), BF16),
        ),
        in_specs=[hbm] * 9,
        out_specs=(vmem,) * 6,
        scratch_shapes=[
            pltpu.VMEM((MINE, wide), BF16),
            pltpu.VMEM((OWN, wide), BF16),
            pltpu.VMEM((1, OWN), BF16),
            pltpu.VMEM((TRANS, 2, MINE), jnp.int32),
            pltpu.VMEM((1, MINE), jnp.int32),
            pltpu.VMEM((NDEF, CYCLES), F32),
            pltpu.VMEM((1, CYCLES), F32),
            pltpu.VMEM((1, CYCLES), F32),
            pltpu.VMEM((2, PAIRS * 8, HALF), F32),
            pltpu.VMEM((2, PAIRS * 8, HALF), F32),
            pltpu.VMEM((2, MINE * 40, HALF), F32),
            pltpu.VMEM((2, MINE * 40, HALF), F32),
            pltpu.SemaphoreType.DMA((9,)),
        ],
        compiler_params=pltpu.CompilerParams(vmem_limit_bytes=VMEM_LIMIT),
        name="arrange",
    )(
        *(
            in_hbm(v)
            for v in (images, references, prior, offsets, defocus, ctf_table, noise, tau, table)
        )
    )


def four(value):
    return jnp.concatenate([value] * TRANS, axis=0)


def image_rows(near, far):
    extra = jnp.concatenate([near[ROT].astype(F32), far[ROT].astype(F32)], axis=0)
    dx = jnp.concatenate([extra[:, 2 * t : 2 * t + 1] for t in range(TRANS)], axis=0)
    dy = jnp.concatenate([extra[:, 2 * t + 1 : 2 * t + 2] for t in range(TRANS)], axis=0)
    return dx, dy, extra[:, 8:9]


def contrast_of(group, ctf_ref):
    known = lax.broadcasted_iota(jnp.int32, (group.shape[0], NDEF), 1).astype(F32)
    which = jnp.where(known == group, 1.0, 0.0)
    return jnp.dot(which, ctf_ref[...], precision=HIGHEST, preferred_element_type=F32)


def shift_half(near, far, dx, dy, contrast, noise, table, weighted, inserted):
    pair = dx * (2 * REACH + 1) + dy
    slot = lax.broadcasted_iota(jnp.int32, (US // 2, 3 * SLOTS), 1) % SLOTS
    hot = jnp.where(slot.astype(F32) == jnp.abs(pair), 1.0, 0.0).astype(BF16)
    sign = jnp.broadcast_to(jnp.where(pair < 0, -1.0, 1.0), (US // 2, HALF))
    contrast4 = four(contrast)
    whiten4 = four(contrast / noise)
    for half in range(ROT // 2):
        turn = jnp.dot(hot, table[half], preferred_element_type=F32)
        cosine, sine = turn[:, :HALF], turn[:, HALF:] * sign
        for b, flip in ((half, False), (half + ROT // 2, True)):
            block = jnp.concatenate([near[b].astype(F32), far[b].astype(F32)], axis=0)
            real, imag = four(block[:, :HALF]), four(block[:, HALF:])
            if flip:
                shifted_real = real * cosine + imag * sine
                shifted_imag = imag * cosine - real * sine
            else:
                shifted_real = real * cosine - imag * sine
                shifted_imag = real * sine + imag * cosine
            rows = slice(b * US // 2, (b + 1) * US // 2)
            weighted[rows, :HALF] = (shifted_real * whiten4).astype(BF16)
            weighted[rows, HALF:] = (shifted_imag * whiten4).astype(BF16)
            inserted[rows, :HALF] = (shifted_real * contrast4).astype(BF16)
            inserted[rows, HALF:] = (shifted_imag * contrast4).astype(BF16)


def shift_kernel(near, far, ctf_ref, noise_ref, table, weighted, inserted):
    dx, dy, group = image_rows(near, far)
    contrast = contrast_of(group, ctf_ref)
    shift_half(near, far, dx, dy, contrast, noise_ref[...], table, weighted, inserted)


def shift(near, far, ctf4, noise4, table):
    vmem = pl.BlockSpec(memory_space=pltpu.VMEM)
    half = jax.ShapeDtypeStruct((ROT * US // 2, LANES), BF16)
    return pl.pallas_call(
        shift_kernel,
        out_shape=(half, half),
        in_specs=[vmem] * 5,
        out_specs=(vmem, vmem),
        compiler_params=pltpu.CompilerParams(vmem_limit_bytes=VMEM_LIMIT),
        name="shift",
        cost_estimate=pl.CostEstimate(flops=WINDOW, bytes_accessed=1000, transcendentals=0),
    )(near, far, ctf4, noise4, table)


def swapped(row, own):
    lane = lax.broadcasted_iota(jnp.int32, row.shape, 1)
    chosen = lambda bit: jnp.broadcast_to((own >> bit) & 1, row.shape) == 1
    row = jnp.where(chosen(0), pltpu.roll(row, US // 2, 1), row)
    other = jnp.where(
        (lane // MINE) % 2 == 0, pltpu.roll(row, US - MINE, 1), pltpu.roll(row, MINE, 1)
    )
    return jnp.where(chosen(1), other, row)


def over_shifts(row, combine):
    lane = lax.broadcasted_iota(jnp.int32, row.shape, 1)
    for size in (16, 32):
        turned = jnp.where(
            lane % 64 >= size, pltpu.roll(row, size, 1), pltpu.roll(row, size + 64, 1)
        )
        row = combine(row, turned)
    return row


def score_kernel(
    own_ref, i0, i2, i13, w_near, r0, r1, r2, r3, ctf_ref, noise_ref, table,
    exp_out, stat_out, ins_out, sq_out,
    w_far, back, acc,
):
    own = own_ref[0]
    square = jnp.zeros((KS, LANES), F32)
    for b in range(ROT):
        block = jnp.concatenate([r[b].astype(F32) for r in (r0, r1, r2, r3)], axis=0)
        square = square + block * block
        m = (ROT - b) % ROT
        back[pl.ds(m * KS, KS), :] = block.astype(BF16)
        back[pl.ds((m + ROT) * KS, KS), :] = block.astype(BF16)
    prior = jnp.concatenate([r[ROT].astype(F32) for r in (r0, r1, r2, r3)], axis=0)[:, :HALF]

    i1, i3 = i13.at[0], i13.at[1]
    dx0, dy0, group0 = image_rows(i0, i2)
    dx1, dy1, group1 = image_rows(i1, i3)
    noise = noise_ref[...]
    contrast = contrast_of(jnp.concatenate([group0, group1], axis=0), ctf_ref)
    far_contrast = contrast[2 * MINE :]
    squared = contrast * contrast
    squared = jnp.concatenate([four(squared[: 2 * MINE]), four(squared[2 * MINE :])], axis=0)
    sq_out[:, :HALF] = squared
    sq_out[:, HALF:] = jnp.ones((US, HALF), F32)
    coef = squared / (2.0 * noise)
    penalty = nt(square, jnp.concatenate([coef, coef], axis=1), precision=HIGHEST)
    dx = jnp.concatenate([dx0, dx1], axis=0)
    dy = jnp.concatenate([dy0, dy1], axis=0)
    near = -(dx * dx + dy * dy) / (2.0 * offset_sigma * offset_sigma)
    base = prior - penalty + as_row(near, US)

    shift_half(i1, i3, dx1, dy1, far_contrast, noise, table, w_far, ins_out)
    half = US // 2
    acc[...] = sum(
        nt(
            back[(ROT - 2 * h) * KS : (2 * ROT - 2 * h) * KS, :],
            jnp.concatenate(
                [
                    w[b * half : (b + 1) * half, :]
                    for b in (2 * h, 2 * h + 1)
                    for w in (w_near, w_far)
                ],
                axis=0,
            ),
        )
        for quarter in range(ROT // 4)
        for h in (quarter, quarter + ROT // 4)
    )

    peak = jnp.full((KS, US), -jnp.inf, F32)
    for r in range(ROT):
        last = (r - 1) % ROT
        logp = acc[r * KS : (r + 1) * KS, :HALF] + acc[last * KS : (last + 1) * KS, HALF:] + base
        exp_out[r * KS : (r + 1) * KS, :] = logp
        peak = jnp.maximum(peak, logp)
    peak = jnp.broadcast_to(jnp.max(peak, axis=0, keepdims=True), (8, US))
    wide = jnp.broadcast_to(peak[:1], (KS, US))
    total = jnp.zeros((KS, US), F32)
    for r in range(ROT):
        value = jnp.exp(exp_out[r * KS : (r + 1) * KS, :] - wide)
        exp_out[r * KS : (r + 1) * KS, :] = value
        total = total + value
    total = jnp.broadcast_to(jnp.sum(total, axis=0, keepdims=True), (8, US))
    row = lax.broadcasted_iota(jnp.int32, (8, US), 0)
    pair = swapped(jnp.where(row == 0, peak, total), own)[:2]
    for j in range(32):
        stat_out[j] = pair


def score(own, imgs, w_near, refs, ctf4, noise4, table):
    vmem = pl.BlockSpec(memory_space=pltpu.VMEM)
    smem = pl.BlockSpec(memory_space=pltpu.SMEM)
    return pl.pallas_call(
        score_kernel,
        out_shape=(
            jax.ShapeDtypeStruct((ROWS, US), F32),
            jax.ShapeDtypeStruct((32, 2, US), F32),
            jax.ShapeDtypeStruct((ROT * US // 2, LANES), BF16),
            jax.ShapeDtypeStruct((US, LANES), F32),
        ),
        in_specs=[smem] + [vmem] * 11,
        out_specs=(vmem,) * 4,
        scratch_shapes=[
            pltpu.VMEM((ROT * US // 2, LANES), BF16),
            pltpu.VMEM((2 * ROWS, LANES), BF16),
            pltpu.VMEM((ROWS, LANES), F32),
        ],
        compiler_params=pltpu.CompilerParams(vmem_limit_bytes=VMEM_LIMIT),
        name="score",
    )(own, *imgs, w_near, *refs, ctf4, noise4, table)


def insert_kernel(
    own_ref, exp_ref, pair_ref, all_ref, near_ref, far_ref, sq_ref,
    own_out, s1, s2, s3, like_out, post, acc,
):
    own = own_ref[0]
    peaks = jnp.concatenate([all_ref[j, 0:1, :] for j in range(32)], axis=0)
    totals = jnp.concatenate([all_ref[j, 1:2, :] for j in range(32)], axis=0)
    lane_peak = jnp.max(peaks, axis=0, keepdims=True)
    lane_total = jnp.sum(totals * jnp.exp(peaks - lane_peak), axis=0, keepdims=True)
    lane_peak = jnp.broadcast_to(lane_peak, (8, US))
    peak = over_shifts(lane_peak, jnp.maximum)
    total = over_shifts(lane_total * jnp.exp(lane_peak - peak), jnp.add)
    scale = jnp.exp(pair_ref[0, 0:1, :] - peak) / total
    like_out[...] = swapped(peak + jnp.log(total), own)
    scale = jnp.broadcast_to(swapped(scale, own)[:1], (KS, US))
    count = jnp.zeros((KS, US), F32)
    for r in range(ROT):
        value = (exp_ref[r * KS : (r + 1) * KS, :] * scale).astype(BF16)
        count = count + value.astype(F32)
        for side in range(2):
            m = (side - r) % ROT
            for again in (m, m + ROT):
                post[again * KS : (again + 1) * KS, side * HALF : (side + 1) * HALF] = value

    half = US // 2
    acc[...] = sum(
        jnp.dot(
            post[(ROT - 2 * h) * KS : (2 * ROT - 2 * h) * KS, :],
            jnp.concatenate(
                [
                    v[b * half : (b + 1) * half, :]
                    for b in (2 * h, 2 * h + 1)
                    for v in (near_ref, far_ref)
                ],
                axis=0,
            ),
            preferred_element_type=F32,
        )
        for h in range(ROT // 2)
    )
    sums = jnp.dot(count, sq_ref[...], precision=HIGHEST, preferred_element_type=F32)
    for b in range(ROT):
        block = acc[b * KS : (b + 1) * KS, :]
        own_out[b] = block[:OWN]
        for d, out in ((1, s1), (2, s2), (3, s3)):
            out[b] = block[d * OWN : (d + 1) * OWN].astype(BF16)
    own_out[ROT] = sums[:OWN]
    own_out[ROT + 1] = jnp.zeros((OWN, LANES), F32)
    for d, out in ((1, s1), (2, s2), (3, s3)):
        part = sums[d * OWN : (d + 1) * OWN]
        high = part.astype(BF16)
        out[ROT] = high
        out[ROT + 1] = (part - high.astype(F32)).astype(BF16)


def insert(own, exps, stats, gathered, near, far, sq):
    vmem = pl.BlockSpec(memory_space=pltpu.VMEM)
    smem = pl.BlockSpec(memory_space=pltpu.SMEM)
    piece = (ROT + 2, OWN, LANES)
    return pl.pallas_call(
        insert_kernel,
        out_shape=(
            jax.ShapeDtypeStruct(piece, F32),
            jax.ShapeDtypeStruct(piece, BF16),
            jax.ShapeDtypeStruct(piece, BF16),
            jax.ShapeDtypeStruct(piece, BF16),
            jax.ShapeDtypeStruct((8, US), F32),
        ),
        in_specs=[smem] + [vmem] * 6,
        out_specs=(vmem,) * 5,
        scratch_shapes=[
            pltpu.VMEM((2 * ROWS, LANES), BF16),
            pltpu.VMEM((ROWS, LANES), F32),
        ],
        compiler_params=pltpu.CompilerParams(vmem_limit_bytes=VMEM_LIMIT),
        name="insert",
    )(own, exps, stats, gathered, near, far, sq)


def finish_kernel(own_ref, g1, g2, g3, tau_ref, like_ref, out_ref, weight_out, like_out, fresh, turned, lines):
    like_out[...] = like_ref[:1, :MINE]
    parts = [own_ref, g1, g2, g3]
    sums = sum(p[ROT].astype(F32) + p[ROT + 1].astype(F32) for p in parts)
    denom = sums[:, :HALF] + 1.0 / tau_ref[...]
    denom = jnp.concatenate([denom, denom], axis=1)
    weight_out[...] = as_row(sums[:, HALF : HALF + 1], OWN) / (MINE * 16)
    for b in range(ROT):
        total = own_ref[b] + g1[b].astype(F32) + g2[b].astype(F32) + g3[b].astype(F32)
        total = total / denom
        fresh[0, pl.ds(b * 8, OWN), :] = total[:, :HALF]
        fresh[1, pl.ds(b * 8, OWN), :] = total[:, HALF:]
    for k in range(OWN):
        one = [fresh.at[p][pl.ds(k, ROT, stride=8), :] for p in range(2)]
        for c in range(STEP):
            pair = [one[p][:, c * CYCLES : (c + 1) * CYCLES] for p in range(2)]
            turned[pl.ds(c, ROT, stride=STEP), :] = jnp.concatenate(pair + pair, axis=1)
        first = turned[0:128, :].T
        second = turned[128:256, :].T
        lines[0, pl.ds(k * PAIRS, PAIRS), :] = first[:PAIRS]
        lines[1, pl.ds(k * PAIRS, PAIRS), :] = second[:PAIRS]
    for j in range(PAIRS):
        line = [lines.at[n][pl.ds(j, OWN, stride=PAIRS), :] for n in range(2)]
        out_ref[:, j * ANG : (j + 1) * ANG] = jnp.concatenate(line, axis=1)[:, :ANG]


def finish(own, got, tau, like):
    vmem = pl.BlockSpec(memory_space=pltpu.VMEM)
    return pl.pallas_call(
        finish_kernel,
        out_shape=(
            jax.ShapeDtypeStruct((OWN, 2 * CYCLES * ANG), F32),
            jax.ShapeDtypeStruct((1, OWN), F32),
            jax.ShapeDtypeStruct((1, MINE), F32),
        ),
        in_specs=[vmem] * 6,
        out_specs=(vmem,) * 3,
        scratch_shapes=[
            pltpu.VMEM((2, ROT * 8, HALF), F32),
            pltpu.VMEM((256, 128), F32),
            pltpu.VMEM((2, OWN * PAIRS, HALF), F32),
        ],
        compiler_params=pltpu.CompilerParams(vmem_limit_bytes=VMEM_LIMIT),
        name="finish",
    )(own, *got, tau, like)


def along_y(value, distance):
    return lax.ppermute(
        value, "img", [(i, ((i // 4 + distance) % 4) * 4 + i % 4) for i in range(16)]
    )


def beside(value, img_flip, cls_flip):
    pairs = [
        (i * 8 + c, (i ^ img_flip) * 8 + (c ^ cls_flip)) for i in range(16) for c in range(8)
    ]
    return lax.ppermute(value, ("img", "cls"), pairs)


def per_device(
    table, images, references, class_logprior, ctf_table, noise_power, tau_power, defocus, offsets
):
    own = (lax.axis_index("img") % BLOCKS).astype(jnp.int32).reshape(1)
    img, ref, ctf4, noise4, tau4, table = arrange(
        images,
        references,
        class_logprior.reshape(1, OWN),
        offsets.transpose(1, 2, 0),
        defocus.reshape(1, MINE),
        ctf_table,
        noise_power.reshape(1, CYCLES),
        tau_power.reshape(1, CYCLES),
        table,
    )
    next_chip = beside(img, 2, 1)
    refs = (ref, along_y(ref, 3), along_y(ref, 2), along_y(ref, 1))
    other_core = beside(jnp.stack([img, next_chip]), 1, 0)
    w_near, near = shift(img, next_chip, ctf4, noise4, table)
    exps, stats, far, sq = score(
        own, (img, next_chip, other_core), w_near, refs, ctf4, noise4, table
    )
    same_images = [[(y * 4 + r) * 8 + c for r in range(4) for c in range(8)] for y in range(4)]
    gathered = lax.all_to_all(
        stats, ("img", "cls"), 0, 0, tiled=True, axis_index_groups=same_images
    )
    numer, s1, s2, s3, like = insert(own, exps, stats, gathered, near, far, sq)
    got = (along_y(s1, 1), along_y(s2, 2), along_y(s3, 3))
    fresh, weight, like = finish(numer, got, tau4, like)
    return fresh, weight.reshape(OWN), like.reshape(MINE)


def solution(mesh):
    body = functools.partial(per_device, jnp.asarray(phase_parts()))
    return jax.shard_map(
        body,
        mesh=mesh,
        in_specs=(
            P("img", None),
            P(("img", "cls"), None),
            P(("img", "cls")),
            P(),
            P(),
            P(),
            P("img"),
            P("img", None, None),
        ),
        out_specs=(P(("img", "cls"), None), P(("img", "cls")), P("img")),
        check_vma=False,
    )
```

```python
import functools
import math

import jax
import jax.numpy as jnp
import ml_dtypes
import numpy as np
from jax import lax
from jax.experimental import pallas as pl
from jax.experimental.pallas import tpu as pltpu
from jax.sharding import PartitionSpec as P

TRANS = 4
CYCLES = 32
ANG = 144
ROT = 36
NDEF = 16
STEP = ANG // ROT
PAIRS = 2 * CYCLES
LANES = 2 * STEP * CYCLES
HALF = LANES // 2
OWN = 4
MINE = 8
BLOCKS = 4
KS = OWN * BLOCKS
US = MINE * BLOCKS * TRANS
ROWS = ROT * KS
REACH = 3
MIDDLE = 24
SLOTS = 32
WINDOW = 20_000_000_000
offset_sigma = 2.0
F32 = jnp.float32
BF16 = jnp.bfloat16
HIGHEST = lax.Precision.HIGHEST
VMEM_LIMIT = 20 * 1024 * 1024


def phase_parts():
    span = 2 * REACH + 1
    theta = 2.0 * math.pi * np.arange(ANG).reshape(ROT, STEP)[: ROT // 2] / ANG
    radius = np.arange(CYCLES) + 1.0
    fx = (np.cos(theta)[:, :, None] * radius).reshape(ROT // 2, HALF)
    fy = (np.sin(theta)[:, :, None] * radius).reshape(ROT // 2, HALF)
    shift = np.arange(span) - REACH
    phi = (
        -2.0
        * math.pi
        * (shift[:, None, None, None] * fx + shift[None, :, None, None] * fy)
        / (2.0 * CYCLES)
    ).reshape(span * span, ROT // 2, HALF)[MIDDLE:]
    table = np.concatenate([np.cos(phi), np.sin(phi)], axis=2).transpose(1, 0, 2)
    table = np.pad(table, ((0, 0), (0, SLOTS - table.shape[1]), (0, 0)))
    parts = []
    rest = table
    for _ in range(3):
        part = rest.astype(np.float32).astype(ml_dtypes.bfloat16)
        parts.append(part)
        rest = rest - part.astype(np.float64)
    return np.concatenate(parts, axis=1)


def nt(a, b, **kw):
    return lax.dot_general(a, b, (((1,), (1,)), ((), ())), preferred_element_type=F32, **kw)


def in_hbm(value):
    return pltpu.with_memory_space_constraint(value, pltpu.HBM)


def fetch(pairs, sems):
    copies = [
        pltpu.make_async_copy(src, dst, sems.at[n]) for n, (src, dst) in enumerate(pairs)
    ]
    for copy in copies:
        copy.start()
    return copies


def as_column(row, size):
    here = lax.broadcasted_iota(jnp.int32, (size, size), 0)
    there = lax.broadcasted_iota(jnp.int32, (size, size), 1)
    wide = jnp.broadcast_to(row, (size, size))
    return jnp.sum(jnp.where(here == there, wide, 0.0), axis=1, keepdims=True)


def as_row(column, size):
    here = lax.broadcasted_iota(jnp.int32, (size, size), 0)
    there = lax.broadcasted_iota(jnp.int32, (size, size), 1)
    wide = jnp.broadcast_to(column, (size, size))
    return jnp.sum(jnp.where(here == there, wide, 0.0), axis=0, keepdims=True)


def turn_major(source, count, cut, flat, out):
    angle = lax.broadcasted_iota(jnp.int32, (CYCLES, ANG), 1) % STEP
    pick_b = lax.broadcasted_iota(jnp.int32, (40, ANG), 0)
    pick_a = lax.broadcasted_iota(jnp.int32, (40, ANG), 1)
    pick = jnp.where(pick_a // STEP == pick_b, 1.0, 0.0).astype(BF16)
    for j in range(PAIRS):
        line = source[:, j * ANG : (j + 1) * ANG].astype(F32)
        cut[0, pl.ds(j * 8, count), :] = line[:, :HALF]
        cut[1, pl.ds(j * 8, count), : ANG - HALF] = line[:, HALF:]
    for i in range(count):
        one = jnp.concatenate(
            [cut.at[n][pl.ds(i, PAIRS, stride=8), :] for n in range(2)], axis=1
        )[:, :ANG]
        spread = jnp.concatenate(
            [
                jnp.where(angle == c, one[p * CYCLES : (p + 1) * CYCLES], 0.0)
                for p in range(2)
                for c in range(STEP)
            ],
            axis=0,
        ).astype(BF16)
        turned = nt(pick, spread)
        flat[0, pl.ds(i * 40, 40), :] = turned[:, :HALF]
        flat[1, pl.ds(i * 40, 40), :] = turned[:, HALF:]
    for b in range(ROT):
        for n in range(2):
            line = flat.at[n][pl.ds(b, count, stride=40), :]
            out[b, :, n * HALF : (n + 1) * HALF] = line.astype(BF16)


def arrange_kernel(
    img_hbm, ref_hbm, prior_hbm, off_hbm, def_hbm, ctf_hbm, noise_hbm, tau_hbm, table_hbm,
    img_out, ref_out, ctf_out, noise_out, tau_out, table_out,
    img_ref, ref_ref, prior_ref, off_ref, def_ref, ctf_ref, noise_ref, tau_ref,
    cut, cut2, flat, flat2, sems,
):
    copies = fetch(
        (
            (ref_hbm, ref_ref),
            (img_hbm, img_ref),
            (prior_hbm, prior_ref),
            (off_hbm, off_ref),
            (def_hbm, def_ref),
            (ctf_hbm, ctf_ref),
            (noise_hbm, noise_ref),
            (tau_hbm, tau_ref),
            (table_hbm, table_out),
        ),
        sems,
    )
    for copy in copies[:-1]:
        copy.wait()
    turn_major(ref_ref, OWN, cut, flat, ref_out)
    turn_major(img_ref, MINE, cut2, flat2, img_out)
    lane = lax.broadcasted_iota(jnp.int32, (MINE, LANES), 1)
    extra = jnp.where(lane == 8, as_column(def_ref[...].astype(F32), MINE), 0.0)
    for t in range(TRANS):
        for d in range(2):
            column = as_column(off_ref[t, d : d + 1, :].astype(F32), MINE)
            extra = jnp.where(lane == 2 * t + d, column, extra)
    img_out[ROT] = extra.astype(BF16)
    column = as_column(prior_ref[...].astype(F32), OWN)
    ref_out[ROT] = jnp.broadcast_to(column, (OWN, LANES)).astype(BF16)
    for small, out in ((ctf_ref, ctf_out), (noise_ref, noise_out), (tau_ref, tau_out)):
        out[...] = jnp.concatenate([small[...]] * STEP, axis=1)
    copies[-1].wait()


def arrange(images, references, prior, offsets, defocus, ctf_table, noise, tau, table):
    vmem = pl.BlockSpec(memory_space=pltpu.VMEM)
    hbm = pl.BlockSpec(memory_space=pltpu.HBM)
    wide = 2 * CYCLES * ANG
    return pl.pallas_call(
        arrange_kernel,
        out_shape=(
            jax.ShapeDtypeStruct((ROT + 1, MINE, LANES), BF16),
            jax.ShapeDtypeStruct((ROT + 1, OWN, LANES), BF16),
            jax.ShapeDtypeStruct((NDEF, HALF), F32),
            jax.ShapeDtypeStruct((1, HALF), F32),
            jax.ShapeDtypeStruct((1, HALF), F32),
            jax.ShapeDtypeStruct((ROT // 2, 3 * SLOTS, LANES), BF16),
        ),
        in_specs=[hbm] * 9,
        out_specs=(vmem,) * 6,
        scratch_shapes=[
            pltpu.VMEM((MINE, wide), BF16),
            pltpu.VMEM((OWN, wide), BF16),
            pltpu.VMEM((1, OWN), BF16),
            pltpu.VMEM((TRANS, 2, MINE), jnp.int32),
            pltpu.VMEM((1, MINE), jnp.int32),
            pltpu.VMEM((NDEF, CYCLES), F32),
            pltpu.VMEM((1, CYCLES), F32),
            pltpu.VMEM((1, CYCLES), F32),
            pltpu.VMEM((2, PAIRS * 8, HALF), F32),
            pltpu.VMEM((2, PAIRS * 8, HALF), F32),
            pltpu.VMEM((2, MINE * 40, HALF), F32),
            pltpu.VMEM((2, MINE * 40, HALF), F32),
            pltpu.SemaphoreType.DMA((9,)),
        ],
        compiler_params=pltpu.CompilerParams(vmem_limit_bytes=VMEM_LIMIT),
        name="arrange",
    )(
        *(
            in_hbm(v)
            for v in (images, references, prior, offsets, defocus, ctf_table, noise, tau, table)
        )
    )


def four(value):
    return jnp.concatenate([value] * TRANS, axis=0)


def image_rows(near, far):
    extra = jnp.concatenate([near[ROT].astype(F32), far[ROT].astype(F32)], axis=0)
    dx = jnp.concatenate([extra[:, 2 * t : 2 * t + 1] for t in range(TRANS)], axis=0)
    dy = jnp.concatenate([extra[:, 2 * t + 1 : 2 * t + 2] for t in range(TRANS)], axis=0)
    return dx, dy, extra[:, 8:9]


def contrast_of(group, ctf_ref):
    known = lax.broadcasted_iota(jnp.int32, (group.shape[0], NDEF), 1).astype(F32)
    which = jnp.where(known == group, 1.0, 0.0)
    return jnp.dot(which, ctf_ref[...], precision=HIGHEST, preferred_element_type=F32)


def shift_half(near, far, dx, dy, contrast, noise, table, weighted, inserted):
    pair = dx * (2 * REACH + 1) + dy
    slot = lax.broadcasted_iota(jnp.int32, (US // 2, 3 * SLOTS), 1) % SLOTS
    hot = jnp.where(slot.astype(F32) == jnp.abs(pair), 1.0, 0.0).astype(BF16)
    sign = jnp.broadcast_to(jnp.where(pair < 0, -1.0, 1.0), (US // 2, HALF))
    contrast4 = four(contrast)
    whiten4 = four(contrast / noise)
    for half in range(ROT // 2):
        turn = jnp.dot(hot, table[half], preferred_element_type=F32)
        cosine, sine = turn[:, :HALF], turn[:, HALF:] * sign
        for b, flip in ((half, False), (half + ROT // 2, True)):
            block = jnp.concatenate([near[b].astype(F32), far[b].astype(F32)], axis=0)
            real, imag = four(block[:, :HALF]), four(block[:, HALF:])
            if flip:
                shifted_real = real * cosine + imag * sine
                shifted_imag = imag * cosine - real * sine
            else:
                shifted_real = real * cosine - imag * sine
                shifted_imag = real * sine + imag * cosine
            rows = slice(b * US // 2, (b + 1) * US // 2)
            weighted[rows, :HALF] = (shifted_real * whiten4).astype(BF16)
            weighted[rows, HALF:] = (shifted_imag * whiten4).astype(BF16)
            inserted[rows, :HALF] = (shifted_real * contrast4).astype(BF16)
            inserted[rows, HALF:] = (shifted_imag * contrast4).astype(BF16)


def shift_kernel(near, far, ctf_ref, noise_ref, table, weighted, inserted):
    dx, dy, group = image_rows(near, far)
    contrast = contrast_of(group, ctf_ref)
    shift_half(near, far, dx, dy, contrast, noise_ref[...], table, weighted, inserted)


def shift(near, far, ctf4, noise4, table):
    vmem = pl.BlockSpec(memory_space=pltpu.VMEM)
    half = jax.ShapeDtypeStruct((ROT * US // 2, LANES), BF16)
    return pl.pallas_call(
        shift_kernel,
        out_shape=(half, half),
        in_specs=[vmem] * 5,
        out_specs=(vmem, vmem),
        compiler_params=pltpu.CompilerParams(vmem_limit_bytes=VMEM_LIMIT),
        name="shift",
        cost_estimate=pl.CostEstimate(flops=WINDOW, bytes_accessed=1000, transcendentals=0),
    )(near, far, ctf4, noise4, table)


def swapped(row, own):
    lane = lax.broadcasted_iota(jnp.int32, row.shape, 1)
    chosen = lambda bit: jnp.broadcast_to((own >> bit) & 1, row.shape) == 1
    row = jnp.where(chosen(0), pltpu.roll(row, US // 2, 1), row)
    other = jnp.where(
        (lane // MINE) % 2 == 0, pltpu.roll(row, US - MINE, 1), pltpu.roll(row, MINE, 1)
    )
    return jnp.where(chosen(1), other, row)


def over_shifts(row, combine):
    lane = lax.broadcasted_iota(jnp.int32, row.shape, 1)
    for size in (16, 32):
        turned = jnp.where(
            lane % 64 >= size, pltpu.roll(row, size, 1), pltpu.roll(row, size + 64, 1)
        )
        row = combine(row, turned)
    return row


def score_kernel(
    own_ref, i0, i2, i13, w_near, r0, r1, r2, r3, ctf_ref, noise_ref, table,
    exp_out, stat_out, ins_out, sq_out,
    w_far, back,
):
    own = own_ref[0]
    square = jnp.zeros((KS, LANES), F32)
    for b in range(ROT):
        block = jnp.concatenate([r[b].astype(F32) for r in (r0, r1, r2, r3)], axis=0)
        square = square + block * block
        m = (ROT - b) % ROT
        back[pl.ds(m * KS, KS), :] = block.astype(BF16)
        back[pl.ds((m + ROT) * KS, KS), :] = block.astype(BF16)
    prior = jnp.concatenate([r[ROT].astype(F32) for r in (r0, r1, r2, r3)], axis=0)[:, :HALF]

    i1, i3 = i13.at[0], i13.at[1]
    dx0, dy0, group0 = image_rows(i0, i2)
    dx1, dy1, group1 = image_rows(i1, i3)
    noise = noise_ref[...]
    contrast = contrast_of(jnp.concatenate([group0, group1], axis=0), ctf_ref)
    far_contrast = contrast[2 * MINE :]
    squared = contrast * contrast
    squared = jnp.concatenate([four(squared[: 2 * MINE]), four(squared[2 * MINE :])], axis=0)
    sq_out[:, :HALF] = squared
    sq_out[:, HALF:] = jnp.ones((US, HALF), F32)
    coef = squared / (2.0 * noise)
    penalty = nt(square, jnp.concatenate([coef, coef], axis=1), precision=HIGHEST)
    dx = jnp.concatenate([dx0, dx1], axis=0)
    dy = jnp.concatenate([dy0, dy1], axis=0)
    near = -(dx * dx + dy * dy) / (2.0 * offset_sigma * offset_sigma)
    base = prior - penalty + as_row(near, US)

    shift_half(i1, i3, dx1, dy1, far_contrast, noise, table, w_far, ins_out)
    half = US // 2
    cross = sum(
        nt(
            back[(ROT - 2 * h) * KS : (2 * ROT - 2 * h) * KS, :],
            jnp.concatenate(
                [
                    w[b * half : (b + 1) * half, :]
                    for b in (2 * h, 2 * h + 1)
                    for w in (w_near, w_far)
                ],
                axis=0,
            ),
        )
        for quarter in range(ROT // 4)
        for h in (quarter, quarter + ROT // 4)
    )

    peak = jnp.full((KS, US), -jnp.inf, F32)
    for r in range(ROT):
        last = (r - 1) % ROT
        logp = cross[r * KS : (r + 1) * KS, :HALF] + cross[last * KS : (last + 1) * KS, HALF:] + base
        exp_out[r * KS : (r + 1) * KS, :] = logp
        peak = jnp.maximum(peak, logp)
    peak = jnp.broadcast_to(jnp.max(peak, axis=0, keepdims=True), (8, US))
    wide = jnp.broadcast_to(peak[:1], (KS, US))
    total = jnp.zeros((KS, US), F32)
    for r in range(ROT):
        value = jnp.exp(exp_out[r * KS : (r + 1) * KS, :] - wide)
        exp_out[r * KS : (r + 1) * KS, :] = value
        total = total + value
    total = jnp.broadcast_to(jnp.sum(total, axis=0, keepdims=True), (8, US))
    row = lax.broadcasted_iota(jnp.int32, (8, US), 0)
    pair = swapped(jnp.where(row == 0, peak, total), own)[:2]
    for j in range(32):
        stat_out[j] = pair


def score(own, imgs, w_near, refs, ctf4, noise4, table):
    vmem = pl.BlockSpec(memory_space=pltpu.VMEM)
    smem = pl.BlockSpec(memory_space=pltpu.SMEM)
    return pl.pallas_call(
        score_kernel,
        out_shape=(
            jax.ShapeDtypeStruct((ROWS, US), F32),
            jax.ShapeDtypeStruct((32, 2, US), F32),
            jax.ShapeDtypeStruct((ROT * US // 2, LANES), BF16),
            jax.ShapeDtypeStruct((US, LANES), F32),
        ),
        in_specs=[smem] + [vmem] * 11,
        out_specs=(vmem,) * 4,
        scratch_shapes=[
            pltpu.VMEM((ROT * US // 2, LANES), BF16),
            pltpu.VMEM((2 * ROWS, LANES), BF16),
        ],
        compiler_params=pltpu.CompilerParams(vmem_limit_bytes=VMEM_LIMIT),
        name="score",
    )(own, *imgs, w_near, *refs, ctf4, noise4, table)


def insert_kernel(
    own_ref, exp_ref, pair_ref, all_ref, near_ref, far_ref, sq_ref,
    own_out, s1, s2, s3, like_out, post,
):
    own = own_ref[0]
    peaks = jnp.concatenate([all_ref[j, 0:1, :] for j in range(32)], axis=0)
    totals = jnp.concatenate([all_ref[j, 1:2, :] for j in range(32)], axis=0)
    lane_peak = jnp.max(peaks, axis=0, keepdims=True)
    lane_total = jnp.sum(totals * jnp.exp(peaks - lane_peak), axis=0, keepdims=True)
    lane_peak = jnp.broadcast_to(lane_peak, (8, US))
    peak = over_shifts(lane_peak, jnp.maximum)
    total = over_shifts(lane_total * jnp.exp(lane_peak - peak), jnp.add)
    scale = jnp.exp(pair_ref[0, 0:1, :] - peak) / total
    like_out[...] = swapped(peak + jnp.log(total), own)
    scale = jnp.broadcast_to(swapped(scale, own)[:1], (KS, US))
    count = jnp.zeros((KS, US), F32)
    for r in range(ROT):
        value = (exp_ref[r * KS : (r + 1) * KS, :] * scale).astype(BF16)
        count = count + value.astype(F32)
        for side in range(2):
            m = (side - r) % ROT
            for again in (m, m + ROT):
                post[again * KS : (again + 1) * KS, side * HALF : (side + 1) * HALF] = value

    half = US // 2
    numer = sum(
        jnp.dot(
            post[(ROT - 2 * h) * KS : (2 * ROT - 2 * h) * KS, :],
            jnp.concatenate(
                [
                    v[b * half : (b + 1) * half, :]
                    for b in (2 * h, 2 * h + 1)
                    for v in (near_ref, far_ref)
                ],
                axis=0,
            ),
            preferred_element_type=F32,
        )
        for h in range(ROT // 2)
    )
    sums = jnp.dot(count, sq_ref[...], precision=HIGHEST, preferred_element_type=F32)
    for b in range(ROT):
        block = numer[b * KS : (b + 1) * KS, :]
        own_out[b] = block[:OWN]
        for d, out in ((1, s1), (2, s2), (3, s3)):
            out[b] = block[d * OWN : (d + 1) * OWN].astype(BF16)
    own_out[ROT] = sums[:OWN]
    own_out[ROT + 1] = jnp.zeros((OWN, LANES), F32)
    for d, out in ((1, s1), (2, s2), (3, s3)):
        part = sums[d * OWN : (d + 1) * OWN]
        high = part.astype(BF16)
        out[ROT] = high
        out[ROT + 1] = (part - high.astype(F32)).astype(BF16)


def insert(own, exps, stats, gathered, near, far, sq):
    vmem = pl.BlockSpec(memory_space=pltpu.VMEM)
    smem = pl.BlockSpec(memory_space=pltpu.SMEM)
    piece = (ROT + 2, OWN, LANES)
    return pl.pallas_call(
        insert_kernel,
        out_shape=(
            jax.ShapeDtypeStruct(piece, F32),
            jax.ShapeDtypeStruct(piece, BF16),
            jax.ShapeDtypeStruct(piece, BF16),
            jax.ShapeDtypeStruct(piece, BF16),
            jax.ShapeDtypeStruct((8, US), F32),
        ),
        in_specs=[smem] + [vmem] * 6,
        out_specs=(vmem,) * 5,
        scratch_shapes=[
            pltpu.VMEM((2 * ROWS, LANES), BF16),
        ],
        compiler_params=pltpu.CompilerParams(vmem_limit_bytes=VMEM_LIMIT),
        name="insert",
    )(own, exps, stats, gathered, near, far, sq)


def finish_kernel(own_ref, g1, g2, g3, tau_ref, like_ref, out_ref, weight_out, like_out, fresh, turned, lines):
    like_out[...] = like_ref[:1, :MINE]
    parts = [own_ref, g1, g2, g3]
    sums = sum(p[ROT].astype(F32) + p[ROT + 1].astype(F32) for p in parts)
    denom = sums[:, :HALF] + 1.0 / tau_ref[...]
    denom = jnp.concatenate([denom, denom], axis=1)
    weight_out[...] = as_row(sums[:, HALF : HALF + 1], OWN) / (MINE * 16)
    for b in range(ROT):
        total = own_ref[b] + g1[b].astype(F32) + g2[b].astype(F32) + g3[b].astype(F32)
        total = total / denom
        fresh[0, pl.ds(b * 8, OWN), :] = total[:, :HALF]
        fresh[1, pl.ds(b * 8, OWN), :] = total[:, HALF:]
    for k in range(OWN):
        one = [fresh.at[p][pl.ds(k, ROT, stride=8), :] for p in range(2)]
        for c in range(STEP):
            pair = [one[p][:, c * CYCLES : (c + 1) * CYCLES] for p in range(2)]
            turned[pl.ds(c, ROT, stride=STEP), :] = jnp.concatenate(pair + pair, axis=1)
        first = turned[0:128, :].T
        second = turned[128:256, :].T
        lines[0, pl.ds(k * PAIRS, PAIRS), :] = first[:PAIRS]
        lines[1, pl.ds(k * PAIRS, PAIRS), :] = second[:PAIRS]
    for j in range(PAIRS):
        line = [lines.at[n][pl.ds(j, OWN, stride=PAIRS), :] for n in range(2)]
        out_ref[:, j * ANG : (j + 1) * ANG] = jnp.concatenate(line, axis=1)[:, :ANG]


def finish(own, got, tau, like):
    vmem = pl.BlockSpec(memory_space=pltpu.VMEM)
    return pl.pallas_call(
        finish_kernel,
        out_shape=(
            jax.ShapeDtypeStruct((OWN, 2 * CYCLES * ANG), F32),
            jax.ShapeDtypeStruct((1, OWN), F32),
            jax.ShapeDtypeStruct((1, MINE), F32),
        ),
        in_specs=[vmem] * 6,
        out_specs=(vmem,) * 3,
        scratch_shapes=[
            pltpu.VMEM((2, ROT * 8, HALF), F32),
            pltpu.VMEM((256, 128), F32),
            pltpu.VMEM((2, OWN * PAIRS, HALF), F32),
        ],
        compiler_params=pltpu.CompilerParams(vmem_limit_bytes=VMEM_LIMIT),
        name="finish",
    )(own, *got, tau, like)


def along_y(value, distance):
    return lax.ppermute(
        value, "img", [(i, ((i // 4 + distance) % 4) * 4 + i % 4) for i in range(16)]
    )


def beside(value, img_flip, cls_flip):
    pairs = [
        (i * 8 + c, (i ^ img_flip) * 8 + (c ^ cls_flip)) for i in range(16) for c in range(8)
    ]
    return lax.ppermute(value, ("img", "cls"), pairs)


def per_device(
    table, images, references, class_logprior, ctf_table, noise_power, tau_power, defocus, offsets
):
    own = (lax.axis_index("img") % BLOCKS).astype(jnp.int32).reshape(1)
    img, ref, ctf4, noise4, tau4, table = arrange(
        images,
        references,
        class_logprior.reshape(1, OWN),
        offsets.transpose(1, 2, 0),
        defocus.reshape(1, MINE),
        ctf_table,
        noise_power.reshape(1, CYCLES),
        tau_power.reshape(1, CYCLES),
        table,
    )
    next_chip = beside(img, 2, 1)
    refs = (ref, along_y(ref, 3), along_y(ref, 2), along_y(ref, 1))
    other_core = beside(jnp.stack([img, next_chip]), 1, 0)
    w_near, near = shift(img, next_chip, ctf4, noise4, table)
    exps, stats, far, sq = score(
        own, (img, next_chip, other_core), w_near, refs, ctf4, noise4, table
    )
    same_images = [[(y * 4 + r) * 8 + c for r in range(4) for c in range(8)] for y in range(4)]
    gathered = lax.all_to_all(
        stats, ("img", "cls"), 0, 0, tiled=True, axis_index_groups=same_images
    )
    numer, s1, s2, s3, like = insert(own, exps, stats, gathered, near, far, sq)
    got = (along_y(s1, 1), along_y(s2, 2), along_y(s3, 3))
    fresh, weight, like = finish(numer, got, tau4, like)
    return fresh, weight.reshape(OWN), like.reshape(MINE)


def solution(mesh):
    body = functools.partial(per_device, jnp.asarray(phase_parts()))
    return jax.shard_map(
        body,
        mesh=mesh,
        in_specs=(
            P("img", None),
            P(("img", "cls"), None),
            P(("img", "cls")),
            P(),
            P(),
            P(),
            P("img"),
            P("img", None, None),
        ),
        out_specs=(P(("img", "cls"), None), P(("img", "cls")), P("img")),
        check_vma=False,
    )
```

```python
import functools
import math

import jax
import jax.numpy as jnp
import ml_dtypes
import numpy as np
from jax import lax
from jax.experimental import pallas as pl
from jax.experimental.pallas import tpu as pltpu
from jax.sharding import PartitionSpec as P

TRANS = 4
CYCLES = 32
ANG = 144
ROT = 36
NDEF = 16
STEP = ANG // ROT
PAIRS = 2 * CYCLES
LANES = 2 * STEP * CYCLES
HALF = LANES // 2
OWN = 4
MINE = 8
BLOCKS = 4
KS = OWN * BLOCKS
US = MINE * BLOCKS * TRANS
ROWS = ROT * KS
REACH = 3
MIDDLE = 24
SLOTS = 32
WINDOW = 20_000_000_000
offset_sigma = 2.0
F32 = jnp.float32
BF16 = jnp.bfloat16
HIGHEST = lax.Precision.HIGHEST
VMEM_LIMIT = 20 * 1024 * 1024


def phase_parts():
    span = 2 * REACH + 1
    theta = 2.0 * math.pi * np.arange(ANG).reshape(ROT, STEP)[: ROT // 2] / ANG
    radius = np.arange(CYCLES) + 1.0
    fx = (np.cos(theta)[:, :, None] * radius).reshape(ROT // 2, HALF)
    fy = (np.sin(theta)[:, :, None] * radius).reshape(ROT // 2, HALF)
    shift = np.arange(span) - REACH
    phi = (
        -2.0
        * math.pi
        * (shift[:, None, None, None] * fx + shift[None, :, None, None] * fy)
        / (2.0 * CYCLES)
    ).reshape(span * span, ROT // 2, HALF)[MIDDLE:]
    table = np.concatenate([np.cos(phi), np.sin(phi)], axis=2).transpose(1, 0, 2)
    table = np.pad(table, ((0, 0), (0, SLOTS - table.shape[1]), (0, 0)))
    parts = []
    rest = table
    for _ in range(3):
        part = rest.astype(np.float32).astype(ml_dtypes.bfloat16)
        parts.append(part)
        rest = rest - part.astype(np.float64)
    return np.concatenate(parts, axis=1)


def nt(a, b, **kw):
    return lax.dot_general(a, b, (((1,), (1,)), ((), ())), preferred_element_type=F32, **kw)


def in_hbm(value):
    return pltpu.with_memory_space_constraint(value, pltpu.HBM)


def fetch(pairs, sems):
    copies = [
        pltpu.make_async_copy(src, dst, sems.at[n]) for n, (src, dst) in enumerate(pairs)
    ]
    for copy in copies:
        copy.start()
    return copies


def as_column(row, size):
    here = lax.broadcasted_iota(jnp.int32, (size, size), 0)
    there = lax.broadcasted_iota(jnp.int32, (size, size), 1)
    wide = jnp.broadcast_to(row, (size, size))
    return jnp.sum(jnp.where(here == there, wide, 0.0), axis=1, keepdims=True)


def as_row(column, size):
    here = lax.broadcasted_iota(jnp.int32, (size, size), 0)
    there = lax.broadcasted_iota(jnp.int32, (size, size), 1)
    wide = jnp.broadcast_to(column, (size, size))
    return jnp.sum(jnp.where(here == there, wide, 0.0), axis=0, keepdims=True)


def turn_major(source, count, cut, flat, out):
    angle = lax.broadcasted_iota(jnp.int32, (CYCLES, ANG), 1) % STEP
    pick_b = lax.broadcasted_iota(jnp.int32, (40, ANG), 0)
    pick_a = lax.broadcasted_iota(jnp.int32, (40, ANG), 1)
    pick = jnp.where(pick_a // STEP == pick_b, 1.0, 0.0).astype(BF16)
    for j in range(PAIRS):
        line = source[:, j * ANG : (j + 1) * ANG].astype(F32)
        cut[0, pl.ds(j * 8, count), :] = line[:, :HALF]
        cut[1, pl.ds(j * 8, count), : ANG - HALF] = line[:, HALF:]
    for i in range(count):
        one = jnp.concatenate(
            [cut.at[n][pl.ds(i, PAIRS, stride=8), :] for n in range(2)], axis=1
        )[:, :ANG]
        spread = jnp.concatenate(
            [
                jnp.where(angle == c, one[p * CYCLES : (p + 1) * CYCLES], 0.0)
                for p in range(2)
                for c in range(STEP)
            ],
            axis=0,
        ).astype(BF16)
        turned = nt(pick, spread)
        flat[0, pl.ds(i * 40, 40), :] = turned[:, :HALF]
        flat[1, pl.ds(i * 40, 40), :] = turned[:, HALF:]
    for b in range(ROT):
        for n in range(2):
            line = flat.at[n][pl.ds(b, count, stride=40), :]
            out[b, :, n * HALF : (n + 1) * HALF] = line.astype(BF16)


def arrange_kernel(
    img_hbm, ref_hbm, prior_hbm, off_hbm, def_hbm, ctf_hbm, noise_hbm, tau_hbm, table_hbm,
    img_out, ref_out, ctf_out, noise_out, tau_out, table_out,
    img_ref, ref_ref, prior_ref, off_ref, def_ref, ctf_ref, noise_ref, tau_ref,
    cut, cut2, flat, flat2, sems,
):
    copies = fetch(
        (
            (ref_hbm, ref_ref),
            (img_hbm, img_ref),
            (prior_hbm, prior_ref),
            (off_hbm, off_ref),
            (def_hbm, def_ref),
            (ctf_hbm, ctf_ref),
            (noise_hbm, noise_ref),
            (tau_hbm, tau_ref),
            (table_hbm, table_out),
        ),
        sems,
    )
    for copy in copies[:-1]:
        copy.wait()
    turn_major(img_ref, MINE, cut2, flat2, img_out)
    lane = lax.broadcasted_iota(jnp.int32, (MINE, LANES), 1)
    extra = jnp.where(lane == 8, as_column(def_ref[...].astype(F32), MINE), 0.0)
    for t in range(TRANS):
        for d in range(2):
            column = as_column(off_ref[t, d : d + 1, :].astype(F32), MINE)
            extra = jnp.where(lane == 2 * t + d, column, extra)
    img_out[ROT] = extra.astype(BF16)
    column = as_column(prior_ref[...].astype(F32), OWN)
    ref_out[ROT] = jnp.broadcast_to(column, (OWN, LANES)).astype(BF16)
    for small, out in ((ctf_ref, ctf_out), (noise_ref, noise_out), (tau_ref, tau_out)):
        out[...] = jnp.concatenate([small[...]] * STEP, axis=1)
    turn_major(ref_ref, OWN, cut, flat, ref_out)
    copies[-1].wait()


def arrange(images, references, prior, offsets, defocus, ctf_table, noise, tau, table):
    vmem = pl.BlockSpec(memory_space=pltpu.VMEM)
    hbm = pl.BlockSpec(memory_space=pltpu.HBM)
    wide = 2 * CYCLES * ANG
    return pl.pallas_call(
        arrange_kernel,
        out_shape=(
            jax.ShapeDtypeStruct((ROT + 1, MINE, LANES), BF16),
            jax.ShapeDtypeStruct((ROT + 1, OWN, LANES), BF16),
            jax.ShapeDtypeStruct((NDEF, HALF), F32),
            jax.ShapeDtypeStruct((1, HALF), F32),
            jax.ShapeDtypeStruct((1, HALF), F32),
            jax.ShapeDtypeStruct((ROT // 2, 3 * SLOTS, LANES), BF16),
        ),
        in_specs=[hbm] * 9,
        out_specs=(vmem,) * 6,
        scratch_shapes=[
            pltpu.VMEM((MINE, wide), BF16),
            pltpu.VMEM((OWN, wide), BF16),
            pltpu.VMEM((1, OWN), BF16),
            pltpu.VMEM((TRANS, 2, MINE), jnp.int32),
            pltpu.VMEM((1, MINE), jnp.int32),
            pltpu.VMEM((NDEF, CYCLES), F32),
            pltpu.VMEM((1, CYCLES), F32),
            pltpu.VMEM((1, CYCLES), F32),
            pltpu.VMEM((2, PAIRS * 8, HALF), F32),
            pltpu.VMEM((2, PAIRS * 8, HALF), F32),
            pltpu.VMEM((2, MINE * 40, HALF), F32),
            pltpu.VMEM((2, MINE * 40, HALF), F32),
            pltpu.SemaphoreType.DMA((9,)),
        ],
        compiler_params=pltpu.CompilerParams(vmem_limit_bytes=VMEM_LIMIT),
        name="arrange",
    )(
        *(
            in_hbm(v)
            for v in (images, references, prior, offsets, defocus, ctf_table, noise, tau, table)
        )
    )


def four(value):
    return jnp.concatenate([value] * TRANS, axis=0)


def image_rows(near, far):
    extra = jnp.concatenate([near[ROT].astype(F32), far[ROT].astype(F32)], axis=0)
    dx = jnp.concatenate([extra[:, 2 * t : 2 * t + 1] for t in range(TRANS)], axis=0)
    dy = jnp.concatenate([extra[:, 2 * t + 1 : 2 * t + 2] for t in range(TRANS)], axis=0)
    return dx, dy, extra[:, 8:9]


def contrast_of(group, ctf_ref):
    known = lax.broadcasted_iota(jnp.int32, (group.shape[0], NDEF), 1).astype(F32)
    which = jnp.where(known == group, 1.0, 0.0)
    return jnp.dot(which, ctf_ref[...], precision=HIGHEST, preferred_element_type=F32)


def shift_half(near, far, dx, dy, contrast, noise, table, weighted, inserted):
    pair = dx * (2 * REACH + 1) + dy
    slot = lax.broadcasted_iota(jnp.int32, (US // 2, 3 * SLOTS), 1) % SLOTS
    hot = jnp.where(slot.astype(F32) == jnp.abs(pair), 1.0, 0.0).astype(BF16)
    sign = jnp.broadcast_to(jnp.where(pair < 0, -1.0, 1.0), (US // 2, HALF))
    contrast4 = four(contrast)
    whiten4 = four(contrast / noise)
    for half in range(ROT // 2):
        turn = jnp.dot(hot, table[half], preferred_element_type=F32)
        cosine, sine = turn[:, :HALF], turn[:, HALF:] * sign
        for b, flip in ((half, False), (half + ROT // 2, True)):
            block = jnp.concatenate([near[b].astype(F32), far[b].astype(F32)], axis=0)
            real, imag = four(block[:, :HALF]), four(block[:, HALF:])
            if flip:
                shifted_real = real * cosine + imag * sine
                shifted_imag = imag * cosine - real * sine
            else:
                shifted_real = real * cosine - imag * sine
                shifted_imag = real * sine + imag * cosine
            rows = slice(b * US // 2, (b + 1) * US // 2)
            weighted[rows, :HALF] = (shifted_real * whiten4).astype(BF16)
            weighted[rows, HALF:] = (shifted_imag * whiten4).astype(BF16)
            inserted[rows, :HALF] = (shifted_real * contrast4).astype(BF16)
            inserted[rows, HALF:] = (shifted_imag * contrast4).astype(BF16)


def shift_kernel(near, far, ctf_ref, noise_ref, table, weighted, inserted):
    dx, dy, group = image_rows(near, far)
    contrast = contrast_of(group, ctf_ref)
    shift_half(near, far, dx, dy, contrast, noise_ref[...], table, weighted, inserted)


def shift(near, far, ctf4, noise4, table):
    vmem = pl.BlockSpec(memory_space=pltpu.VMEM)
    half = jax.ShapeDtypeStruct((ROT * US // 2, LANES), BF16)
    return pl.pallas_call(
        shift_kernel,
        out_shape=(half, half),
        in_specs=[vmem] * 5,
        out_specs=(vmem, vmem),
        compiler_params=pltpu.CompilerParams(vmem_limit_bytes=VMEM_LIMIT),
        name="shift",
        cost_estimate=pl.CostEstimate(flops=WINDOW, bytes_accessed=1000, transcendentals=0),
    )(near, far, ctf4, noise4, table)


def swapped(row, own):
    lane = lax.broadcasted_iota(jnp.int32, row.shape, 1)
    chosen = lambda bit: jnp.broadcast_to((own >> bit) & 1, row.shape) == 1
    row = jnp.where(chosen(0), pltpu.roll(row, US // 2, 1), row)
    other = jnp.where(
        (lane // MINE) % 2 == 0, pltpu.roll(row, US - MINE, 1), pltpu.roll(row, MINE, 1)
    )
    return jnp.where(chosen(1), other, row)


def over_shifts(row, combine):
    lane = lax.broadcasted_iota(jnp.int32, row.shape, 1)
    for size in (16, 32):
        turned = jnp.where(
            lane % 64 >= size, pltpu.roll(row, size, 1), pltpu.roll(row, size + 64, 1)
        )
        row = combine(row, turned)
    return row


def score_kernel(
    own_ref, i0, i2, i13, w_near, r0, r1, r2, r3, ctf_ref, noise_ref, table,
    exp_out, stat_out, ins_out, sq_out,
    w_far, back, acc,
):
    own = own_ref[0]
    square = jnp.zeros((KS, LANES), F32)
    for b in range(ROT):
        block = jnp.concatenate([r[b].astype(F32) for r in (r0, r1, r2, r3)], axis=0)
        square = square + block * block
        m = (ROT - b) % ROT
        back[pl.ds(m * KS, KS), :] = block.astype(BF16)
        back[pl.ds((m + ROT) * KS, KS), :] = block.astype(BF16)
    prior = jnp.concatenate([r[ROT].astype(F32) for r in (r0, r1, r2, r3)], axis=0)[:, :HALF]

    i1, i3 = i13.at[0], i13.at[1]
    dx0, dy0, group0 = image_rows(i0, i2)
    dx1, dy1, group1 = image_rows(i1, i3)
    noise = noise_ref[...]
    contrast = contrast_of(jnp.concatenate([group0, group1], axis=0), ctf_ref)
    far_contrast = contrast[2 * MINE :]
    squared = contrast * contrast
    squared = jnp.concatenate([four(squared[: 2 * MINE]), four(squared[2 * MINE :])], axis=0)
    sq_out[:, :HALF] = squared
    sq_out[:, HALF:] = jnp.ones((US, HALF), F32)
    coef = squared / (2.0 * noise)
    penalty = nt(square, jnp.concatenate([coef, coef], axis=1), precision=HIGHEST)
    dx = jnp.concatenate([dx0, dx1], axis=0)
    dy = jnp.concatenate([dy0, dy1], axis=0)
    near = -(dx * dx + dy * dy) / (2.0 * offset_sigma * offset_sigma)
    base = prior - penalty + as_row(near, US)

    shift_half(i1, i3, dx1, dy1, far_contrast, noise, table, w_far, ins_out)
    half = US // 2
    acc[...] = sum(
        nt(
            back[(ROT - 2 * h) * KS : (2 * ROT - 2 * h) * KS, :],
            jnp.concatenate(
                [
                    w[b * half : (b + 1) * half, :]
                    for b in (2 * h, 2 * h + 1)
                    for w in (w_near, w_far)
                ],
                axis=0,
            ),
        )
        for quarter in range(ROT // 4)
        for h in (quarter, quarter + ROT // 4)
    )

    peak = jnp.full((KS, US), -jnp.inf, F32)
    for r in range(ROT):
        last = (r - 1) % ROT
        logp = acc[r * KS : (r + 1) * KS, :HALF] + acc[last * KS : (last + 1) * KS, HALF:] + base
        exp_out[r * KS : (r + 1) * KS, :] = logp
        peak = jnp.maximum(peak, logp)
    peak = jnp.broadcast_to(jnp.max(peak, axis=0, keepdims=True), (8, US))
    wide = jnp.broadcast_to(peak[:1], (KS, US))
    total = jnp.zeros((KS, US), F32)
    for r in range(ROT):
        value = jnp.exp(exp_out[r * KS : (r + 1) * KS, :] - wide)
        exp_out[r * KS : (r + 1) * KS, :] = value
        total = total + value
    total = jnp.broadcast_to(jnp.sum(total, axis=0, keepdims=True), (8, US))
    row = lax.broadcasted_iota(jnp.int32, (8, US), 0)
    pair = swapped(jnp.where(row == 0, peak, total), own)[:2]
    for j in range(32):
        stat_out[j] = pair


def score(own, imgs, w_near, refs, ctf4, noise4, table):
    vmem = pl.BlockSpec(memory_space=pltpu.VMEM)
    smem = pl.BlockSpec(memory_space=pltpu.SMEM)
    return pl.pallas_call(
        score_kernel,
        out_shape=(
            jax.ShapeDtypeStruct((ROWS, US), F32),
            jax.ShapeDtypeStruct((32, 2, US), F32),
            jax.ShapeDtypeStruct((ROT * US // 2, LANES), BF16),
            jax.ShapeDtypeStruct((US, LANES), F32),
        ),
        in_specs=[smem] + [vmem] * 11,
        out_specs=(vmem,) * 4,
        scratch_shapes=[
            pltpu.VMEM((ROT * US // 2, LANES), BF16),
            pltpu.VMEM((2 * ROWS, LANES), BF16),
            pltpu.VMEM((ROWS, LANES), F32),
        ],
        compiler_params=pltpu.CompilerParams(vmem_limit_bytes=VMEM_LIMIT),
        name="score",
    )(own, *imgs, w_near, *refs, ctf4, noise4, table)


def insert_kernel(
    own_ref, exp_ref, pair_ref, all_ref, near_ref, far_ref, sq_ref,
    own_out, s1, s2, s3, like_out, post, acc,
):
    own = own_ref[0]
    peaks = jnp.concatenate([all_ref[j, 0:1, :] for j in range(32)], axis=0)
    totals = jnp.concatenate([all_ref[j, 1:2, :] for j in range(32)], axis=0)
    lane_peak = jnp.max(peaks, axis=0, keepdims=True)
    lane_total = jnp.sum(totals * jnp.exp(peaks - lane_peak), axis=0, keepdims=True)
    lane_peak = jnp.broadcast_to(lane_peak, (8, US))
    peak = over_shifts(lane_peak, jnp.maximum)
    total = over_shifts(lane_total * jnp.exp(lane_peak - peak), jnp.add)
    scale = jnp.exp(pair_ref[0, 0:1, :] - peak) / total
    like_out[...] = swapped(peak + jnp.log(total), own)
    scale = jnp.broadcast_to(swapped(scale, own)[:1], (KS, US))
    count = jnp.zeros((KS, US), F32)
    for r in range(ROT):
        value = (exp_ref[r * KS : (r + 1) * KS, :] * scale).astype(BF16)
        count = count + value.astype(F32)
        for side in range(2):
            m = (side - r) % ROT
            for again in (m, m + ROT):
                post[again * KS : (again + 1) * KS, side * HALF : (side + 1) * HALF] = value

    half = US // 2
    acc[...] = sum(
        jnp.dot(
            post[(ROT - 2 * h) * KS : (2 * ROT - 2 * h) * KS, :],
            jnp.concatenate(
                [
                    v[b * half : (b + 1) * half, :]
                    for b in (2 * h, 2 * h + 1)
                    for v in (near_ref, far_ref)
                ],
                axis=0,
            ),
            preferred_element_type=F32,
        )
        for h in range(ROT // 2)
    )
    sums = jnp.dot(count, sq_ref[...], precision=HIGHEST, preferred_element_type=F32)
    for b in range(ROT):
        block = acc[b * KS : (b + 1) * KS, :]
        own_out[b] = block[:OWN]
        for d, out in ((1, s1), (2, s2), (3, s3)):
            out[b] = block[d * OWN : (d + 1) * OWN].astype(BF16)
    own_out[ROT] = sums[:OWN]
    own_out[ROT + 1] = jnp.zeros((OWN, LANES), F32)
    for d, out in ((1, s1), (2, s2), (3, s3)):
        part = sums[d * OWN : (d + 1) * OWN]
        high = part.astype(BF16)
        out[ROT] = high
        out[ROT + 1] = (part - high.astype(F32)).astype(BF16)


def insert(own, exps, stats, gathered, near, far, sq):
    vmem = pl.BlockSpec(memory_space=pltpu.VMEM)
    smem = pl.BlockSpec(memory_space=pltpu.SMEM)
    piece = (ROT + 2, OWN, LANES)
    return pl.pallas_call(
        insert_kernel,
        out_shape=(
            jax.ShapeDtypeStruct(piece, F32),
            jax.ShapeDtypeStruct(piece, BF16),
            jax.ShapeDtypeStruct(piece, BF16),
            jax.ShapeDtypeStruct(piece, BF16),
            jax.ShapeDtypeStruct((8, US), F32),
        ),
        in_specs=[smem] + [vmem] * 6,
        out_specs=(vmem,) * 5,
        scratch_shapes=[
            pltpu.VMEM((2 * ROWS, LANES), BF16),
            pltpu.VMEM((ROWS, LANES), F32),
        ],
        compiler_params=pltpu.CompilerParams(vmem_limit_bytes=VMEM_LIMIT),
        name="insert",
    )(own, exps, stats, gathered, near, far, sq)


def finish_kernel(own_ref, g1, g2, g3, tau_ref, like_ref, out_ref, weight_out, like_out, fresh, turned, lines):
    like_out[...] = like_ref[:1, :MINE]
    parts = [own_ref, g1, g2, g3]
    sums = sum(p[ROT].astype(F32) + p[ROT + 1].astype(F32) for p in parts)
    denom = sums[:, :HALF] + 1.0 / tau_ref[...]
    denom = jnp.concatenate([denom, denom], axis=1)
    weight_out[...] = as_row(sums[:, HALF : HALF + 1], OWN) / (MINE * 16)
    for b in range(ROT):
        total = own_ref[b] + g1[b].astype(F32) + g2[b].astype(F32) + g3[b].astype(F32)
        total = total / denom
        fresh[0, pl.ds(b * 8, OWN), :] = total[:, :HALF]
        fresh[1, pl.ds(b * 8, OWN), :] = total[:, HALF:]
    for k in range(OWN):
        one = [fresh.at[p][pl.ds(k, ROT, stride=8), :] for p in range(2)]
        for c in range(STEP):
            pair = [one[p][:, c * CYCLES : (c + 1) * CYCLES] for p in range(2)]
            turned[pl.ds(c, ROT, stride=STEP), :] = jnp.concatenate(pair + pair, axis=1)
        first = turned[0:128, :].T
        second = turned[128:256, :].T
        lines[0, pl.ds(k * PAIRS, PAIRS), :] = first[:PAIRS]
        lines[1, pl.ds(k * PAIRS, PAIRS), :] = second[:PAIRS]
    for j in range(PAIRS):
        line = [lines.at[n][pl.ds(j, OWN, stride=PAIRS), :] for n in range(2)]
        out_ref[:, j * ANG : (j + 1) * ANG] = jnp.concatenate(line, axis=1)[:, :ANG]


def finish(own, got, tau, like):
    vmem = pl.BlockSpec(memory_space=pltpu.VMEM)
    return pl.pallas_call(
        finish_kernel,
        out_shape=(
            jax.ShapeDtypeStruct((OWN, 2 * CYCLES * ANG), F32),
            jax.ShapeDtypeStruct((1, OWN), F32),
            jax.ShapeDtypeStruct((1, MINE), F32),
        ),
        in_specs=[vmem] * 6,
        out_specs=(vmem,) * 3,
        scratch_shapes=[
            pltpu.VMEM((2, ROT * 8, HALF), F32),
            pltpu.VMEM((256, 128), F32),
            pltpu.VMEM((2, OWN * PAIRS, HALF), F32),
        ],
        compiler_params=pltpu.CompilerParams(vmem_limit_bytes=VMEM_LIMIT),
        name="finish",
    )(own, *got, tau, like)


def along_y(value, distance):
    return lax.ppermute(
        value, "img", [(i, ((i // 4 + distance) % 4) * 4 + i % 4) for i in range(16)]
    )


def beside(value, img_flip, cls_flip):
    pairs = [
        (i * 8 + c, (i ^ img_flip) * 8 + (c ^ cls_flip)) for i in range(16) for c in range(8)
    ]
    return lax.ppermute(value, ("img", "cls"), pairs)


def per_device(
    table, images, references, class_logprior, ctf_table, noise_power, tau_power, defocus, offsets
):
    own = (lax.axis_index("img") % BLOCKS).astype(jnp.int32).reshape(1)
    img, ref, ctf4, noise4, tau4, table = arrange(
        images,
        references,
        class_logprior.reshape(1, OWN),
        offsets.transpose(1, 2, 0),
        defocus.reshape(1, MINE),
        ctf_table,
        noise_power.reshape(1, CYCLES),
        tau_power.reshape(1, CYCLES),
        table,
    )
    next_chip = beside(img, 2, 1)
    refs = (ref, along_y(ref, 3), along_y(ref, 2), along_y(ref, 1))
    other_core = beside(jnp.stack([img, next_chip]), 1, 0)
    w_near, near = shift(img, next_chip, ctf4, noise4, table)
    exps, stats, far, sq = score(
        own, (img, next_chip, other_core), w_near, refs, ctf4, noise4, table
    )
    same_images = [[(y * 4 + r) * 8 + c for r in range(4) for c in range(8)] for y in range(4)]
    gathered = lax.all_to_all(
        stats, ("img", "cls"), 0, 0, tiled=True, axis_index_groups=same_images
    )
    numer, s1, s2, s3, like = insert(own, exps, stats, gathered, near, far, sq)
    got = (along_y(s1, 1), along_y(s2, 2), along_y(s3, 3))
    fresh, weight, like = finish(numer, got, tau4, like)
    return fresh, weight.reshape(OWN), like.reshape(MINE)


def solution(mesh):
    body = functools.partial(per_device, jnp.asarray(phase_parts()))
    return jax.shard_map(
        body,
        mesh=mesh,
        in_specs=(
            P("img", None),
            P(("img", "cls"), None),
            P(("img", "cls")),
            P(),
            P(),
            P(),
            P("img"),
            P("img", None, None),
        ),
        out_specs=(P(("img", "cls"), None), P(("img", "cls")), P("img")),
        check_vma=False,
    )
```
